768 devices in a mesh: blk: 96 (over z_lo, y, x), grp: 8 (over z_hi, core).
Axes of the slice: x: 4, y: 8, z: 12 (z_hi: 4, z_lo: 3; z = z_hi * 3 + z_lo), core: 2. Of those that a mesh axis runs over, the one named last changes fastest.
Arguments:
- latent: bfloat16 [393216, 128], P(('blk', 'grp')), may hold values from -6 to 6
- positions: float32 [3, 393216], P(None, ('blk', 'grp')), may hold values from -6 to 6
- tile_send: int32 [96, 8, 16], P('blk', 'grp'), may hold values from 0 to 31, as said below
- tile_recv: int32 [96, 8, 16], P('blk', 'grp'), may hold values from 0 to 11
- tile_mask: int32 [96, 8, 16, 128, 128], P('blk', 'grp'), may hold values 0 or 1
- tile_count: int32 [96, 8], P('blk', 'grp'), may hold values from 1 to 16
- w_send: bfloat16 [128, 128], replicated, may hold values from -0.5 to 0.5
- w_recv: bfloat16 [128, 128], replicated, may hold values from -0.5 to 0.5
- pos_weight: float32 [3, 128], replicated, may hold values from -3.5 to 3.5
- edge_bias: float32 [128], replicated, may hold values from -3 to 3
- w_edge_out: bfloat16 [128, 128], replicated, may hold values from -0.125 to 0.125
- w_node_self: bfloat16 [128, 128], replicated, may hold values from -0.375 to 0.375
- w_node_msg: bfloat16 [128, 128], replicated, may hold values from -0.375 to 0.375
- node_bias: float32 [128], replicated, may hold values from -3 to 3
- w_node_out: bfloat16 [128, 128], replicated, may hold values from -0.5 to 0.5
- gain: float32 [128], replicated, may hold values from 0.5 to 1.5
- cotangent: bfloat16 [393216, 128], P(('blk', 'grp')), may hold values from -6 to 6
Outputs:
- new_latent: bfloat16 [393216, 128], P(('blk', 'grp'))
- latent_grad: float32 [393216, 128], P(('blk', 'grp'))
- weight_grads: float32 [6, 128, 128], replicated
The draws below stay inside these ranges and needn't reach their ends.
Inputs may be any that keep to these rules, and one draw needn't show every extreme that they name: `tile_send`: the sender block of every tile lies in the same slab; tile 0 of member g names a block of member (g + 4) mod 8.
All inputs are finite; a program needn't handle non-finite values. No bound on the sum of `tile_mask` on one device may be relied on, other than what follows from the above.
Results may differ from the reference program's by a relative error of at most 0.012.
Values may be sent and summed in bfloat16 or wider, within the bound.
A program may use at most 32 MiB of HBM per device.

```python
import jax
import jax.numpy as jnp
from jax import lax

W = 128
BS = 128
NB = 4
TD = 16
SLABS = 96
GROUP = 8
NODES = 393216
N_BLK = 96
N_GRP = 8


def draw_tile_send(key, part):
    key_main = jax.random.fold_in(key, 11)
    key_far = jax.random.fold_in(key, 12)
    values = jax.random.randint(key_main, (N_BLK, N_GRP, TD), 0, N_GRP * NB)
    member = jnp.arange(N_GRP, dtype=jnp.int32)[None, :, None]
    far_member = (member + N_GRP // 2) % N_GRP
    far_block = far_member * NB + jax.random.randint(key_far, (N_BLK, N_GRP, TD), 0, NB)
    slot_index = jnp.arange(TD, dtype=jnp.int32)[None, None, :]
    values = jnp.where(slot_index == 0, far_block, values)
    values = values.at[0, 0, 1].set(0).at[0, 1, 1].set(N_GRP * NB - 1)
    return values.astype(jnp.int32)


def draw_tile_count(key, part):
    values = jax.random.randint(key, (N_BLK, N_GRP), 1, TD + 1)
    values = values.at[0, 0].set(TD).at[0, 1].set(1)
    return values.astype(jnp.int32)


def plant(result, key, least, top_value):
    index_at = [jax.random.randint(jax.random.fold_in(key, axis), (), 0, length) for axis, length in enumerate(result.shape)]
    main_axis = result.shape.index(max(result.shape))
    neighbour = index_at[:main_axis] + [(index_at[main_axis] + 1) % result.shape[main_axis]] + index_at[main_axis + 1:]
    return result.at[tuple(index_at)].set(least).at[tuple(neighbour)].set(top_value)


def steps_of(stream_key, dims, split, low, top_value):
    level, own = 1.0, jax.random.fold_in(stream_key, 6)
    for position, blocks in split:
        draws = jnp.exp(jax.random.uniform(jax.random.fold_in(own, position), (blocks,), jnp.float32, low / len(split), top_value / len(split)))
        level = level * jnp.repeat(draws, dims[position] // blocks).reshape([-1 if axis == position else 1 for axis in range(len(dims))])
    return level


def bell_draw(key, dims, scale, most, shards=(), kind=jnp.bfloat16):
    result = scale * jax.random.normal(key, dims, jnp.float32)
    if shards:
        result = result * steps_of(key, dims, shards, -0.22, 0.18)
    return jnp.clip(result, -most, most).astype(kind)


def setup_inputs(seed: int = 0) -> dict:
    key_list = jax.random.split(jax.random.key(seed), 18)
    return {
        "latent": bell_draw(key_list[0], (NODES, W), 1.0, 6.0, ((0, 768),)),
        "positions": bell_draw(key_list[1], (3, NODES), 1.0, 6.0, ((1, 768),), jnp.float32),
        "tile_send": draw_tile_send(jax.random.fold_in(key_list[17], 71), 0),
        "tile_recv": plant(jax.random.randint(key_list[3], (SLABS, GROUP, TD), 0, 3 * NB), jax.random.fold_in(key_list[3], 1), 0, (3 * NB) - 1).astype(jnp.int32),
        "tile_mask": plant((jax.random.randint(key_list[4], (SLABS, GROUP, TD, BS, BS), 0, 16) < 1).astype(jnp.int32), jax.random.fold_in(key_list[4], 1), 0, 1),
        "tile_count": draw_tile_count(jax.random.fold_in(key_list[17], 71), 0),
        "w_send": bell_draw(key_list[6], (W, W), W ** -0.5, 0.5),
        "w_recv": bell_draw(key_list[7], (W, W), W ** -0.5, 0.5),
        "pos_weight": bell_draw(key_list[8], (3, W), 3 ** -0.5, 3.5, (), jnp.float32),
        "edge_bias": bell_draw(key_list[9], (W,), 0.5, 3.0, (), jnp.float32),
        "w_edge_out": bell_draw(key_list[10], (W, W), (16 * W) ** -0.5, 0.125),
        "w_node_self": bell_draw(key_list[11], (W, W), (2 * W) ** -0.5, 0.375),
        "w_node_msg": bell_draw(key_list[12], (W, W), (2 * W) ** -0.5, 0.375),
        "node_bias": bell_draw(key_list[13], (W,), 0.5, 3.0, (), jnp.float32),
        "w_node_out": bell_draw(key_list[14], (W, W), W ** -0.5, 0.5),
        "gain": jnp.clip(1.0 + 0.1 * jax.random.normal(key_list[15], (W,), jnp.float32), 0.5, 1.5),
        "cotangent": bell_draw(key_list[16], (NODES, W), 1.0, 6.0, ((0, 768),)),
    }


def contract_rows(left_rows, right_rows):
    return lax.dot_general(left_rows, right_rows, (((0,), (0,)), ((), ())), preferred_element_type=jnp.float32)

def edge_forward(send_block, recv_block, edge_mask, with_counts):
    size_rows = recv_block.shape[0]
    width = recv_block.shape[1]
    group_rows = min(32, size_rows)
    group_count = size_rows // group_rows
    sender_values = send_block.astype(jnp.float32)

    def one_group(pieces):
        recv_part, mask_part = pieces
        preact = recv_part.astype(jnp.float32)[:, None, :] + sender_values[None, :, :]
        summed = lax.optimization_barrier(jnp.sum(mask_part[:, :, None] * jnp.maximum(preact, 0.0), axis=1))
        if with_counts:
            counted = lax.optimization_barrier(jnp.sum(mask_part[:, :, None] * (preact > 0.0).astype(jnp.float32), axis=1))
            return (summed, counted)
        return (summed,)
    results = lax.map(one_group, (recv_block.reshape(group_count, group_rows, width), edge_mask.reshape(group_count, group_rows, size_rows)))
    return tuple((item.reshape(size_rows, width) for item in results))

def edge_backward(send_block, recv_block, edge_mask, grad_block, with_recv):
    size_rows = recv_block.shape[0]
    width = recv_block.shape[1]
    group_rows = min(32, size_rows)
    group_count = size_rows // group_rows
    sender_values = send_block.astype(jnp.float32)

    def one_group(running, pieces):
        recv_part, mask_part, grad_part = pieces
        preact = recv_part.astype(jnp.float32)[:, None, :] + sender_values[None, :, :]
        terms = mask_part[:, :, None] * (preact > 0.0).astype(jnp.float32) * grad_part[:, None, :]
        running = running + lax.optimization_barrier(jnp.sum(terms, axis=0))
        if with_recv:
            return (running, lax.optimization_barrier(jnp.sum(terms, axis=1)))
        return (running, None)
    pieces = (recv_block.reshape(group_count, group_rows, width), edge_mask.reshape(group_count, group_rows, size_rows), grad_block.reshape(group_count, group_rows, width))
    send_grad, recv_grad = lax.scan(one_group, jnp.zeros((size_rows, width), jnp.float32), pieces)
    if with_recv:
        recv_grad = recv_grad.reshape(size_rows, width)
    return (send_grad, recv_grad)

def node_update(latent, aggregate, cotangent, w_edge_out, w_node_self, w_node_msg, node_bias, w_node_out, gain):
    aggregate_b = aggregate.astype(jnp.bfloat16)
    message = jnp.dot(aggregate_b, w_edge_out, preferred_element_type=jnp.float32).astype(jnp.bfloat16)
    hidden_pre = jnp.dot(latent, w_node_self, preferred_element_type=jnp.float32) + jnp.dot(message, w_node_msg, preferred_element_type=jnp.float32) + node_bias
    logistic = jax.nn.sigmoid(hidden_pre)
    hidden = (hidden_pre * logistic).astype(jnp.bfloat16)
    update = jnp.dot(hidden, w_node_out, preferred_element_type=jnp.float32)
    average = lax.optimization_barrier(jnp.mean(update, axis=-1, keepdims=True))
    centred = update - average
    variance = lax.optimization_barrier(jnp.mean(centred * centred, axis=-1, keepdims=True))
    inv_std = lax.rsqrt(variance + 1e-05)
    normed = centred * inv_std
    new_latent = (latent.astype(jnp.float32) + normed * gain).astype(jnp.bfloat16)
    cot_float = cotangent.astype(jnp.float32)
    d_normed = cot_float * gain
    d_update = (inv_std * (d_normed - lax.optimization_barrier(jnp.mean(d_normed, axis=-1, keepdims=True)) - normed * lax.optimization_barrier(jnp.mean(d_normed * normed, axis=-1, keepdims=True)))).astype(jnp.bfloat16)
    d_hidden = jnp.dot(d_update, w_node_out.T, preferred_element_type=jnp.float32)
    d_hidden_pre = (d_hidden * logistic * (1.0 + hidden_pre * (1.0 - logistic))).astype(jnp.bfloat16)
    d_message = jnp.dot(d_hidden_pre, w_node_msg.T, preferred_element_type=jnp.float32).astype(jnp.bfloat16)
    d_aggregate = jnp.dot(d_message, w_edge_out.T, preferred_element_type=jnp.float32)
    direct = cot_float + jnp.dot(d_hidden_pre, w_node_self.T, preferred_element_type=jnp.float32)
    grad_list = [contract_rows(aggregate_b, d_message), contract_rows(latent, d_hidden_pre), contract_rows(message, d_hidden_pre), contract_rows(hidden, d_update)]
    return (new_latent, d_aggregate, direct, grad_list)

def reference(latent, positions, tile_send, tile_recv, tile_mask, tile_count, w_send, w_recv, pos_weight, edge_bias, w_edge_out, w_node_self, w_node_msg, node_bias, w_node_out, gain, cotangent):
    placed = lax.dot_general(positions, pos_weight, (((0,), (0,)), ((), ())), precision=lax.Precision.HIGHEST, preferred_element_type=jnp.float32)
    send_rows = (jnp.dot(latent, w_send, preferred_element_type=jnp.float32) + placed).astype(jnp.bfloat16)
    recv_rows = (jnp.dot(latent, w_recv, preferred_element_type=jnp.float32) - placed + edge_bias).astype(jnp.bfloat16)
    slab_blocks = N_GRP * NB

    def locate(tile_index):
        slab_index = tile_index // (N_GRP * TD)
        member = tile_index // TD % N_GRP
        slot_index = tile_index % TD
        rel_send = tile_send[slab_index, member, slot_index]
        rel_recv = tile_recv[slab_index, member, slot_index]
        send_block = slab_index * slab_blocks + rel_send
        recv_slab = (slab_index + rel_recv // NB - 1 + N_BLK) % N_BLK
        recv_block = recv_slab * slab_blocks + member * NB + rel_recv % NB
        tile_alive = (slot_index < tile_count[slab_index, member]).astype(jnp.float32)
        edge_mask = tile_mask[slab_index, member, slot_index].astype(jnp.float32) * tile_alive
        return ((send_block * BS).astype(jnp.int32), (recv_block * BS).astype(jnp.int32), edge_mask)
    tile_ids = jnp.arange(N_BLK * N_GRP * TD, dtype=jnp.int32)

    def forward_step(aggregate, tile_index):
        send_start, recv_start, edge_mask = locate(tile_index)
        send_block = lax.dynamic_slice_in_dim(send_rows, send_start, BS, 0)
        recv_block = lax.dynamic_slice_in_dim(recv_rows, recv_start, BS, 0)
        added = edge_forward(send_block, recv_block, edge_mask, False)[0]
        current = lax.dynamic_slice_in_dim(aggregate, recv_start, BS, 0)
        return (lax.dynamic_update_slice_in_dim(aggregate, current + added, recv_start, 0), None)
    aggregate, unused = lax.scan(forward_step, jnp.zeros((NODES, W), jnp.float32), tile_ids)
    new_latent, d_aggregate, direct, grad_list = node_update(latent, aggregate, cotangent, w_edge_out, w_node_self, w_node_msg, node_bias, w_node_out, gain)

    def backward_step(running, tile_index):
        d_send, d_recv = running
        send_start, recv_start, edge_mask = locate(tile_index)
        send_block = lax.dynamic_slice_in_dim(send_rows, send_start, BS, 0)
        recv_block = lax.dynamic_slice_in_dim(recv_rows, recv_start, BS, 0)
        grad_block = lax.dynamic_slice_in_dim(d_aggregate, recv_start, BS, 0)
        send_part, recv_part = edge_backward(send_block, recv_block, edge_mask, grad_block, True)
        d_send = lax.dynamic_update_slice_in_dim(d_send, lax.dynamic_slice_in_dim(d_send, send_start, BS, 0) + send_part, send_start, 0)
        d_recv = lax.dynamic_update_slice_in_dim(d_recv, lax.dynamic_slice_in_dim(d_recv, recv_start, BS, 0) + recv_part, recv_start, 0)
        return ((d_send, d_recv), None)
    zero_rows = jnp.zeros((NODES, W), jnp.float32)
    (d_send, d_recv), unused = lax.scan(backward_step, (zero_rows, zero_rows), tile_ids)
    send_bf = d_send.astype(jnp.bfloat16)
    recv_bf = d_recv.astype(jnp.bfloat16)
    latent_grad = direct + jnp.dot(send_bf, w_send.T, preferred_element_type=jnp.float32) + jnp.dot(recv_bf, w_recv.T, preferred_element_type=jnp.float32)
    weight_grads = jnp.stack([contract_rows(latent, send_bf), contract_rows(latent, recv_bf)] + grad_list)
    return (new_latent, latent_grad, weight_grads)
```

```python
import functools

import jax
import jax.numpy as jnp
from jax import lax
from jax.experimental import pallas as pl
from jax.experimental.pallas import tpu as pltpu
from jax.sharding import PartitionSpec as P

F32, BF16 = jnp.float32, jnp.bfloat16
DN0 = (((0,), (0,)), ((), ()))
DN1 = (((1,), (1,)), ((), ()))
MESH = pl.DeviceIdType.MESH
SMEM = pl.BlockSpec(memory_space=pltpu.SMEM)
VM = pl.BlockSpec(memory_space=pltpu.VMEM)
NX, NY, NZ, ZLO, ZHI = 4, 8, 12, 3, 4
SLABS = NX * NY * ZLO
LIMIT = 56 << 20


class Place:
    def __init__(self):
        self.blk = lax.axis_index("blk")
        self.grp = lax.axis_index("grp")
        self.x = self.blk % NX
        self.y = (self.blk // NX) % NY
        self.zl = self.blk // (NX * NY)
        self.core = self.grp % 2
        self.zh = self.grp // 2
        self.z = self.zh * ZLO + self.zl

    def at(self, x=None, y=None, z=None, core=None):
        x = self.x if x is None else x
        y = self.y if y is None else y
        z = self.z if z is None else z
        core = self.core if core is None else core
        return ((z % ZLO) * (NX * NY) + y * NX + x, (z // ZLO) * 2 + core)

    def slab(self, step):
        return ((self.blk + step + SLABS) % SLABS, self.grp)

    def member(self, step):
        return (self.blk, ((self.zh + step + ZHI) % ZHI) * 2 + self.core)

    def partner(self):
        return (self.blk, self.zh * 2 + 1 - self.core)


def meet(peers):
    barrier = pltpu.get_barrier_semaphore()
    for peer in peers:
        pl.semaphore_signal(barrier, inc=1, device_id=peer, device_id_type=MESH)
    pl.semaphore_wait(barrier, len(peers))


class Copies:
    def __init__(self, send_sem, recv_sem):
        self.send_sem, self.recv_sem, self.started = send_sem, recv_sem, []

    def start(self, src, dst, device):
        number = len(self.started)
        copy = pltpu.make_async_remote_copy(
            src_ref=src, dst_ref=dst, send_sem=self.send_sem.at[number],
            recv_sem=self.recv_sem.at[number], device_id=device, device_id_type=MESH)
        copy.start()
        self.started.append(copy)
        return copy

    def sent(self):
        for copy in self.started:
            copy.wait_send()


def sd(shape, dtype):
    return jax.ShapeDtypeStruct(shape, dtype)


def dot(a, b):
    return jnp.dot(a, b, preferred_element_type=F32)


def dot_t(a, b):
    return lax.dot_general(a, b, DN1, preferred_element_type=F32)


def contract(a, b):
    return lax.dot_general(a, b, DN0, preferred_element_type=F32)


GATHER_COPIES = 24


def gather_kernel(lat, pos, lat_all, pos_all, lat_nb, pos_nb, send_sem, recv_sem):
    me = Place()
    own = lat.shape[0]
    g = me.grp
    up, dn, sib = me.member(1), me.member(-1), me.partner()
    nxt, prv = me.slab(1), me.slab(-1)
    meet([up, dn, sib, nxt, prv])
    cs = Copies(send_sem, recv_sem)
    halves = (pl.ds(0, own // 2), pl.ds(own // 2, own // 2))

    def half(index, h):
        return lat_all.at[index, halves[h]]

    up_pos = cs.start(pos, pos_all.at[g], up)
    dn_pos = cs.start(pos, pos_all.at[g], dn)
    up_a = cs.start(lat.at[halves[0]], half(g, 0), up)
    dn_b = cs.start(lat.at[halves[1]], half(g, 1), dn)
    up_b = cs.start(lat.at[halves[1]], half(g, 1), up)
    dn_a = cs.start(lat.at[halves[0]], half(g, 0), dn)
    waits = [
        cs.start(lat, lat_nb.at[0], nxt),
        cs.start(lat, lat_nb.at[1], prv),
        cs.start(pos, pos_nb.at[0], nxt),
        cs.start(pos, pos_nb.at[1], prv),
        cs.start(lat, lat_all.at[g], sib),
        cs.start(pos, pos_all.at[g], sib),
    ]
    lat_all[g] = lat[...]
    pos_all[g] = pos[...]
    iu, idn, far = up[1], dn[1], me.member(2)[1]

    def pass_on(ref):
        waits.append(cs.start(ref, ref, sib))

    up_pos.wait_recv()
    far_pos = cs.start(pos_all.at[idn], pos_all.at[idn], up)
    pass_on(pos_all.at[idn])
    dn_pos.wait_recv()
    pass_on(pos_all.at[iu])
    up_a.wait_recv()
    far_a = cs.start(half(idn, 0), half(idn, 0), up)
    pass_on(half(idn, 0))
    dn_b.wait_recv()
    far_b = cs.start(half(iu, 1), half(iu, 1), dn)
    pass_on(half(iu, 1))
    up_b.wait_recv()
    pass_on(half(idn, 1))
    dn_a.wait_recv()
    pass_on(half(iu, 0))
    far_pos.wait_recv()
    pass_on(pos_all.at[far])
    far_a.wait_recv()
    pass_on(half(far, 0))
    far_b.wait_recv()
    pass_on(half(far, 1))
    for copy in waits:
        copy.wait_recv()
    cs.sent()


def gather(lat, pos):
    own = lat.shape[0]
    n = GATHER_COPIES
    return pl.pallas_call(
        gather_kernel,
        out_shape=[sd((8, own, 128), BF16), sd((8, 3, own), F32), sd((2, own, 128), BF16),
                   sd((2, 3, own), F32)],
        in_specs=[VM] * 2,
        out_specs=[VM] * 4,
        scratch_shapes=[pltpu.SemaphoreType.DMA((n,)), pltpu.SemaphoreType.DMA((n,))],
        compiler_params=pltpu.CompilerParams(collective_id=0, has_side_effects=True),
        name="gather",
    )(lat, pos)


NODE_COPIES = 6


def node_kernel(agg_own, agg_nb, cnt_own, cnt_nb, lat, cot, w_edge_out, w_node_self, w_node_msg,
                node_bias, w_node_out, gain, w_recv, new_lat, dagg, part, grads, agg_in, cnt_in,
                send_sem, recv_sem):
    me = Place()
    nxt, prv = me.slab(1), me.slab(-1)
    meet([nxt, prv])
    cs = Copies(send_sem, recv_sem)
    a_prv = cs.start(agg_nb.at[0], agg_in.at[0], prv)
    a_nxt = cs.start(agg_nb.at[1], agg_in.at[1], nxt)
    c_prv = cs.start(cnt_nb.at[0], cnt_in.at[0], prv)
    c_nxt = cs.start(cnt_nb.at[1], cnt_in.at[1], nxt)
    latent = lat[...]
    self_pre = dot(latent, w_node_self[...]) + node_bias[...]
    a_prv.wait_recv()
    a_nxt.wait_recv()
    aggregate = agg_own[...] + agg_in[0].astype(F32) + agg_in[1].astype(F32)
    aggregate_b = aggregate.astype(BF16)
    message = dot(aggregate_b, w_edge_out[...]).astype(BF16)
    hidden_pre = self_pre + dot(message, w_node_msg[...])
    logistic = jax.nn.sigmoid(hidden_pre)
    hidden = (hidden_pre * logistic).astype(BF16)
    update = dot(hidden, w_node_out[...])
    average = jnp.mean(update, axis=-1, keepdims=True)
    centred = update - average
    variance = jnp.mean(centred * centred, axis=-1, keepdims=True)
    inv_std = lax.rsqrt(variance + 1e-05)
    normed = centred * inv_std
    new_lat[...] = (latent.astype(F32) + normed * gain[...]).astype(BF16)
    c = cot[...].astype(F32)
    d_normed = c * gain[...]
    d_update = (inv_std * (d_normed - jnp.mean(d_normed, axis=-1, keepdims=True)
                           - normed * jnp.mean(d_normed * normed, axis=-1, keepdims=True))
                ).astype(BF16)
    d_hidden = dot_t(d_update, w_node_out[...])
    d_hidden_pre = (d_hidden * logistic * (1.0 + hidden_pre * (1.0 - logistic))).astype(BF16)
    d_message = dot_t(d_hidden_pre, w_node_msg[...]).astype(BF16)
    d_aggregate = dot_t(d_message, w_edge_out[...])
    dagg[1] = d_aggregate.astype(BF16)
    d_nxt = cs.start(dagg.at[1], dagg.at[0], nxt)
    d_prv = cs.start(dagg.at[1], dagg.at[2], prv)
    grads[1] = contract(aggregate_b, d_message)
    grads[2] = contract(latent, d_hidden_pre)
    grads[3] = contract(message, d_hidden_pre)
    grads[4] = contract(hidden, d_update)
    direct = c + dot_t(d_hidden_pre, w_node_self[...])
    c_prv.wait_recv()
    c_nxt.wait_recv()
    count = cnt_own[...] + cnt_in[0].astype(F32) + cnt_in[1].astype(F32)
    d_recv = (count * d_aggregate).astype(BF16)
    grads[0] = contract(latent, d_recv)
    part[...] = direct + dot_t(d_recv, w_recv[...])
    d_nxt.wait_recv()
    d_prv.wait_recv()
    cs.sent()


def node(agg_own, agg_nb, cnt_own, cnt_nb, lat, cot, *weights):
    own = lat.shape[0]
    n = NODE_COPIES
    return pl.pallas_call(
        node_kernel,
        out_shape=[sd((own, 128), BF16), sd((3, own, 128), BF16), sd((own, 128), F32),
                   sd((5, 128, 128), F32)],
        in_specs=[VM] * 13,
        out_specs=[VM] * 4,
        scratch_shapes=[pltpu.VMEM((2, own, 128), BF16), pltpu.VMEM((2, own, 128), BF16),
                        pltpu.SemaphoreType.DMA((n,)), pltpu.SemaphoreType.DMA((n,))],
        compiler_params=pltpu.CompilerParams(collective_id=1, has_side_effects=True),
        name="node",
    )(agg_own, agg_nb, cnt_own, cnt_nb, lat, cot, *weights)


FINAL_COPIES = 43


def final_kernel(dsend, gsend, grads, part, w_send, latent_grad, weight_grads, v, in_core, vx, in_x,
                 vy, in_y, in_z, out_y, out_x, out_core, rs_core, cs_sum, in_ra, in_rb, in_da, in_db,
                 in_fa, in_fb, fwd_a, fwd_b, vz, send_sem, recv_sem):
    me = Place()
    own = part.shape[0]
    up, dn, sib = me.member(1), me.member(-1), me.partner()
    core, zh = me.core, me.zh
    mats = [gsend[...]] + [grads[i] for i in range(5)]
    zero = jnp.zeros((128, 128), BF16)
    for i in range(8):
        v[i // 4, i % 4] = mats[i].astype(BF16) if i < 6 else zero
    xs = [me.at(x=(me.x + d) % NX) for d in range(1, NX)]
    ys = [me.at(y=(me.y + d) % NY) for d in range(1, NY)]
    zs = [me.at(z=(me.z + d) % NZ) for d in range(1, NZ)]
    meet([sib] + xs + ys + zs)
    cs = Copies(send_sem, recv_sem)
    ha, hb = pl.ds(0, own // 2), pl.ds(own // 2, own // 2)

    ar_core = cs.start(v.at[1 - core], in_core, sib)
    order = [2, 1, 3, 0]
    rs = [cs.start(dsend.at[((zh + o) % ZHI) * 2 + 1 - core], rs_core.at[(zh + o) % ZHI], sib)
          for o in order]
    ar_core.wait_recv()
    vx[...] = (v[core].astype(F32) + in_core[...].astype(F32)).astype(BF16)
    ar_x = [cs.start(vx.at[(me.x + d) % NX], in_x.at[d - 1], xs[d - 1]) for d in range(1, NX)]

    def chip_sum(i):
        rs[i].wait_recv()
        k = (zh + order[i]) % ZHI
        cs_sum[k] = (dsend[k * 2 + core].astype(F32) + rs_core[k].astype(F32)).astype(BF16)
        return k

    far = chip_sum(0)
    ra = cs.start(cs_sum.at[far, ha], in_ra, up)
    rb = cs.start(cs_sum.at[far, hb], in_rb, dn)
    ku = chip_sum(1)
    db = cs.start(cs_sum.at[ku, hb], in_db, up)
    kd = chip_sum(2)
    da = cs.start(cs_sum.at[kd, ha], in_da, dn)
    chip_sum(3)

    for copy in ar_x:
        copy.wait_recv()
    total = vx[me.x].astype(F32)
    for d in range(NX - 1):
        total = total + in_x[d].astype(F32)
    vy[...] = total.astype(BF16).reshape(NY, 16, 128)
    ar_y = [cs.start(vy.at[(me.y + d) % NY], in_y.at[d - 1], ys[d - 1]) for d in range(1, NY)]

    for copy in ar_y:
        copy.wait_recv()
    total = vy[me.y].astype(F32)
    for d in range(NY - 1):
        total = total + in_y[d].astype(F32)
    vz[...] = total.astype(BF16)
    in_z[me.z] = total.astype(BF16)
    ar_z = [cs.start(vz, in_z.at[me.z], zs[d - 1]) for d in range(1, NZ)]

    ra.wait_recv()
    fwd_a[...] = (in_ra[...].astype(F32) + cs_sum[ku, ha].astype(F32)).astype(BF16)
    fa = cs.start(fwd_a, in_fa, up)
    rb.wait_recv()
    fwd_b[...] = (in_rb[...].astype(F32) + cs_sum[kd, hb].astype(F32)).astype(BF16)
    fb = cs.start(fwd_b, in_fb, dn)

    for copy in ar_z:
        copy.wait_recv()
    total = in_z[0].astype(F32)
    for d in range(1, NZ):
        total = total + in_z[d].astype(F32)
    mine = pl.ds(pl.multiple_of(me.y * 16, 16), 16)
    out_y[mine] = total.astype(BF16)
    ag_y = [cs.start(out_y.at[mine], out_y.at[mine], ys[d - 1]) for d in range(1, NY)]

    da.wait_recv()
    db.wait_recv()
    fa.wait_recv()
    d_a = cs_sum[zh, ha].astype(F32) + in_da[...].astype(F32) + in_fa[...].astype(F32)
    latent_grad[ha] = part[ha] + dot_t(d_a.astype(BF16), w_send[...])
    fb.wait_recv()
    d_b = cs_sum[zh, hb].astype(F32) + in_db[...].astype(F32) + in_fb[...].astype(F32)
    latent_grad[hb] = part[hb] + dot_t(d_b.astype(BF16), w_send[...])

    for copy in ag_y:
        copy.wait_recv()
    out_x[me.x] = out_y[...]
    ag_x = [cs.start(out_y, out_x.at[me.x], xs[d - 1]) for d in range(1, NX)]
    for copy in ag_x:
        copy.wait_recv()
    out_core[core] = out_x[...]
    ag_core = cs.start(out_x, out_core.at[core], sib)
    ag_core.wait_recv()
    for i in range(6):
        weight_grads[i] = out_core[i // 4, i % 4].astype(F32)
    cs.sent()


def final(dsend, gsend, grads, part, w_send):
    own = part.shape[0]
    n = FINAL_COPIES
    b = lambda *shape: pltpu.VMEM(shape, BF16)
    h = own // 2
    return pl.pallas_call(
        final_kernel,
        out_shape=[sd((own, 128), F32), sd((6, 128, 128), F32)],
        in_specs=[VM] * 5,
        out_specs=[VM] * 2,
        scratch_shapes=[
            b(2, NX, 128, 128), b(NX, 128, 128), b(NX, 128, 128), b(NX - 1, 128, 128),
            b(NY, 16, 128), b(NY - 1, 16, 128), b(NZ, 16, 128), b(128, 128),
            b(NX, 128, 128), b(2, NX, 128, 128), b(ZHI, own, 128), b(ZHI, own, 128),
            b(h, 128), b(h, 128), b(h, 128), b(h, 128), b(h, 128), b(h, 128), b(h, 128), b(h, 128),
            b(16, 128),
            pltpu.SemaphoreType.DMA((n,)), pltpu.SemaphoreType.DMA((n,))],
        compiler_params=pltpu.CompilerParams(collective_id=2, has_side_effects=True),
        name="final",
    )(dsend, gsend, grads, part, w_send)


def placed_of(pos, pw):
    return lax.dot_general(pos, pw, DN0, precision=lax.Precision.HIGHEST,
                           preferred_element_type=F32)


def rank_rows(mb, upper):
    before = dot(mb, upper)
    return jnp.where(mb > 0, before, -1.0).astype(BF16)


def forward_kernel(NS, ts, tr, tc, lat_all, pos_all, lat_nb, pos_nb, lat, pos, mask, w_send,
                   w_recv, pw, bias, agg_own, agg_nb, cnt_own, cnt_nb, s_out, r_out, rank_t, kout,
                   rank_r, deg_s, rf, agg, cnt, kvec, ksm, sem):
    tiles = mask.shape[0]
    row = lax.broadcasted_iota(jnp.int32, (128, 128), 0)
    col = lax.broadcasted_iota(jnp.int32, (128, 128), 1)
    upper = jnp.where(row < col, 1.0, 0.0).astype(BF16)
    ones = jnp.ones((128, 128), BF16)

    def prep(t, _):
        mf = mask[t].astype(F32)
        mb = mf.astype(BF16)
        rank_r[t] = rank_rows(mb, upper)
        deg = dot(mb, ones)
        deg_s[t] = deg
        kvec[pl.ds(t, 1), :] = jnp.max(deg, axis=0, keepdims=True).astype(jnp.int32)
        mtb = mf.T.astype(BF16)
        rank_t[t] = rank_rows(mtb, upper)
        degt = dot(mtb, ones)
        kvec[pl.ds(t + tiles, 1), :] = jnp.max(degt, axis=0, keepdims=True).astype(jnp.int32)
        return 0

    lax.fori_loop(0, tiles, prep, 0)
    cp = pltpu.make_async_copy(kvec, ksm, sem)
    cp.start()
    kout[...] = kvec[...]

    for slab in range(3):
        la = lat[...] if slab == 1 else lat_nb[slab // 2]
        po = pos[...] if slab == 1 else pos_nb[slab // 2]
        rr = (dot(la, w_recv[...]) - placed_of(po, pw[...]) + bias[...]).astype(BF16)
        for b in range(4):
            r_out[slab * 4 + b] = rr[b * 128:(b + 1) * 128]
            rf[slab * 4 + b] = rr[b * 128:(b + 1) * 128].astype(F32)
    agg[...] = jnp.zeros_like(agg)
    cnt[...] = jnp.zeros_like(cnt)
    cp.wait()

    def tile(t, _):
        sb = ts[t]
        rb = tr[t]
        g = sb // 4
        b = sb % 4
        po = pos_all[g, :, pl.ds(pl.multiple_of(b * 128, 128), 128)]
        s = (dot(lat_all[sb], w_send[...]) + placed_of(po, pw[...])).astype(BF16)
        s_out[t] = s
        r = rf[rb]
        kmax = ksm[t, 0]
        n = (kmax + NS - 1) // NS
        rk = rank_r[t]

        def slot(i, carry):
            a, c = carry
            base = i * NS
            for q in range(NS):
                kk = (base + q).astype(F32).astype(BF16)
                p = jnp.where(rk == kk, jnp.ones((), BF16), jnp.zeros((), BF16))
                pre = dot(p, s) + r
                a = a + jnp.maximum(pre, 0.0)
                c = c + jnp.where(pre > 0.0, 1.0, 0.0)
            return a, c

        z = jnp.zeros((128, 128), F32)
        a, c = lax.fori_loop(0, n, slot, (z, z))
        spare = (n * NS).astype(F32) - deg_s[t]
        agg[rb] += a - spare * jnp.maximum(r, 0.0)
        cnt[rb] += c - spare * jnp.where(r > 0.0, 1.0, 0.0)
        return 0

    lax.fori_loop(0, tc[0], tile, 0)
    for b in range(4):
        sl = pl.ds(b * 128, 128)
        agg_own[sl] = agg[4 + b]
        cnt_own[sl] = cnt[4 + b]
        agg_nb[0, sl] = agg[b].astype(BF16)
        agg_nb[1, sl] = agg[8 + b].astype(BF16)
        cnt_nb[0, sl] = cnt[b].astype(BF16)
        cnt_nb[1, sl] = cnt[8 + b].astype(BF16)


def forward(ts, tr, tc, lat_all, pos_all, lat_nb, pos_nb, lat, pos, mask, w_send, w_recv, pw, bias,
            NS=4):
    own = lat.shape[0]
    T = mask.shape[0]
    return pl.pallas_call(
        functools.partial(forward_kernel, NS),
        out_shape=[sd((own, 128), F32), sd((2, own, 128), BF16), sd((own, 128), F32),
                   sd((2, own, 128), BF16), sd((T, 128, 128), BF16), sd((12, 128, 128), BF16),
                   sd((T, 128, 128), BF16), sd((2 * T, 128), jnp.int32)],
        in_specs=[SMEM] * 3 + [VM] * 11,
        out_specs=[VM] * 8,
        scratch_shapes=[pltpu.VMEM((T, 128, 128), BF16), pltpu.VMEM((T, 128, 128), F32),
                        pltpu.VMEM((12, 128, 128), F32), pltpu.VMEM((12, 128, 128), F32),
                        pltpu.VMEM((12, 128, 128), F32), pltpu.VMEM((2 * T, 128), jnp.int32),
                        pltpu.SMEM((2 * T, 128), jnp.int32), pltpu.SemaphoreType.DMA(())],
        compiler_params=pltpu.CompilerParams(vmem_limit_bytes=LIMIT),
        name="forward",
    )(ts, tr, tc, lat_all, pos_all, lat_nb, pos_nb, lat, pos, mask, w_send, w_recv, pw, bias)


def backward_kernel(NS, ts, tr, tc, ksm, rank_t, s_in, r_in, dagg, lat_all, dsend, gsend, acc):
    acc[...] = jnp.zeros_like(acc)
    tiles = rank_t.shape[0]

    def tile(t, _):
        sb = ts[t]
        rb = tr[t]
        s = s_in[t].astype(F32)
        rhs = jnp.concatenate([r_in[rb], dagg[rb]], axis=1)
        kmax = ksm[t + tiles, 0]
        n = (kmax + NS - 1) // NS
        rk = rank_t[t]

        def slot(i, a):
            base = i * NS
            for q in range(NS):
                kk = (base + q).astype(F32).astype(BF16)
                p = jnp.where(rk == kk, jnp.ones((), BF16), jnp.zeros((), BF16))
                x = dot(p, rhs)
                a = a + jnp.where(x[:, :128] + s > 0.0, x[:, 128:], 0.0)
            return a

        a = lax.fori_loop(0, n, slot, jnp.zeros((128, 128), F32))
        acc[sb] += a
        return 0

    lax.fori_loop(0, tc[0], tile, 0)
    g = jnp.zeros((128, 128), F32)
    for b in range(8):
        d = acc[pl.ds(4 * b, 4)].reshape(512, 128).astype(BF16)
        dsend[b] = d
        g = g + lax.dot_general(lat_all[b], d, DN0, preferred_element_type=F32)
    gsend[...] = g


def backward(ts, tr, tc, kout, rank_t, s_in, r_in, dagg, lat_all, NS=4):
    return pl.pallas_call(
        functools.partial(backward_kernel, NS),
        out_shape=[sd((8, 512, 128), BF16), sd((128, 128), F32)],
        in_specs=[SMEM] * 4 + [VM] * 5,
        out_specs=[VM] * 2,
        scratch_shapes=[pltpu.VMEM((32, 128, 128), F32)],
        compiler_params=pltpu.CompilerParams(vmem_limit_bytes=LIMIT),
        name="backward",
    )(ts, tr, tc, kout, rank_t, s_in, r_in, dagg, lat_all)


def body(latent, positions, tile_send, tile_recv, tile_mask, tile_count, w_send, w_recv, pos_weight,
         edge_bias, w_edge_out, w_node_self, w_node_msg, node_bias, w_node_out, gain, cotangent):
    own = latent.shape[0]
    ts, tr, tc = tile_send[0, 0], tile_recv[0, 0], tile_count[0]
    lat_all, pos_all, lat_nb, pos_nb = gather(latent, positions)
    agg_own, agg_nb, cnt_own, cnt_nb, s_rows, r_rows, rank_t, slots = forward(
        ts, tr, tc, lat_all.reshape(32, 128, 128), pos_all, lat_nb, pos_nb, latent, positions,
        tile_mask[0, 0], w_send, w_recv, pos_weight, edge_bias[None])
    new_latent, dagg, part, grads = node(
        agg_own, agg_nb, cnt_own, cnt_nb, latent, cotangent, w_edge_out, w_node_self, w_node_msg,
        node_bias[None], w_node_out, gain[None], w_recv)
    dsend, gsend = backward(ts, tr, tc, slots, rank_t, s_rows, r_rows, dagg.reshape(12, 128, 128),
                            lat_all)
    latent_grad, weight_grads = final(dsend, gsend, grads, part, w_send)
    return new_latent, latent_grad, weight_grads


def solution(mesh):
    in_specs = (
        P(("blk", "grp"), None),
        P(None, ("blk", "grp")),
        P("blk", "grp", None),
        P("blk", "grp", None),
        P("blk", "grp", None, None, None),
        P("blk", "grp"),
        P(),
        P(),
        P(),
        P(),
        P(),
        P(),
        P(),
        P(),
        P(),
        P(),
        P(("blk", "grp"), None),
    )
    out_specs = (P(("blk", "grp"), None), P(("blk", "grp"), None), P())
    return jax.shard_map(body, mesh=mesh, in_specs=in_specs, out_specs=out_specs, check_vma=False)
```

```python
import functools

import jax
import jax.numpy as jnp
from jax import lax
from jax.experimental import pallas as pl
from jax.experimental.pallas import tpu as pltpu
from jax.sharding import PartitionSpec as P

F32, BF16 = jnp.float32, jnp.bfloat16
DN0 = (((0,), (0,)), ((), ()))
DN1 = (((1,), (1,)), ((), ()))
MESH = pl.DeviceIdType.MESH
SMEM = pl.BlockSpec(memory_space=pltpu.SMEM)
VM = pl.BlockSpec(memory_space=pltpu.VMEM)
NX, NY, NZ, ZLO, ZHI = 4, 8, 12, 3, 4
SLABS = NX * NY * ZLO
LIMIT = 56 << 20


class Place:
    def __init__(self):
        self.blk = lax.axis_index("blk")
        self.grp = lax.axis_index("grp")
        self.x = self.blk % NX
        self.y = (self.blk // NX) % NY
        self.zl = self.blk // (NX * NY)
        self.core = self.grp % 2
        self.zh = self.grp // 2
        self.z = self.zh * ZLO + self.zl

    def at(self, x=None, y=None, z=None, core=None):
        x = self.x if x is None else x
        y = self.y if y is None else y
        z = self.z if z is None else z
        core = self.core if core is None else core
        return ((z % ZLO) * (NX * NY) + y * NX + x, (z // ZLO) * 2 + core)

    def slab(self, step):
        return ((self.blk + step + SLABS) % SLABS, self.grp)

    def member(self, step):
        return (self.blk, ((self.zh + step + ZHI) % ZHI) * 2 + self.core)

    def partner(self):
        return (self.blk, self.zh * 2 + 1 - self.core)


def meet(peers):
    barrier = pltpu.get_barrier_semaphore()
    for peer in peers:
        pl.semaphore_signal(barrier, inc=1, device_id=peer, device_id_type=MESH)
    pl.semaphore_wait(barrier, len(peers))


class Copies:
    def __init__(self, send_sem, recv_sem):
        self.send_sem, self.recv_sem, self.started = send_sem, recv_sem, []

    def start(self, src, dst, device):
        number = len(self.started)
        copy = pltpu.make_async_remote_copy(
            src_ref=src, dst_ref=dst, send_sem=self.send_sem.at[number],
            recv_sem=self.recv_sem.at[number], device_id=device, device_id_type=MESH)
        copy.start()
        self.started.append(copy)
        return copy

    def sent(self):
        for copy in self.started:
            copy.wait_send()


def sd(shape, dtype):
    return jax.ShapeDtypeStruct(shape, dtype)


def dot(a, b):
    return jnp.dot(a, b, preferred_element_type=F32)


def dot_t(a, b):
    return lax.dot_general(a, b, DN1, preferred_element_type=F32)


def contract(a, b):
    return lax.dot_general(a, b, DN0, preferred_element_type=F32)


def placed_of(pos, pw):
    return lax.dot_general(pos, pw, DN0, precision=lax.Precision.HIGHEST,
                           preferred_element_type=F32)


def rank_tiles(mask, rank_r, rank_t, top):
    tiles = mask.shape[0]
    row = lax.broadcasted_iota(jnp.int32, (128, 128), 0)
    col = lax.broadcasted_iota(jnp.int32, (128, 128), 1)
    upper = jnp.where(row < col, 1.0, 0.0).astype(BF16)

    def ranks(values):
        return jnp.where(values > 0.0, dot(values.astype(BF16), upper), -1.0)

    def tile(t, _):
        values = mask[t].astype(F32)
        by_row = ranks(values)
        rank_r[t] = by_row.astype(BF16)
        top[pl.ds(t, 1), :] = jnp.max(by_row, axis=0, keepdims=True)
        by_col = ranks(values.T)
        rank_t[t] = by_col.astype(BF16)
        top[pl.ds(t + tiles, 1), :] = jnp.max(by_col, axis=0, keepdims=True)
        return 0

    lax.fori_loop(0, tiles, tile, 0)


def slot_counts(top):
    most = jnp.max(top[...], axis=1, keepdims=True) + 1.0
    return jnp.broadcast_to(most, top.shape).astype(jnp.int32)


def picks(ranks, slot):
    one, none = jnp.ones((), BF16), jnp.zeros((), BF16)
    if isinstance(slot, int):
        slot = jnp.full((), slot, BF16)
    else:
        slot = slot.astype(F32).astype(BF16)
    return jnp.where(ranks == slot, one, none)


def forward_kernel(first, more, ts, tr, tc, most, s_rows, r_rows, rank_r, agg_own, agg_nb, cnt_own,
                   cnt_nb, agg, cnt):
    agg[...] = jnp.zeros_like(agg)
    cnt[...] = jnp.zeros_like(cnt)
    ones = jnp.ones((128, 128), BF16)

    def tile(t, _):
        rb = tr[t]
        s = s_rows[ts[t]]
        rk = rank_r[t]
        floor = -(r_rows[rb].astype(F32))

        def add(slot, a, c):
            x = dot(picks(rk, slot), s)
            return a + jnp.maximum(x, floor), c + jnp.where(x > floor, 1.0, 0.0)

        a = jnp.zeros((128, 128), F32)
        c = jnp.zeros((128, 128), F32)
        for slot in range(first):
            a, c = add(slot, a, c)
        n = (jnp.maximum(most[t, 0] - first, 0) + more - 1) // more

        def rest(i, carry):
            a, c = carry
            for q in range(more):
                a, c = add(first + i * more + q, a, c)
            return a, c

        a, c = lax.fori_loop(0, n, rest, (a, c))
        degree = dot(jnp.where(rk >= jnp.zeros((), BF16), jnp.ones((), BF16), jnp.zeros((), BF16)), ones)
        spare = (first + n * more).astype(F32) - degree
        agg[rb] += a - degree * floor - spare * jnp.maximum(floor, 0.0)
        cnt[rb] += c - spare * jnp.where(floor < 0.0, 1.0, 0.0)
        return 0

    lax.fori_loop(0, tc[0], tile, 0)
    for b in range(4):
        sl = pl.ds(b * 128, 128)
        agg_own[sl] = agg[4 + b]
        cnt_own[sl] = cnt[4 + b]
        agg_nb[0, sl] = agg[b].astype(BF16)
        agg_nb[1, sl] = agg[8 + b].astype(BF16)
        cnt_nb[0, sl] = cnt[b].astype(BF16)
        cnt_nb[1, sl] = cnt[8 + b].astype(BF16)


def forward(ts, tr, tc, most, s_rows, r_rows, rank_r, first=18, more=4):
    own = 512
    return pl.pallas_call(
        functools.partial(forward_kernel, first, more),
        out_shape=[sd((own, 128), F32), sd((2, own, 128), BF16), sd((own, 128), F32),
                   sd((2, own, 128), BF16)],
        in_specs=[SMEM] * 4 + [VM] * 3,
        out_specs=[VM] * 4,
        scratch_shapes=[pltpu.VMEM((12, 128, 128), F32), pltpu.VMEM((12, 128, 128), F32)],
        compiler_params=pltpu.CompilerParams(vmem_limit_bytes=LIMIT),
        name="forward",
    )(ts, tr, tc, most, s_rows, r_rows, rank_r)


def backward_kernel(first, more, ts, tr, tc, most, rank_t, s_rows, r_rows, dagg, lat_all, dsend,
                    gsend, acc):
    acc[...] = jnp.zeros_like(acc)
    tiles = rank_t.shape[0]

    def tile(t, _):
        sb = ts[t]
        rb = tr[t]
        floor = -(s_rows[sb].astype(F32))
        rhs = jnp.concatenate([r_rows[rb], dagg[rb]], axis=1)
        rk = rank_t[t]

        def add(slot, a):
            x = dot(picks(rk, slot), rhs)
            return a + jnp.where(x[:, :128] > floor, x[:, 128:], 0.0)

        a = jnp.zeros((128, 128), F32)
        for slot in range(first):
            a = add(slot, a)
        n = (jnp.maximum(most[t + tiles, 0] - first, 0) + more - 1) // more

        def rest(i, a):
            for q in range(more):
                a = add(first + i * more + q, a)
            return a

        acc[sb] += lax.fori_loop(0, n, rest, a)
        return 0

    lax.fori_loop(0, tc[0], tile, 0)
    g = jnp.zeros((128, 128), F32)
    for b in range(8):
        d = acc[pl.ds(4 * b, 4)].reshape(512, 128).astype(BF16)
        dsend[b] = d
        g = g + contract(lat_all[b], d)
    gsend[...] = g


def backward(ts, tr, tc, most, rank_t, s_rows, r_rows, dagg, lat_all, first=18, more=4):
    return pl.pallas_call(
        functools.partial(backward_kernel, first, more),
        out_shape=[sd((8, 512, 128), BF16), sd((128, 128), F32)],
        in_specs=[SMEM] * 4 + [VM] * 5,
        out_specs=[VM] * 2,
        scratch_shapes=[pltpu.VMEM((32, 128, 128), F32)],
        compiler_params=pltpu.CompilerParams(vmem_limit_bytes=LIMIT),
        name="backward",
    )(ts, tr, tc, most, rank_t, s_rows, r_rows, dagg, lat_all)


GATHER_COPIES = 24


def gather_kernel(lat, pos, w_send, w_recv, pw, bias, mask_in, lat_all, s_rows, r_rows, rank_r,
                  rank_t, most, mask, top, pos_all, lat_nb, pos_nb, mask_sem, send_sem, recv_sem):
    load = pltpu.make_async_copy(mask_in, mask, mask_sem)
    load.start()
    me = Place()
    own = lat.shape[0]
    g = me.grp
    up, dn, sib = me.member(1), me.member(-1), me.partner()
    nxt, prv = me.slab(1), me.slab(-1)
    meet([up, dn, sib, nxt, prv])
    cs = Copies(send_sem, recv_sem)
    halves = (pl.ds(0, own // 2), pl.ds(own // 2, own // 2))

    def half(index, h):
        return lat_all.at[index, halves[h]]

    up_pos = cs.start(pos, pos_all.at[g], up)
    dn_pos = cs.start(pos, pos_all.at[g], dn)
    up_a = cs.start(lat.at[halves[0]], half(g, 0), up)
    dn_b = cs.start(lat.at[halves[1]], half(g, 1), dn)
    up_b = cs.start(lat.at[halves[1]], half(g, 1), up)
    dn_a = cs.start(lat.at[halves[0]], half(g, 0), dn)
    beside = [
        cs.start(lat, lat_nb.at[0], nxt),
        cs.start(lat, lat_nb.at[1], prv),
        cs.start(pos, pos_nb.at[0], nxt),
        cs.start(pos, pos_nb.at[1], prv),
    ]
    partner = [
        cs.start(lat, lat_all.at[g], sib),
        cs.start(pos, pos_all.at[g], sib),
    ]
    lat_all[g] = lat[...]
    pos_all[g] = pos[...]
    iu, idn, far = up[1], dn[1], me.member(2)[1]

    def pass_on(ref):
        return cs.start(ref, ref, sib)

    def send_rows(index):
        s_rows[index] = (dot(lat_all[index], w_send[...])
                         + placed_of(pos_all[index], pw[...])).astype(BF16)

    def recv_rows(slab, rows, places):
        r_rows[slab] = (dot(rows, w_recv[...]) - placed_of(places, pw[...])
                        + bias[...]).astype(BF16)

    def other(index):
        return (index // 2) * 2 + 1 - me.core

    recv_rows(1, lat[...], pos[...])
    send_rows(g)
    load.wait()
    rank_tiles(mask, rank_r, rank_t, top)
    most[...] = slot_counts(top)

    up_pos.wait_recv()
    far_pos = cs.start(pos_all.at[idn], pos_all.at[idn], up)
    near = [pass_on(pos_all.at[idn])]
    dn_pos.wait_recv()
    near.append(pass_on(pos_all.at[iu]))
    up_a.wait_recv()
    far_a = cs.start(half(idn, 0), half(idn, 0), up)
    near.append(pass_on(half(idn, 0)))
    dn_b.wait_recv()
    far_b = cs.start(half(iu, 1), half(iu, 1), dn)
    near.append(pass_on(half(iu, 1)))
    for copy in beside + partner:
        copy.wait_recv()
    recv_rows(0, lat_nb[0], pos_nb[0])
    recv_rows(2, lat_nb[1], pos_nb[1])
    send_rows(sib[1])
    up_b.wait_recv()
    near.append(pass_on(half(idn, 1)))
    send_rows(idn)
    dn_a.wait_recv()
    near.append(pass_on(half(iu, 0)))
    send_rows(iu)
    far_pos.wait_recv()
    last = [pass_on(pos_all.at[far])]
    for copy in near:
        copy.wait_recv()
    send_rows(other(idn))
    send_rows(other(iu))
    far_a.wait_recv()
    last.append(pass_on(half(far, 0)))
    far_b.wait_recv()
    last.append(pass_on(half(far, 1)))
    send_rows(far)
    for copy in last:
        copy.wait_recv()
    send_rows(other(far))
    cs.sent()


def gather(lat, pos, w_send, w_recv, pw, bias, mask):
    own = lat.shape[0]
    n = GATHER_COPIES
    tiles = mask.shape[0]
    ranks = sd((tiles, 128, 128), BF16)
    return pl.pallas_call(
        gather_kernel,
        out_shape=[sd((8, own, 128), BF16), sd((8, own, 128), BF16), sd((3, own, 128), BF16),
                   ranks, ranks, sd((2 * tiles, 128), jnp.int32)],
        in_specs=[VM] * 6 + [pl.BlockSpec(memory_space=pl.ANY)],
        out_specs=[VM] * 6,
        scratch_shapes=[pltpu.VMEM((tiles, 128, 128), jnp.int32), pltpu.VMEM((2 * tiles, 128), F32),
                        pltpu.VMEM((8, 3, own), F32), pltpu.VMEM((2, own, 128), BF16),
                        pltpu.VMEM((2, 3, own), F32), pltpu.SemaphoreType.DMA(()),
                        pltpu.SemaphoreType.DMA((n,)), pltpu.SemaphoreType.DMA((n,))],
        compiler_params=pltpu.CompilerParams(collective_id=0, has_side_effects=True,
                                             vmem_limit_bytes=LIMIT),
        name="gather",
    )(lat, pos, w_send, w_recv, pw, bias, mask)


NODE_COPIES = 6


def node_kernel(agg_own, agg_nb, cnt_own, cnt_nb, lat, cot, w_edge_out, w_node_self, w_node_msg,
                node_bias, w_node_out, gain, w_recv, new_lat, dagg, part, grads, agg_in, cnt_in,
                send_sem, recv_sem):
    me = Place()
    nxt, prv = me.slab(1), me.slab(-1)
    meet([nxt, prv])
    cs = Copies(send_sem, recv_sem)
    a_prv = cs.start(agg_nb.at[0], agg_in.at[0], prv)
    a_nxt = cs.start(agg_nb.at[1], agg_in.at[1], nxt)
    latent = lat[...]
    self_pre = dot(latent, w_node_self[...]) + node_bias[...]
    a_prv.wait_recv()
    a_nxt.wait_recv()
    c_prv = cs.start(cnt_nb.at[0], cnt_in.at[0], prv)
    c_nxt = cs.start(cnt_nb.at[1], cnt_in.at[1], nxt)
    aggregate = agg_own[...] + agg_in[0].astype(F32) + agg_in[1].astype(F32)
    aggregate_b = aggregate.astype(BF16)
    message = dot(aggregate_b, w_edge_out[...]).astype(BF16)
    hidden_pre = self_pre + dot(message, w_node_msg[...])
    logistic = jax.nn.sigmoid(hidden_pre)
    hidden = (hidden_pre * logistic).astype(BF16)
    update = dot(hidden, w_node_out[...])
    average = jnp.mean(update, axis=-1, keepdims=True)
    centred = update - average
    variance = jnp.mean(centred * centred, axis=-1, keepdims=True)
    inv_std = lax.rsqrt(variance + 1e-05)
    normed = centred * inv_std
    new_lat[...] = (latent.astype(F32) + normed * gain[...]).astype(BF16)
    c = cot[...].astype(F32)
    d_normed = c * gain[...]
    d_update = (inv_std * (d_normed - jnp.mean(d_normed, axis=-1, keepdims=True)
                           - normed * jnp.mean(d_normed * normed, axis=-1, keepdims=True))
                ).astype(BF16)
    d_hidden = dot_t(d_update, w_node_out[...])
    d_hidden_pre = (d_hidden * logistic * (1.0 + hidden_pre * (1.0 - logistic))).astype(BF16)
    d_message = dot_t(d_hidden_pre, w_node_msg[...]).astype(BF16)
    d_aggregate = dot_t(d_message, w_edge_out[...])
    dagg[1] = d_aggregate.astype(BF16)
    d_nxt = cs.start(dagg.at[1], dagg.at[0], nxt)
    d_prv = cs.start(dagg.at[1], dagg.at[2], prv)
    grads[1] = contract(aggregate_b, d_message)
    grads[2] = contract(latent, d_hidden_pre)
    grads[3] = contract(message, d_hidden_pre)
    grads[4] = contract(hidden, d_update)
    direct = c + dot_t(d_hidden_pre, w_node_self[...])
    c_prv.wait_recv()
    c_nxt.wait_recv()
    count = cnt_own[...] + cnt_in[0].astype(F32) + cnt_in[1].astype(F32)
    d_recv = (count * d_aggregate).astype(BF16)
    grads[0] = contract(latent, d_recv)
    part[...] = direct + dot_t(d_recv, w_recv[...])
    d_nxt.wait_recv()
    d_prv.wait_recv()
    cs.sent()


def node(agg_own, agg_nb, cnt_own, cnt_nb, lat, cot, *weights):
    own = lat.shape[0]
    n = NODE_COPIES
    return pl.pallas_call(
        node_kernel,
        out_shape=[sd((own, 128), BF16), sd((3, own, 128), BF16), sd((own, 128), F32),
                   sd((5, 128, 128), F32)],
        in_specs=[VM] * 13,
        out_specs=[VM] * 4,
        scratch_shapes=[pltpu.VMEM((2, own, 128), BF16), pltpu.VMEM((2, own, 128), BF16),
                        pltpu.SemaphoreType.DMA((n,)), pltpu.SemaphoreType.DMA((n,))],
        compiler_params=pltpu.CompilerParams(collective_id=1, has_side_effects=True),
        name="node",
    )(agg_own, agg_nb, cnt_own, cnt_nb, lat, cot, *weights)


FINAL_COPIES = 43


def final_kernel(dsend, gsend, grads, part, w_send, latent_grad, weight_grads, v, in_core, vx, in_x,
                 vy, in_y, in_z, out_y, out_x, out_core, rs_core, cs_sum, in_ra, in_rb, in_da, in_db,
                 in_fa, in_fb, fwd_a, fwd_b, vz, send_sem, recv_sem):
    me = Place()
    own = part.shape[0]
    up, dn, sib = me.member(1), me.member(-1), me.partner()
    core, zh = me.core, me.zh
    mats = [gsend[...]] + [grads[i] for i in range(5)]
    zero = jnp.zeros((128, 128), BF16)
    for i in range(8):
        v[i // 4, i % 4] = mats[i].astype(BF16) if i < 6 else zero
    xs = [me.at(x=(me.x + d) % NX) for d in range(1, NX)]
    ys = [me.at(y=(me.y + d) % NY) for d in range(1, NY)]
    zs = [me.at(z=(me.z + d) % NZ) for d in range(1, NZ)]
    meet([sib] + xs + ys + zs)
    cs = Copies(send_sem, recv_sem)
    ha, hb = pl.ds(0, own // 2), pl.ds(own // 2, own // 2)

    ar_core = cs.start(v.at[1 - core], in_core, sib)
    order = [2, 1, 3, 0]
    rs = [cs.start(dsend.at[((zh + o) % ZHI) * 2 + 1 - core], rs_core.at[(zh + o) % ZHI], sib)
          for o in order]
    ar_core.wait_recv()
    vx[...] = (v[core].astype(F32) + in_core[...].astype(F32)).astype(BF16)
    ar_x = [cs.start(vx.at[(me.x + d) % NX], in_x.at[d - 1], xs[d - 1]) for d in range(1, NX)]

    def chip_sum(i):
        rs[i].wait_recv()
        k = (zh + order[i]) % ZHI
        cs_sum[k] = (dsend[k * 2 + core].astype(F32) + rs_core[k].astype(F32)).astype(BF16)
        return k

    far = chip_sum(0)
    ra = cs.start(cs_sum.at[far, ha], in_ra, up)
    rb = cs.start(cs_sum.at[far, hb], in_rb, dn)
    ku = chip_sum(1)
    db = cs.start(cs_sum.at[ku, hb], in_db, up)
    kd = chip_sum(2)
    da = cs.start(cs_sum.at[kd, ha], in_da, dn)
    chip_sum(3)

    for copy in ar_x:
        copy.wait_recv()
    total = vx[me.x].astype(F32)
    for d in range(NX - 1):
        total = total + in_x[d].astype(F32)
    vy[...] = total.astype(BF16).reshape(NY, 16, 128)
    ar_y = [cs.start(vy.at[(me.y + d) % NY], in_y.at[d - 1], ys[d - 1]) for d in range(1, NY)]

    for copy in ar_y:
        copy.wait_recv()
    total = vy[me.y].astype(F32)
    for d in range(NY - 1):
        total = total + in_y[d].astype(F32)
    vz[...] = total.astype(BF16)
    in_z[me.z] = total.astype(BF16)
    ar_z = [cs.start(vz, in_z.at[me.z], zs[d - 1]) for d in range(1, NZ)]

    ra.wait_recv()
    fwd_a[...] = (in_ra[...].astype(F32) + cs_sum[ku, ha].astype(F32)).astype(BF16)
    fa = cs.start(fwd_a, in_fa, up)
    rb.wait_recv()
    fwd_b[...] = (in_rb[...].astype(F32) + cs_sum[kd, hb].astype(F32)).astype(BF16)
    fb = cs.start(fwd_b, in_fb, dn)

    for copy in ar_z:
        copy.wait_recv()
    total = in_z[0].astype(F32)
    for d in range(1, NZ):
        total = total + in_z[d].astype(F32)
    mine = pl.ds(pl.multiple_of(me.y * 16, 16), 16)
    out_y[mine] = total.astype(BF16)
    ag_y = [cs.start(out_y.at[mine], out_y.at[mine], ys[d - 1]) for d in range(1, NY)]

    da.wait_recv()
    db.wait_recv()
    fa.wait_recv()
    d_a = cs_sum[zh, ha].astype(F32) + in_da[...].astype(F32) + in_fa[...].astype(F32)
    latent_grad[ha] = part[ha] + dot_t(d_a.astype(BF16), w_send[...])
    fb.wait_recv()
    d_b = cs_sum[zh, hb].astype(F32) + in_db[...].astype(F32) + in_fb[...].astype(F32)
    latent_grad[hb] = part[hb] + dot_t(d_b.astype(BF16), w_send[...])

    for copy in ag_y:
        copy.wait_recv()
    out_x[me.x] = out_y[...]
    ag_x = [cs.start(out_y, out_x.at[me.x], xs[d - 1]) for d in range(1, NX)]
    for copy in ag_x:
        copy.wait_recv()
    out_core[core] = out_x[...]
    ag_core = cs.start(out_x, out_core.at[core], sib)
    ag_core.wait_recv()
    for i in range(6):
        weight_grads[i] = out_core[i // 4, i % 4].astype(F32)
    cs.sent()


def final(dsend, gsend, grads, part, w_send):
    own = part.shape[0]
    n = FINAL_COPIES
    b = lambda *shape: pltpu.VMEM(shape, BF16)
    h = own // 2
    return pl.pallas_call(
        final_kernel,
        out_shape=[sd((own, 128), F32), sd((6, 128, 128), F32)],
        in_specs=[VM] * 5,
        out_specs=[VM] * 2,
        scratch_shapes=[
            b(2, NX, 128, 128), b(NX, 128, 128), b(NX, 128, 128), b(NX - 1, 128, 128),
            b(NY, 16, 128), b(NY - 1, 16, 128), b(NZ, 16, 128), b(128, 128),
            b(NX, 128, 128), b(2, NX, 128, 128), b(ZHI, own, 128), b(ZHI, own, 128),
            b(h, 128), b(h, 128), b(h, 128), b(h, 128), b(h, 128), b(h, 128), b(h, 128), b(h, 128),
            b(16, 128),
            pltpu.SemaphoreType.DMA((n,)), pltpu.SemaphoreType.DMA((n,))],
        compiler_params=pltpu.CompilerParams(collective_id=2, has_side_effects=True),
        name="final",
    )(dsend, gsend, grads, part, w_send)


def body(latent, positions, tile_send, tile_recv, tile_mask, tile_count, w_send, w_recv, pos_weight,
         edge_bias, w_edge_out, w_node_self, w_node_msg, node_bias, w_node_out, gain, cotangent):
    ts, tr, tc = tile_send[0, 0], tile_recv[0, 0], tile_count[0]
    lat_all, s_rows, r_rows, rank_r, rank_t, most = gather(
        latent, positions, w_send, w_recv, pos_weight, edge_bias[None], tile_mask[0, 0])
    s_rows = s_rows.reshape(32, 128, 128)
    r_rows = r_rows.reshape(12, 128, 128)
    agg_own, agg_nb, cnt_own, cnt_nb = forward(ts, tr, tc, most, s_rows, r_rows, rank_r)
    new_latent, dagg, part, grads = node(
        agg_own, agg_nb, cnt_own, cnt_nb, latent, cotangent, w_edge_out, w_node_self, w_node_msg,
        node_bias[None], w_node_out, gain[None], w_recv)
    dsend, gsend = backward(ts, tr, tc, most, rank_t, s_rows, r_rows, dagg.reshape(12, 128, 128),
                            lat_all)
    latent_grad, weight_grads = final(dsend, gsend, grads, part, w_send)
    return new_latent, latent_grad, weight_grads


def solution(mesh):
    in_specs = (
        P(("blk", "grp"), None),
        P(None, ("blk", "grp")),
        P("blk", "grp", None),
        P("blk", "grp", None),
        P("blk", "grp", None, None, None),
        P("blk", "grp"),
        P(),
        P(),
        P(),
        P(),
        P(),
        P(),
        P(),
        P(),
        P(),
        P(),
        P(("blk", "grp"), None),
    )
    out_specs = (P(("blk", "grp"), None), P(("blk", "grp"), None), P())
    return jax.shard_map(body, mesh=mesh, in_specs=in_specs, out_specs=out_specs, check_vma=False)
```

```python
import functools

import jax
import jax.numpy as jnp
from jax import lax
from jax.experimental import pallas as pl
from jax.experimental.pallas import tpu as pltpu
from jax.sharding import PartitionSpec as P

F32, BF16 = jnp.float32, jnp.bfloat16
DN0 = (((0,), (0,)), ((), ()))
DN1 = (((1,), (1,)), ((), ()))
MESH = pl.DeviceIdType.MESH
SMEM = pl.BlockSpec(memory_space=pltpu.SMEM)
VM = pl.BlockSpec(memory_space=pltpu.VMEM)
NX, NY, NZ, ZLO, ZHI = 4, 8, 12, 3, 4
SLABS = NX * NY * ZLO
LIMIT = 16 << 20


class Place:
    def __init__(self):
        self.blk = lax.axis_index("blk")
        self.grp = lax.axis_index("grp")
        self.x = self.blk % NX
        self.y = (self.blk // NX) % NY
        self.zl = self.blk // (NX * NY)
        self.core = self.grp % 2
        self.zh = self.grp // 2
        self.z = self.zh * ZLO + self.zl

    def at(self, x=None, y=None, z=None, core=None):
        x = self.x if x is None else x
        y = self.y if y is None else y
        z = self.z if z is None else z
        core = self.core if core is None else core
        return ((z % ZLO) * (NX * NY) + y * NX + x, (z // ZLO) * 2 + core)

    def slab(self, step):
        return ((self.blk + step + SLABS) % SLABS, self.grp)

    def member(self, step):
        return (self.blk, ((self.zh + step + ZHI) % ZHI) * 2 + self.core)

    def partner(self):
        return (self.blk, self.zh * 2 + 1 - self.core)


def meet(peers):
    barrier = pltpu.get_barrier_semaphore()
    for peer in peers:
        pl.semaphore_signal(barrier, inc=1, device_id=peer, device_id_type=MESH)
    pl.semaphore_wait(barrier, len(peers))


class Copies:
    def __init__(self, send_sem, recv_sem):
        self.send_sem, self.recv_sem, self.started = send_sem, recv_sem, []

    def start(self, src, dst, device):
        number = len(self.started)
        copy = pltpu.make_async_remote_copy(
            src_ref=src, dst_ref=dst, send_sem=self.send_sem.at[number],
            recv_sem=self.recv_sem.at[number], device_id=device, device_id_type=MESH)
        copy.start()
        self.started.append(copy)
        return copy

    def sent(self):
        for copy in self.started:
            copy.wait_send()


def sd(shape, dtype):
    return jax.ShapeDtypeStruct(shape, dtype)


def dot(a, b):
    return jnp.dot(a, b, preferred_element_type=F32)


def dot_t(a, b):
    return lax.dot_general(a, b, DN1, preferred_element_type=F32)


def contract(a, b):
    return lax.dot_general(a, b, DN0, preferred_element_type=F32)


def placed_of(pos, pw):
    return lax.dot_general(pos, pw, DN0, precision=lax.Precision.HIGHEST,
                           preferred_element_type=F32)


def rank_tiles(mask, rank_r, rank_t, top):
    tiles = mask.shape[0]
    row = lax.broadcasted_iota(jnp.int32, (128, 128), 0)
    col = lax.broadcasted_iota(jnp.int32, (128, 128), 1)
    upper = jnp.where(row < col, 1.0, 0.0).astype(BF16)

    def ranks(values):
        return jnp.where(values > 0.0, dot(values.astype(BF16), upper), -1.0)

    def tile(t, _):
        values = mask[t].astype(F32)
        by_row = ranks(values)
        rank_r[t] = by_row.astype(BF16)
        top[pl.ds(t, 1), :] = jnp.max(by_row, axis=0, keepdims=True)
        by_col = ranks(values.T)
        rank_t[t] = by_col.astype(BF16)
        top[pl.ds(t + tiles, 1), :] = jnp.max(by_col, axis=0, keepdims=True)
        return 0

    lax.fori_loop(0, tiles, tile, 0)


def slot_counts(top):
    most = jnp.max(top[...], axis=1, keepdims=True) + 1.0
    return jnp.broadcast_to(most, top.shape).astype(jnp.int32)


def picks(ranks, slot):
    one, none = jnp.ones((), BF16), jnp.zeros((), BF16)
    if isinstance(slot, int):
        slot = jnp.full((), slot, BF16)
    else:
        slot = slot.astype(F32).astype(BF16)
    return jnp.where(ranks == slot, one, none)


def forward_kernel(first, more, ts, tr, tc, most, s_rows, r_rows, rank_r, agg_own, agg_nb, cnt_own,
                   cnt_nb, agg, cnt):
    agg[...] = jnp.zeros_like(agg)
    cnt[...] = jnp.zeros_like(cnt)
    ones = jnp.ones((128, 128), BF16)

    def tile(t, _):
        rb = tr[t]
        s = s_rows[ts[t]]
        rk = rank_r[t]
        floor = -(r_rows[rb].astype(F32))

        def add(slot, a, c):
            x = dot(picks(rk, slot), s)
            return a + jnp.maximum(x, floor), c + jnp.where(x > floor, 1.0, 0.0)

        a = jnp.zeros((128, 128), F32)
        c = jnp.zeros((128, 128), F32)
        for slot in range(first):
            a, c = add(slot, a, c)
        n = (jnp.maximum(most[t, 0] - first, 0) + more - 1) // more

        def rest(i, carry):
            a, c = carry
            for q in range(more):
                a, c = add(first + i * more + q, a, c)
            return a, c

        a, c = lax.fori_loop(0, n, rest, (a, c))
        degree = dot(jnp.where(rk >= jnp.zeros((), BF16), jnp.ones((), BF16), jnp.zeros((), BF16)), ones)
        spare = (first + n * more).astype(F32) - degree
        agg[rb] += a - degree * floor - spare * jnp.maximum(floor, 0.0)
        cnt[rb] += c - spare * jnp.where(floor < 0.0, 1.0, 0.0)
        return 0

    lax.fori_loop(0, tc[0], tile, 0)
    for b in range(4):
        sl = pl.ds(b * 128, 128)
        agg_own[sl] = agg[4 + b]
        cnt_own[sl] = cnt[4 + b]
        agg_nb[0, sl] = agg[b].astype(BF16)
        agg_nb[1, sl] = agg[8 + b].astype(BF16)
        cnt_nb[0, sl] = cnt[b].astype(BF16)
        cnt_nb[1, sl] = cnt[8 + b].astype(BF16)


def forward(ts, tr, tc, most, s_rows, r_rows, rank_r, first=18, more=4):
    own = 512
    return pl.pallas_call(
        functools.partial(forward_kernel, first, more),
        out_shape=[sd((own, 128), F32), sd((2, own, 128), BF16), sd((own, 128), F32),
                   sd((2, own, 128), BF16)],
        in_specs=[SMEM] * 4 + [VM] * 3,
        out_specs=[VM] * 4,
        scratch_shapes=[pltpu.VMEM((12, 128, 128), F32), pltpu.VMEM((12, 128, 128), F32)],
        compiler_params=pltpu.CompilerParams(vmem_limit_bytes=LIMIT),
        name="forward",
    )(ts, tr, tc, most, s_rows, r_rows, rank_r)


def backward_kernel(first, more, ts, tr, tc, most, rank_t, s_rows, r_rows, dagg, lat_all, new_in,
                    dsend, gsend, new_out, acc):
    new_out[...] = new_in[...]
    acc[...] = jnp.zeros_like(acc)
    tiles = rank_t.shape[0]

    def tile(t, _):
        sb = ts[t]
        rb = tr[t]
        floor = -(s_rows[sb].astype(F32))
        rhs = jnp.concatenate([r_rows[rb], dagg[rb]], axis=1)
        rk = rank_t[t]

        def add(slot, a):
            x = dot(picks(rk, slot), rhs)
            return a + jnp.where(x[:, :128] > floor, x[:, 128:], 0.0)

        a = jnp.zeros((128, 128), F32)
        for slot in range(first):
            a = add(slot, a)
        n = (jnp.maximum(most[t + tiles, 0] - first, 0) + more - 1) // more

        def rest(i, a):
            for q in range(more):
                a = add(first + i * more + q, a)
            return a

        acc[sb] += lax.fori_loop(0, n, rest, a)
        return 0

    lax.fori_loop(0, tc[0], tile, 0)
    g = jnp.zeros((128, 128), F32)
    for b in range(8):
        d = acc[pl.ds(4 * b, 4)].reshape(512, 128).astype(BF16)
        dsend[b] = d
        g = g + contract(lat_all[b], d)
    gsend[...] = g


def backward(ts, tr, tc, most, rank_t, s_rows, r_rows, dagg, lat_all, new_lat, first=18, more=4):
    return pl.pallas_call(
        functools.partial(backward_kernel, first, more),
        out_shape=[sd((8, 512, 128), BF16), sd((128, 128), F32), sd((512, 128), BF16)],
        in_specs=[SMEM] * 4 + [VM] * 6,
        out_specs=[VM] * 3,
        scratch_shapes=[pltpu.VMEM((32, 128, 128), F32)],
        compiler_params=pltpu.CompilerParams(vmem_limit_bytes=LIMIT),
        name="backward",
    )(ts, tr, tc, most, rank_t, s_rows, r_rows, dagg, lat_all, new_lat)


GATHER_COPIES = 24


def gather_kernel(lat, pos, w_send, w_recv, pw, bias, mask_in, lat_all, s_rows, r_rows, rank_r,
                  rank_t, most, mask, top, pos_all, lat_nb, pos_nb, mask_sem, send_sem, recv_sem):
    load = pltpu.make_async_copy(mask_in, mask, mask_sem)
    load.start()
    me = Place()
    own = lat.shape[0]
    g = me.grp
    up, dn, sib = me.member(1), me.member(-1), me.partner()
    nxt, prv = me.slab(1), me.slab(-1)
    meet([up, dn, sib, nxt, prv])
    cs = Copies(send_sem, recv_sem)
    halves = (pl.ds(0, own // 2), pl.ds(own // 2, own // 2))

    def half(index, h):
        return lat_all.at[index, halves[h]]

    up_pos = cs.start(pos, pos_all.at[g], up)
    dn_pos = cs.start(pos, pos_all.at[g], dn)
    up_a = cs.start(lat.at[halves[0]], half(g, 0), up)
    dn_b = cs.start(lat.at[halves[1]], half(g, 1), dn)
    up_b = cs.start(lat.at[halves[1]], half(g, 1), up)
    dn_a = cs.start(lat.at[halves[0]], half(g, 0), dn)
    beside = [
        cs.start(lat, lat_nb.at[0], nxt),
        cs.start(lat, lat_nb.at[1], prv),
        cs.start(pos, pos_nb.at[0], nxt),
        cs.start(pos, pos_nb.at[1], prv),
    ]
    partner = [
        cs.start(lat, lat_all.at[g], sib),
        cs.start(pos, pos_all.at[g], sib),
    ]
    lat_all[g] = lat[...]
    pos_all[g] = pos[...]
    iu, idn, far = up[1], dn[1], me.member(2)[1]

    def pass_on(ref):
        return cs.start(ref, ref, sib)

    def send_rows(index):
        s_rows[index] = (dot(lat_all[index], w_send[...])
                         + placed_of(pos_all[index], pw[...])).astype(BF16)

    def recv_rows(slab, rows, places):
        r_rows[slab] = (dot(rows, w_recv[...]) - placed_of(places, pw[...])
                        + bias[...]).astype(BF16)

    def other(index):
        return (index // 2) * 2 + 1 - me.core

    recv_rows(1, lat[...], pos[...])
    send_rows(g)
    load.wait()
    rank_tiles(mask, rank_r, rank_t, top)
    most[...] = slot_counts(top)

    up_pos.wait_recv()
    far_pos = cs.start(pos_all.at[idn], pos_all.at[idn], up)
    near = [pass_on(pos_all.at[idn])]
    dn_pos.wait_recv()
    near.append(pass_on(pos_all.at[iu]))
    up_a.wait_recv()
    far_a = cs.start(half(idn, 0), half(idn, 0), up)
    near.append(pass_on(half(idn, 0)))
    dn_b.wait_recv()
    far_b = cs.start(half(iu, 1), half(iu, 1), dn)
    near.append(pass_on(half(iu, 1)))
    for copy in beside + partner:
        copy.wait_recv()
    recv_rows(0, lat_nb[0], pos_nb[0])
    recv_rows(2, lat_nb[1], pos_nb[1])
    send_rows(sib[1])
    up_b.wait_recv()
    near.append(pass_on(half(idn, 1)))
    send_rows(idn)
    dn_a.wait_recv()
    near.append(pass_on(half(iu, 0)))
    send_rows(iu)
    far_pos.wait_recv()
    last = [pass_on(pos_all.at[far])]
    for copy in near:
        copy.wait_recv()
    send_rows(other(idn))
    send_rows(other(iu))
    far_a.wait_recv()
    last.append(pass_on(half(far, 0)))
    far_b.wait_recv()
    last.append(pass_on(half(far, 1)))
    send_rows(far)
    for copy in last:
        copy.wait_recv()
    send_rows(other(far))
    cs.sent()


def gather(lat, pos, w_send, w_recv, pw, bias, mask):
    own = lat.shape[0]
    n = GATHER_COPIES
    tiles = mask.shape[0]
    ranks = sd((tiles, 128, 128), BF16)
    return pl.pallas_call(
        gather_kernel,
        out_shape=[sd((8, own, 128), BF16), sd((8, own, 128), BF16), sd((3, own, 128), BF16),
                   ranks, ranks, sd((2 * tiles, 128), jnp.int32)],
        in_specs=[VM] * 6 + [pl.BlockSpec(memory_space=pltpu.HBM)],
        out_specs=[VM] * 6,
        scratch_shapes=[pltpu.VMEM((tiles, 128, 128), jnp.int32), pltpu.VMEM((2 * tiles, 128), F32),
                        pltpu.VMEM((8, 3, own), F32), pltpu.VMEM((2, own, 128), BF16),
                        pltpu.VMEM((2, 3, own), F32), pltpu.SemaphoreType.DMA(()),
                        pltpu.SemaphoreType.DMA((n,)), pltpu.SemaphoreType.DMA((n,))],
        compiler_params=pltpu.CompilerParams(collective_id=0, has_side_effects=True,
                                             vmem_limit_bytes=LIMIT),
        name="gather",
    )(lat, pos, w_send, w_recv, pw, bias, mask)


PIECES = 1
NODE_COPIES = 4 * PIECES + 2


def node_kernel(agg_own, agg_nb, cnt_own, cnt_nb, lat, cot, w_edge_out, w_node_self, w_node_msg,
                node_bias, w_node_out, gain, w_recv, new_lat, dagg, part, grads, agg_in, cnt_in,
                d_agg, direct, agg_b, message_b, hidden_b, d_update_b, d_pre_b, d_message_b, send_sem,
                recv_sem):
    me = Place()
    nxt, prv = me.slab(1), me.slab(-1)
    meet([nxt, prv])
    cs = Copies(send_sem, recv_sem)
    size = lat.shape[0] // PIECES
    pieces = [pl.ds(p * size, size) for p in range(PIECES)]
    arrive = []
    for p in pieces:
        arrive.append((cs.start(agg_nb.at[0, p], agg_in.at[0, p], prv),
                       cs.start(agg_nb.at[1, p], agg_in.at[1, p], nxt)))
    counts, leave = [], []
    for i, p in enumerate(pieces):
        latent = lat[p]
        self_pre = dot(latent, w_node_self[...]) + node_bias[...]
        c = cot[p].astype(F32)
        d_normed = c * gain[...]
        d_centre = d_normed - jnp.mean(d_normed, axis=-1, keepdims=True)
        for copy in arrive[i]:
            copy.wait_recv()
        if i == PIECES - 1:
            counts = [cs.start(cnt_nb.at[0], cnt_in.at[0], prv),
                      cs.start(cnt_nb.at[1], cnt_in.at[1], nxt)]
        aggregate = agg_own[p] + agg_in[0, p].astype(F32) + agg_in[1, p].astype(F32)
        aggregate_b = aggregate.astype(BF16)
        message = dot(aggregate_b, w_edge_out[...]).astype(BF16)
        hidden_pre = self_pre + dot(message, w_node_msg[...])
        logistic = jax.nn.sigmoid(hidden_pre)
        hidden = (hidden_pre * logistic).astype(BF16)
        update = dot(hidden, w_node_out[...])
        average = jnp.mean(update, axis=-1, keepdims=True)
        centred = update - average
        variance = jnp.mean(centred * centred, axis=-1, keepdims=True)
        inv_std = lax.rsqrt(variance + 1e-05)
        normed = centred * inv_std
        d_update = (inv_std * (d_centre - normed * jnp.mean(d_normed * normed, axis=-1, keepdims=True))
                    ).astype(BF16)
        d_hidden = dot_t(d_update, w_node_out[...])
        d_hidden_pre = (d_hidden * logistic * (1.0 + hidden_pre * (1.0 - logistic))).astype(BF16)
        d_message = dot_t(d_hidden_pre, w_node_msg[...]).astype(BF16)
        d_aggregate = dot_t(d_message, w_edge_out[...])
        dagg[1, p] = d_aggregate.astype(BF16)
        leave.append(cs.start(dagg.at[1, p], dagg.at[0, p], nxt))
        leave.append(cs.start(dagg.at[1, p], dagg.at[2, p], prv))
        new_lat[p] = (latent.astype(F32) + normed * gain[...]).astype(BF16)
        d_agg[p] = d_aggregate
        agg_b[p] = aggregate_b
        message_b[p] = message
        hidden_b[p] = hidden
        d_update_b[p] = d_update
        d_pre_b[p] = d_hidden_pre
        d_message_b[p] = d_message
        direct[p] = c
    latent = lat[...]
    d_hidden_pre = d_pre_b[...]
    grads[1] = contract(agg_b[...], d_message_b[...])
    grads[2] = contract(latent, d_hidden_pre)
    grads[3] = contract(message_b[...], d_hidden_pre)
    grads[4] = contract(hidden_b[...], d_update_b[...])
    base = direct[...] + dot_t(d_hidden_pre, w_node_self[...])
    for copy in counts:
        copy.wait_recv()
    count = cnt_own[...] + cnt_in[0].astype(F32) + cnt_in[1].astype(F32)
    d_recv = (count * d_agg[...]).astype(BF16)
    grads[0] = contract(latent, d_recv)
    part[...] = base + dot_t(d_recv, w_recv[...])
    for copy in leave:
        copy.wait_recv()
    cs.sent()


def node(agg_own, agg_nb, cnt_own, cnt_nb, lat, cot, *weights):
    own = lat.shape[0]
    n = NODE_COPIES
    rows = pltpu.VMEM((own, 128), BF16)
    return pl.pallas_call(
        node_kernel,
        out_shape=[sd((own, 128), BF16), sd((3, own, 128), BF16), sd((own, 128), F32),
                   sd((5, 128, 128), F32)],
        in_specs=[VM] * 13,
        out_specs=[VM] * 4,
        scratch_shapes=[pltpu.VMEM((2, own, 128), BF16), pltpu.VMEM((2, own, 128), BF16),
                        pltpu.VMEM((own, 128), F32), pltpu.VMEM((own, 128), F32),
                        rows, rows, rows, rows, rows, rows,
                        pltpu.SemaphoreType.DMA((n,)), pltpu.SemaphoreType.DMA((n,))],
        compiler_params=pltpu.CompilerParams(collective_id=1, has_side_effects=True,
                                             vmem_limit_bytes=LIMIT),
        name="node",
    )(agg_own, agg_nb, cnt_own, cnt_nb, lat, cot, *weights)


FINAL_COPIES = 49


def final_kernel(dsend, gsend, grads, part, w_send, latent_grad, weight_grads, v, in_xc, vy, in_y,
                 vz, in_z, out_y, out, rs_core, cs_sum, in_ra, in_rb, in_da, in_db, in_fa, in_fb,
                 fwd_a, fwd_b, ready_y, ready_z, send_sem, recv_sem):
    me = Place()
    own = part.shape[0]
    up, dn, sib = me.member(1), me.member(-1), me.partner()
    core, zh = me.core, me.zh
    v[pl.ds(0, 128)] = gsend[...].astype(BF16)
    for i in range(5):
        v[pl.ds(128 * (i + 1), 128)] = grads[i].astype(BF16)
    vy[...] = jnp.zeros_like(vy)

    def chunk(c, x):
        return pl.ds(pl.multiple_of((c * NX + x) * 96, 16), 96)

    def y_peer(d):
        return me.at(y=(me.y + d + NY) % NY)

    def z_peer(d):
        return me.at(z=(me.z + d + NZ) % NZ)

    plane = [(dx, dc) for dx in range(NX) for dc in range(2) if dx or dc]
    spots = [((core + dc) % 2, (me.x + dx) % NX) for dx, dc in plane]
    peers = [me.at(x=x, core=c) for c, x in spots]
    meet(peers + [y_peer(d) for d in (1, 2, -1, -2)] + [z_peer(d) for d in (1, 2, 3, -1, -2, -3)])
    for d in (2, -2):
        pl.semaphore_signal(ready_y, inc=1, device_id=y_peer(d), device_id_type=MESH)
    for d in (3, -3):
        pl.semaphore_signal(ready_z, inc=1, device_id=z_peer(d), device_id_type=MESH)
    cs = Copies(send_sem, recv_sem)
    ha, hb = pl.ds(0, own // 2), pl.ds(own // 2, own // 2)

    ar_xc = [cs.start(v.at[chunk(*spots[j])], in_xc.at[j], peers[j]) for j in range(len(peers))]
    order = [2, 1, 3, 0]
    rs = [cs.start(dsend.at[((zh + o) % ZHI) * 2 + 1 - core], rs_core.at[(zh + o) % ZHI], sib)
          for o in order]

    def chip_sum(i):
        rs[i].wait_recv()
        k = (zh + order[i]) % ZHI
        cs_sum[k] = (dsend[k * 2 + core].astype(F32) + rs_core[k].astype(F32)).astype(BF16)
        return k

    far = chip_sum(0)
    ra = cs.start(cs_sum.at[far, ha], in_ra, up)
    rb = cs.start(cs_sum.at[far, hb], in_rb, dn)
    ku = chip_sum(1)
    db = cs.start(cs_sum.at[ku, hb], in_db, up)
    kd = chip_sum(2)
    da = cs.start(cs_sum.at[kd, ha], in_da, dn)

    for copy in ar_xc:
        copy.wait_recv()
    total = v[chunk(core, me.x)].astype(F32)
    for j in range(len(peers)):
        total = total + in_xc[j].astype(F32)
    for q in range(NY):
        vy[q, pl.ds(0, 12)] = total[12 * q:12 * q + 12].astype(BF16)
    pl.semaphore_wait(ready_y, 2)
    ar_y = [cs.start(vy.at[(me.y + d) % NY], in_y.at[d - 1], y_peer(d)) for d in range(1, NY)]
    chip_sum(3)

    for copy in ar_y:
        copy.wait_recv()
    total = vy[me.y].astype(F32)
    for d in range(NY - 1):
        total = total + in_y[d].astype(F32)
    vz[...] = total.astype(BF16)
    in_z[me.z] = total.astype(BF16)
    pl.semaphore_wait(ready_z, 2)
    ar_z = [cs.start(vz, in_z.at[me.z], z_peer(d)) for d in range(1, NZ)]

    ra.wait_recv()
    fwd_a[...] = (in_ra[...].astype(F32) + cs_sum[ku, ha].astype(F32)).astype(BF16)
    fa = cs.start(fwd_a, in_fa, up)
    rb.wait_recv()
    fwd_b[...] = (in_rb[...].astype(F32) + cs_sum[kd, hb].astype(F32)).astype(BF16)
    fb = cs.start(fwd_b, in_fb, dn)

    for copy in ar_z:
        copy.wait_recv()
    total = in_z[0].astype(F32)
    for d in range(1, NZ):
        total = total + in_z[d].astype(F32)
    out_y[me.y] = total.astype(BF16)
    ag_y = [cs.start(out_y.at[me.y], out_y.at[me.y], y_peer(d)) for d in range(1, NY)]

    da.wait_recv()
    db.wait_recv()
    fa.wait_recv()
    d_a = cs_sum[zh, ha].astype(F32) + in_da[...].astype(F32) + in_fa[...].astype(F32)
    latent_grad[ha] = part[ha] + dot_t(d_a.astype(BF16), w_send[...])
    fb.wait_recv()
    d_b = cs_sum[zh, hb].astype(F32) + in_db[...].astype(F32) + in_fb[...].astype(F32)
    latent_grad[hb] = part[hb] + dot_t(d_b.astype(BF16), w_send[...])

    for copy in ag_y:
        copy.wait_recv()
    mine = chunk(core, me.x)
    out[mine] = jnp.concatenate([out_y[q].astype(F32)[:12] for q in range(NY)], 0).astype(BF16)
    ag_xc = [cs.start(out.at[mine], out.at[mine], peer) for peer in peers]
    for copy in ag_xc:
        copy.wait_recv()
    for i in range(6):
        weight_grads[i] = out[pl.ds(128 * i, 128)].astype(F32)
    cs.sent()


def final(dsend, gsend, grads, part, w_send):
    own = part.shape[0]
    n = FINAL_COPIES
    b = lambda *shape: pltpu.VMEM(shape, BF16)
    h = own // 2
    return pl.pallas_call(
        final_kernel,
        out_shape=[sd((own, 128), F32), sd((6, 128, 128), F32)],
        in_specs=[VM] * 5,
        out_specs=[VM] * 2,
        scratch_shapes=[
            b(768, 128), b(2 * NX - 1, 96, 128), b(NY, 16, 128), b(NY - 1, 16, 128), b(16, 128),
            b(NZ, 16, 128), b(NY, 16, 128), b(768, 128), b(ZHI, own, 128), b(ZHI, own, 128),
            b(h, 128), b(h, 128), b(h, 128), b(h, 128), b(h, 128), b(h, 128), b(h, 128), b(h, 128),
            pltpu.SemaphoreType.REGULAR, pltpu.SemaphoreType.REGULAR,
            pltpu.SemaphoreType.DMA((n,)), pltpu.SemaphoreType.DMA((n,))],
        compiler_params=pltpu.CompilerParams(collective_id=2, has_side_effects=True,
                                             vmem_limit_bytes=LIMIT),
        name="final",
    )(dsend, gsend, grads, part, w_send)


def body(latent, positions, tile_send, tile_recv, tile_mask, tile_count, w_send, w_recv, pos_weight,
         edge_bias, w_edge_out, w_node_self, w_node_msg, node_bias, w_node_out, gain, cotangent):
    ts, tr, tc = tile_send[0, 0], tile_recv[0, 0], tile_count[0]
    lat_all, s_rows, r_rows, rank_r, rank_t, most = gather(
        latent, positions, w_send, w_recv, pos_weight, edge_bias[None], tile_mask[0, 0])
    s_rows = s_rows.reshape(32, 128, 128)
    r_rows = r_rows.reshape(12, 128, 128)
    agg_own, agg_nb, cnt_own, cnt_nb = forward(ts, tr, tc, most, s_rows, r_rows, rank_r)
    new_latent, dagg, part, grads = node(
        agg_own, agg_nb, cnt_own, cnt_nb, latent, cotangent, w_edge_out, w_node_self, w_node_msg,
        node_bias[None], w_node_out, gain[None], w_recv)
    dsend, gsend, new_latent = backward(ts, tr, tc, most, rank_t, s_rows, r_rows, dagg.reshape(12, 128, 128),
                            lat_all, new_latent)
    latent_grad, weight_grads = final(dsend, gsend, grads, part, w_send)
    return new_latent, latent_grad, weight_grads


def solution(mesh):
    in_specs = (
        P(("blk", "grp"), None),
        P(None, ("blk", "grp")),
        P("blk", "grp", None),
        P("blk", "grp", None),
        P("blk", "grp", None, None, None),
        P("blk", "grp"),
        P(),
        P(),
        P(),
        P(),
        P(),
        P(),
        P(),
        P(),
        P(),
        P(),
        P(("blk", "grp"), None),
    )
    out_specs = (P(("blk", "grp"), None), P(("blk", "grp"), None), P())
    return jax.shard_map(body, mesh=mesh, in_specs=in_specs, out_specs=out_specs, check_vma=False)
```

```python
import functools

import jax
import jax.numpy as jnp
from jax import lax
from jax.experimental import pallas as pl
from jax.experimental.pallas import tpu as pltpu
from jax.sharding import PartitionSpec as P

F32, BF16 = jnp.float32, jnp.bfloat16
DN0 = (((0,), (0,)), ((), ()))
DN1 = (((1,), (1,)), ((), ()))
MESH = pl.DeviceIdType.MESH
SMEM = pl.BlockSpec(memory_space=pltpu.SMEM)
VM = pl.BlockSpec(memory_space=pltpu.VMEM)
HBM = pl.BlockSpec(memory_space=pltpu.HBM)
NX, NY, NZ, ZLO, ZHI = 4, 8, 12, 3, 4
SLABS = NX * NY * ZLO
LIMIT = 16 << 20


class Place:
    def __init__(self):
        self.blk = lax.axis_index("blk")
        self.grp = lax.axis_index("grp")
        self.x = self.blk % NX
        self.y = (self.blk // NX) % NY
        self.zl = self.blk // (NX * NY)
        self.core = self.grp % 2
        self.zh = self.grp // 2
        self.z = self.zh * ZLO + self.zl

    def at(self, x=None, y=None, z=None, core=None):
        x = self.x if x is None else x
        y = self.y if y is None else y
        z = self.z if z is None else z
        core = self.core if core is None else core
        return ((z % ZLO) * (NX * NY) + y * NX + x, (z // ZLO) * 2 + core)

    def slab(self, step):
        return ((self.blk + step + SLABS) % SLABS, self.grp)

    def member(self, step):
        return (self.blk, ((self.zh + step + ZHI) % ZHI) * 2 + self.core)

    def partner(self):
        return (self.blk, self.zh * 2 + 1 - self.core)


def meet(peers):
    barrier = pltpu.get_barrier_semaphore()
    for peer in peers:
        pl.semaphore_signal(barrier, inc=1, device_id=peer, device_id_type=MESH)
    pl.semaphore_wait(barrier, len(peers))


class Copies:
    def __init__(self, send_sem, recv_sem):
        self.send_sem, self.recv_sem, self.started = send_sem, recv_sem, []

    def start(self, src, dst, device):
        number = len(self.started)
        copy = pltpu.make_async_remote_copy(
            src_ref=src, dst_ref=dst, send_sem=self.send_sem.at[number],
            recv_sem=self.recv_sem.at[number], device_id=device, device_id_type=MESH)
        copy.start()
        self.started.append(copy)
        return copy

    def sent(self):
        for copy in self.started:
            copy.wait_send()


def fetch(pairs, sem):
    copies = [pltpu.make_async_copy(src, dst, sem.at[i]) for i, (src, dst) in enumerate(pairs)]
    for copy in copies:
        copy.start()
    return copies


def in_hbm(*arrays):
    return [pltpu.with_memory_space_constraint(a, pltpu.HBM) for a in arrays]


def sd(shape, dtype):
    return jax.ShapeDtypeStruct(shape, dtype)


def dot(a, b):
    return jnp.dot(a, b, preferred_element_type=F32)


def dot_t(a, b):
    return lax.dot_general(a, b, DN1, preferred_element_type=F32)


def contract(a, b):
    return lax.dot_general(a, b, DN0, preferred_element_type=F32)


def placed_of(pos, pw):
    return lax.dot_general(pos, pw, DN0, precision=lax.Precision.HIGHEST,
                           preferred_element_type=F32)


def rank_tiles(mask, rank_r, rank_t, top):
    tiles = mask.shape[0]
    row = lax.broadcasted_iota(jnp.int32, (128, 128), 0)
    col = lax.broadcasted_iota(jnp.int32, (128, 128), 1)
    upper = jnp.where(row < col, 1.0, 0.0).astype(BF16)

    def ranks(values):
        return jnp.where(values > 0.0, dot(values.astype(BF16), upper), -1.0)

    def tile(t, _):
        values = mask[t].astype(F32)
        by_row = ranks(values)
        rank_r[t] = by_row.astype(BF16)
        top[pl.ds(t, 1), :] = jnp.max(by_row, axis=0, keepdims=True)
        by_col = ranks(values.T)
        rank_t[t] = by_col.astype(BF16)
        top[pl.ds(t + tiles, 1), :] = jnp.max(by_col, axis=0, keepdims=True)
        return 0

    lax.fori_loop(0, tiles, tile, 0)


def slot_counts(top):
    most = jnp.max(top[...], axis=1, keepdims=True) + 1.0
    return jnp.broadcast_to(most, top.shape).astype(jnp.int32)


def picks(ranks, slot):
    one, none = jnp.ones((), BF16), jnp.zeros((), BF16)
    if isinstance(slot, int):
        slot = jnp.full((), slot, BF16)
    else:
        slot = slot.astype(F32).astype(BF16)
    return jnp.where(ranks == slot, one, none)


def forward_kernel(first, more, ts, tr, tc, most, s_rows, r_rows, rank_r, agg_own, agg_nb, cnt_own,
                   cnt_nb, agg, cnt):
    agg[...] = jnp.zeros_like(agg)
    cnt[...] = jnp.zeros_like(cnt)
    ones = jnp.ones((128, 128), BF16)

    def tile(t, _):
        rb = tr[t]
        s = s_rows[ts[t]]
        rk = rank_r[t]
        floor = -(r_rows[rb].astype(F32))

        def add(slot, a, c):
            x = dot(picks(rk, slot), s)
            return a + jnp.maximum(x, floor), c + jnp.where(x > floor, 1.0, 0.0)

        a = jnp.zeros((128, 128), F32)
        c = jnp.zeros((128, 128), F32)
        for slot in range(first):
            a, c = add(slot, a, c)
        n = (jnp.maximum(most[t, 0] - first, 0) + more - 1) // more

        def rest(i, carry):
            a, c = carry
            for q in range(more):
                a, c = add(first + i * more + q, a, c)
            return a, c

        a, c = lax.fori_loop(0, n, rest, (a, c))
        degree = dot(jnp.where(rk >= jnp.zeros((), BF16), jnp.ones((), BF16), jnp.zeros((), BF16)), ones)
        spare = (first + n * more).astype(F32) - degree
        agg[rb] += a - degree * floor - spare * jnp.maximum(floor, 0.0)
        cnt[rb] += c - spare * jnp.where(floor < 0.0, 1.0, 0.0)
        return 0

    lax.fori_loop(0, tc[0], tile, 0)
    for b in range(4):
        sl = pl.ds(b * 128, 128)
        agg_own[sl] = agg[4 + b]
        cnt_own[sl] = cnt[4 + b]
        agg_nb[0, sl] = agg[b].astype(BF16)
        agg_nb[1, sl] = agg[8 + b].astype(BF16)
        cnt_nb[0, sl] = cnt[b].astype(BF16)
        cnt_nb[1, sl] = cnt[8 + b].astype(BF16)


def forward(ts, tr, tc, most, s_rows, r_rows, rank_r, first=18, more=4):
    own = 512
    return pl.pallas_call(
        functools.partial(forward_kernel, first, more),
        out_shape=[sd((own, 128), F32), sd((2, own, 128), BF16), sd((own, 128), F32),
                   sd((2, own, 128), BF16)],
        in_specs=[SMEM] * 4 + [VM] * 3,
        out_specs=[VM] * 4,
        scratch_shapes=[pltpu.VMEM((12, 128, 128), F32), pltpu.VMEM((12, 128, 128), F32)],
        compiler_params=pltpu.CompilerParams(vmem_limit_bytes=LIMIT),
        name="forward",
    )(ts, tr, tc, most, s_rows, r_rows, rank_r)


def backward_kernel(first, more, ts, tr, tc, most, rank_t, s_rows, r_rows, dagg, lat_all, new_in,
                    dsend, gsend, new_out, acc):
    new_out[...] = new_in[...]
    acc[...] = jnp.zeros_like(acc)
    tiles = rank_t.shape[0]

    def tile(t, _):
        sb = ts[t]
        rb = tr[t]
        floor = -(s_rows[sb].astype(F32))
        rhs = jnp.concatenate([r_rows[rb], dagg[rb]], axis=1)
        rk = rank_t[t]

        def add(slot, a):
            x = dot(picks(rk, slot), rhs)
            return a + jnp.where(x[:, :128] > floor, x[:, 128:], 0.0)

        a = jnp.zeros((128, 128), F32)
        for slot in range(first):
            a = add(slot, a)
        n = (jnp.maximum(most[t + tiles, 0] - first, 0) + more - 1) // more

        def rest(i, a):
            for q in range(more):
                a = add(first + i * more + q, a)
            return a

        acc[sb] += lax.fori_loop(0, n, rest, a)
        return 0

    lax.fori_loop(0, tc[0], tile, 0)
    g = jnp.zeros((128, 128), F32)
    for b in range(8):
        d = acc[pl.ds(4 * b, 4)].reshape(512, 128).astype(BF16)
        dsend[b] = d
        g = g + contract(lat_all[b], d)
    gsend[...] = g


def backward(ts, tr, tc, most, rank_t, s_rows, r_rows, dagg, lat_all, new_lat, first=18, more=4):
    return pl.pallas_call(
        functools.partial(backward_kernel, first, more),
        out_shape=[sd((8, 512, 128), BF16), sd((128, 128), F32), sd((512, 128), BF16)],
        in_specs=[SMEM] * 4 + [VM] * 6,
        out_specs=[VM] * 3,
        scratch_shapes=[pltpu.VMEM((32, 128, 128), F32)],
        compiler_params=pltpu.CompilerParams(vmem_limit_bytes=LIMIT),
        name="backward",
    )(ts, tr, tc, most, rank_t, s_rows, r_rows, dagg, lat_all, new_lat)


GATHER_COPIES = 24


def gather_kernel(lat, pos, w_send_in, w_recv_in, pw_in, bias_in, mask_in, ts_in, tr_in, tc_in,
                  lat_all, s_rows, r_rows, rank_r, rank_t, most, ts, tr, tc, mask, top, pos_all,
                  lat_nb, pos_nb, w_send, w_recv, pw, bias, load_sem, send_sem, recv_sem):
    me = Place()
    own = lat.shape[0]
    g = me.grp
    loads = fetch([(lat, lat_all.at[g]), (pos, pos_all.at[g]), (w_send_in, w_send),
                   (w_recv_in, w_recv), (pw_in, pw), (bias_in, bias), (mask_in, mask), (ts_in, ts),
                   (tr_in, tr), (tc_in, tc)], load_sem)
    up, dn, sib = me.member(1), me.member(-1), me.partner()
    nxt, prv = me.slab(1), me.slab(-1)
    meet([up, dn, sib, nxt, prv])
    cs = Copies(send_sem, recv_sem)
    halves = (pl.ds(0, own // 2), pl.ds(own // 2, own // 2))

    def half(index, h):
        return lat_all.at[index, halves[h]]

    up_pos = cs.start(pos, pos_all.at[g], up)
    dn_pos = cs.start(pos, pos_all.at[g], dn)
    up_a = cs.start(lat.at[halves[0]], half(g, 0), up)
    dn_b = cs.start(lat.at[halves[1]], half(g, 1), dn)
    up_b = cs.start(lat.at[halves[1]], half(g, 1), up)
    dn_a = cs.start(lat.at[halves[0]], half(g, 0), dn)
    beside = [
        cs.start(lat, lat_nb.at[0], nxt),
        cs.start(lat, lat_nb.at[1], prv),
        cs.start(pos, pos_nb.at[0], nxt),
        cs.start(pos, pos_nb.at[1], prv),
    ]
    partner = [
        cs.start(lat, lat_all.at[g], sib),
        cs.start(pos, pos_all.at[g], sib),
    ]
    iu, idn, far = up[1], dn[1], me.member(2)[1]

    def pass_on(ref):
        return cs.start(ref, ref, sib)

    def send_rows(index):
        s_rows[index] = (dot(lat_all[index], w_send[...])
                         + placed_of(pos_all[index], pw[...])).astype(BF16)

    def recv_rows(slab, rows, places):
        r_rows[slab] = (dot(rows, w_recv[...]) - placed_of(places, pw[...])
                        + bias[...]).astype(BF16)

    def other(index):
        return (index // 2) * 2 + 1 - me.core

    for load in loads:
        load.wait()
    recv_rows(1, lat_all[g], pos_all[g])
    send_rows(g)
    rank_tiles(mask, rank_r, rank_t, top)
    most[...] = slot_counts(top)

    up_pos.wait_recv()
    far_pos = cs.start(pos_all.at[idn], pos_all.at[idn], up)
    near = [pass_on(pos_all.at[idn])]
    dn_pos.wait_recv()
    near.append(pass_on(pos_all.at[iu]))
    up_a.wait_recv()
    far_a = cs.start(half(idn, 0), half(idn, 0), up)
    near.append(pass_on(half(idn, 0)))
    dn_b.wait_recv()
    far_b = cs.start(half(iu, 1), half(iu, 1), dn)
    near.append(pass_on(half(iu, 1)))
    for copy in beside + partner:
        copy.wait_recv()
    recv_rows(0, lat_nb[0], pos_nb[0])
    recv_rows(2, lat_nb[1], pos_nb[1])
    send_rows(sib[1])
    up_b.wait_recv()
    near.append(pass_on(half(idn, 1)))
    send_rows(idn)
    dn_a.wait_recv()
    near.append(pass_on(half(iu, 0)))
    send_rows(iu)
    far_pos.wait_recv()
    last = [pass_on(pos_all.at[far])]
    for copy in near:
        copy.wait_recv()
    send_rows(other(idn))
    send_rows(other(iu))
    far_a.wait_recv()
    last.append(pass_on(half(far, 0)))
    far_b.wait_recv()
    last.append(pass_on(half(far, 1)))
    send_rows(far)
    for copy in last:
        copy.wait_recv()
    send_rows(other(far))
    cs.sent()


def gather(lat, pos, w_send, w_recv, pw, bias, mask, ts, tr, tc):
    own = lat.shape[0]
    n = GATHER_COPIES
    tiles = mask.shape[0]
    ranks = sd((tiles, 128, 128), BF16)
    return pl.pallas_call(
        gather_kernel,
        out_shape=[sd((8, own, 128), BF16), sd((8, own, 128), BF16), sd((3, own, 128), BF16),
                   ranks, ranks, sd((2 * tiles, 128), jnp.int32), sd((tiles,), jnp.int32),
                   sd((tiles,), jnp.int32), sd((1,), jnp.int32)],
        in_specs=[HBM] * 10,
        out_specs=[VM] * 9,
        scratch_shapes=[pltpu.VMEM((tiles, 128, 128), jnp.int32), pltpu.VMEM((2 * tiles, 128), F32),
                        pltpu.VMEM((8, 3, own), F32), pltpu.VMEM((2, own, 128), BF16),
                        pltpu.VMEM((2, 3, own), F32), pltpu.VMEM((128, 128), BF16),
                        pltpu.VMEM((128, 128), BF16), pltpu.VMEM((3, 128), F32),
                        pltpu.VMEM((1, 128), F32), pltpu.SemaphoreType.DMA((10,)),
                        pltpu.SemaphoreType.DMA((n,)), pltpu.SemaphoreType.DMA((n,))],
        compiler_params=pltpu.CompilerParams(collective_id=0, has_side_effects=True,
                                             vmem_limit_bytes=LIMIT),
        name="gather",
    )(*in_hbm(lat, pos, w_send, w_recv, pw, bias, mask, ts, tr), tc)


PIECES = 1
NODE_COPIES = 4 * PIECES + 2


def node_kernel(agg_own, agg_nb, cnt_own, cnt_nb, lat, cot, w_edge_out, w_node_self, w_node_msg,
                node_bias_in, w_node_out, gain_in, w_recv, new_lat, dagg, part, grads, agg_in, cnt_in,
                d_agg, direct, agg_b, message_b, hidden_b, d_update_b, d_pre_b, d_message_b,
                node_bias, gain, load_sem, send_sem, recv_sem):
    loads = fetch([(node_bias_in, node_bias), (gain_in, gain)], load_sem)
    me = Place()
    nxt, prv = me.slab(1), me.slab(-1)
    meet([nxt, prv])
    cs = Copies(send_sem, recv_sem)
    size = lat.shape[0] // PIECES
    pieces = [pl.ds(p * size, size) for p in range(PIECES)]
    arrive = []
    for p in pieces:
        arrive.append((cs.start(agg_nb.at[0, p], agg_in.at[0, p], prv),
                       cs.start(agg_nb.at[1, p], agg_in.at[1, p], nxt)))
    counts, leave = [], []
    for load in loads:
        load.wait()
    for i, p in enumerate(pieces):
        latent = lat[p]
        self_pre = dot(latent, w_node_self[...]) + node_bias[...]
        c = cot[p].astype(F32)
        d_normed = c * gain[...]
        d_centre = d_normed - jnp.mean(d_normed, axis=-1, keepdims=True)
        for copy in arrive[i]:
            copy.wait_recv()
        if i == PIECES - 1:
            counts = [cs.start(cnt_nb.at[0], cnt_in.at[0], prv),
                      cs.start(cnt_nb.at[1], cnt_in.at[1], nxt)]
        aggregate = agg_own[p] + agg_in[0, p].astype(F32) + agg_in[1, p].astype(F32)
        aggregate_b = aggregate.astype(BF16)
        message = dot(aggregate_b, w_edge_out[...]).astype(BF16)
        hidden_pre = self_pre + dot(message, w_node_msg[...])
        logistic = jax.nn.sigmoid(hidden_pre)
        hidden = (hidden_pre * logistic).astype(BF16)
        update = dot(hidden, w_node_out[...])
        average = jnp.mean(update, axis=-1, keepdims=True)
        centred = update - average
        variance = jnp.mean(centred * centred, axis=-1, keepdims=True)
        inv_std = lax.rsqrt(variance + 1e-05)
        normed = centred * inv_std
        d_update = (inv_std * (d_centre - normed * jnp.mean(d_normed * normed, axis=-1, keepdims=True))
                    ).astype(BF16)
        d_hidden = dot_t(d_update, w_node_out[...])
        d_hidden_pre = (d_hidden * logistic * (1.0 + hidden_pre * (1.0 - logistic))).astype(BF16)
        d_message = dot_t(d_hidden_pre, w_node_msg[...]).astype(BF16)
        d_aggregate = dot_t(d_message, w_edge_out[...])
        dagg[1, p] = d_aggregate.astype(BF16)
        leave.append(cs.start(dagg.at[1, p], dagg.at[0, p], nxt))
        leave.append(cs.start(dagg.at[1, p], dagg.at[2, p], prv))
        new_lat[p] = (latent.astype(F32) + normed * gain[...]).astype(BF16)
        d_agg[p] = d_aggregate
        agg_b[p] = aggregate_b
        message_b[p] = message
        hidden_b[p] = hidden
        d_update_b[p] = d_update
        d_pre_b[p] = d_hidden_pre
        d_message_b[p] = d_message
        direct[p] = c
    latent = lat[...]
    d_hidden_pre = d_pre_b[...]
    grads[1] = contract(agg_b[...], d_message_b[...])
    grads[2] = contract(latent, d_hidden_pre)
    grads[3] = contract(message_b[...], d_hidden_pre)
    grads[4] = contract(hidden_b[...], d_update_b[...])
    base = direct[...] + dot_t(d_hidden_pre, w_node_self[...])
    for copy in counts:
        copy.wait_recv()
    count = cnt_own[...] + cnt_in[0].astype(F32) + cnt_in[1].astype(F32)
    d_recv = (count * d_agg[...]).astype(BF16)
    grads[0] = contract(latent, d_recv)
    part[...] = base + dot_t(d_recv, w_recv[...])
    for copy in leave:
        copy.wait_recv()
    cs.sent()


def node(agg_own, agg_nb, cnt_own, cnt_nb, lat, cot, *weights):
    own = lat.shape[0]
    n = NODE_COPIES
    rows = pltpu.VMEM((own, 128), BF16)
    return pl.pallas_call(
        node_kernel,
        out_shape=[sd((own, 128), BF16), sd((3, own, 128), BF16), sd((own, 128), F32),
                   sd((5, 128, 128), F32)],
        in_specs=[VM] * 9 + [HBM, VM, HBM, VM],
        out_specs=[VM] * 4,
        scratch_shapes=[pltpu.VMEM((2, own, 128), BF16), pltpu.VMEM((2, own, 128), BF16),
                        pltpu.VMEM((own, 128), F32), pltpu.VMEM((own, 128), F32),
                        rows, rows, rows, rows, rows, rows, pltpu.VMEM((1, 128), F32),
                        pltpu.VMEM((1, 128), F32), pltpu.SemaphoreType.DMA((2,)),
                        pltpu.SemaphoreType.DMA((n,)), pltpu.SemaphoreType.DMA((n,))],
        compiler_params=pltpu.CompilerParams(collective_id=1, has_side_effects=True,
                                             vmem_limit_bytes=LIMIT),
        name="node",
    )(agg_own, agg_nb, cnt_own, cnt_nb, lat, cot, *weights)


FINAL_COPIES = 49


def final_kernel(dsend, gsend, grads, part, w_send, latent_grad, weight_grads, v, in_xc, vy, in_y,
                 vz, in_z, out_y, out, rs_core, cs_sum, in_ra, in_rb, in_da, in_db, in_fa, in_fb,
                 fwd_a, fwd_b, ready_y, ready_z, send_sem, recv_sem):
    me = Place()
    own = part.shape[0]
    up, dn, sib = me.member(1), me.member(-1), me.partner()
    core, zh = me.core, me.zh
    v[pl.ds(0, 128)] = gsend[...].astype(BF16)
    for i in range(5):
        v[pl.ds(128 * (i + 1), 128)] = grads[i].astype(BF16)
    vy[...] = jnp.zeros_like(vy)

    def chunk(c, x):
        return pl.ds(pl.multiple_of((c * NX + x) * 96, 16), 96)

    def y_peer(d):
        return me.at(y=(me.y + d + NY) % NY)

    def z_peer(d):
        return me.at(z=(me.z + d + NZ) % NZ)

    plane = [(dx, dc) for dx in range(NX) for dc in range(2) if dx or dc]
    spots = [((core + dc) % 2, (me.x + dx) % NX) for dx, dc in plane]
    peers = [me.at(x=x, core=c) for c, x in spots]
    meet(peers + [y_peer(d) for d in (1, 2, -1, -2)] + [z_peer(d) for d in (1, 2, 3, -1, -2, -3)])
    for d in (2, -2):
        pl.semaphore_signal(ready_y, inc=1, device_id=y_peer(d), device_id_type=MESH)
    for d in (3, -3):
        pl.semaphore_signal(ready_z, inc=1, device_id=z_peer(d), device_id_type=MESH)
    cs = Copies(send_sem, recv_sem)
    ha, hb = pl.ds(0, own // 2), pl.ds(own // 2, own // 2)

    ar_xc = [cs.start(v.at[chunk(*spots[j])], in_xc.at[j], peers[j]) for j in range(len(peers))]
    order = [2, 1, 3, 0]
    rs = [cs.start(dsend.at[((zh + o) % ZHI) * 2 + 1 - core], rs_core.at[(zh + o) % ZHI], sib)
          for o in order]

    def chip_sum(i):
        rs[i].wait_recv()
        k = (zh + order[i]) % ZHI
        cs_sum[k] = (dsend[k * 2 + core].astype(F32) + rs_core[k].astype(F32)).astype(BF16)
        return k

    far = chip_sum(0)
    ra = cs.start(cs_sum.at[far, ha], in_ra, up)
    rb = cs.start(cs_sum.at[far, hb], in_rb, dn)
    ku = chip_sum(1)
    db = cs.start(cs_sum.at[ku, hb], in_db, up)
    kd = chip_sum(2)
    da = cs.start(cs_sum.at[kd, ha], in_da, dn)

    for copy in ar_xc:
        copy.wait_recv()
    total = v[chunk(core, me.x)].astype(F32)
    for j in range(len(peers)):
        total = total + in_xc[j].astype(F32)
    for q in range(NY):
        vy[q, pl.ds(0, 12)] = total[12 * q:12 * q + 12].astype(BF16)
    pl.semaphore_wait(ready_y, 2)
    ar_y = [cs.start(vy.at[(me.y + d) % NY], in_y.at[d - 1], y_peer(d)) for d in range(1, NY)]
    chip_sum(3)

    for copy in ar_y:
        copy.wait_recv()
    total = vy[me.y].astype(F32)
    for d in range(NY - 1):
        total = total + in_y[d].astype(F32)
    vz[...] = total.astype(BF16)
    in_z[me.z] = total.astype(BF16)
    pl.semaphore_wait(ready_z, 2)
    ar_z = [cs.start(vz, in_z.at[me.z], z_peer(d)) for d in range(1, NZ)]

    for copy in ar_z:
        copy.wait_recv()
    total = in_z[0].astype(F32)
    for d in range(1, NZ):
        total = total + in_z[d].astype(F32)
    out_y[me.y] = total.astype(BF16)
    ag_y = [cs.start(out_y.at[me.y], out_y.at[me.y], y_peer(d)) for d in range(1, NY)]

    ra.wait_recv()
    fwd_a[...] = (in_ra[...].astype(F32) + cs_sum[ku, ha].astype(F32)).astype(BF16)
    fa = cs.start(fwd_a, in_fa, up)
    rb.wait_recv()
    fwd_b[...] = (in_rb[...].astype(F32) + cs_sum[kd, hb].astype(F32)).astype(BF16)
    fb = cs.start(fwd_b, in_fb, dn)

    for copy in ag_y:
        copy.wait_recv()
    mine = chunk(core, me.x)
    out[mine] = jnp.concatenate([out_y[q].astype(F32)[:12] for q in range(NY)], 0).astype(BF16)
    ag_xc = [cs.start(out.at[mine], out.at[mine], peer) for peer in peers]
    da.wait_recv()
    db.wait_recv()
    fa.wait_recv()
    d_a = cs_sum[zh, ha].astype(F32) + in_da[...].astype(F32) + in_fa[...].astype(F32)
    latent_grad[ha] = part[ha] + dot_t(d_a.astype(BF16), w_send[...])
    fb.wait_recv()
    d_b = cs_sum[zh, hb].astype(F32) + in_db[...].astype(F32) + in_fb[...].astype(F32)
    latent_grad[hb] = part[hb] + dot_t(d_b.astype(BF16), w_send[...])

    for copy in ag_xc:
        copy.wait_recv()
    for i in range(6):
        weight_grads[i] = out[pl.ds(128 * i, 128)].astype(F32)
    cs.sent()


def final(dsend, gsend, grads, part, w_send):
    own = part.shape[0]
    n = FINAL_COPIES
    b = lambda *shape: pltpu.VMEM(shape, BF16)
    h = own // 2
    return pl.pallas_call(
        final_kernel,
        out_shape=[sd((own, 128), F32), sd((6, 128, 128), F32)],
        in_specs=[VM] * 5,
        out_specs=[VM] * 2,
        scratch_shapes=[
            b(768, 128), b(2 * NX - 1, 96, 128), b(NY, 16, 128), b(NY - 1, 16, 128), b(16, 128),
            b(NZ, 16, 128), b(NY, 16, 128), b(768, 128), b(ZHI, own, 128), b(ZHI, own, 128),
            b(h, 128), b(h, 128), b(h, 128), b(h, 128), b(h, 128), b(h, 128), b(h, 128), b(h, 128),
            pltpu.SemaphoreType.REGULAR, pltpu.SemaphoreType.REGULAR,
            pltpu.SemaphoreType.DMA((n,)), pltpu.SemaphoreType.DMA((n,))],
        compiler_params=pltpu.CompilerParams(collective_id=2, has_side_effects=True,
                                             vmem_limit_bytes=LIMIT),
        name="final",
    )(dsend, gsend, grads, part, w_send)


def finish_kernel(a, b, a_out, b_out, sem):
    for copy in fetch([(a, a_out), (b, b_out)], sem):
        copy.wait()


def finish(a, b):
    return pl.pallas_call(
        finish_kernel,
        out_shape=[sd(a.shape, a.dtype), sd(b.shape, b.dtype)],
        in_specs=[VM] * 2,
        out_specs=[HBM] * 2,
        scratch_shapes=[pltpu.SemaphoreType.DMA((2,))],
        compiler_params=pltpu.CompilerParams(vmem_limit_bytes=LIMIT),
        name="finish",
    )(a, b)


def body(latent, positions, tile_send, tile_recv, tile_mask, tile_count, w_send, w_recv, pos_weight,
         edge_bias, w_edge_out, w_node_self, w_node_msg, node_bias, w_node_out, gain, cotangent):
    ts, tr, tc = tile_send[0, 0], tile_recv[0, 0], tile_count[0]
    lat_all, s_rows, r_rows, rank_r, rank_t, most, ts, tr, tc = gather(
        latent, positions, w_send, w_recv, pos_weight, edge_bias[None], tile_mask[0, 0], ts, tr, tc)
    s_rows = s_rows.reshape(32, 128, 128)
    r_rows = r_rows.reshape(12, 128, 128)
    agg_own, agg_nb, cnt_own, cnt_nb = forward(ts, tr, tc, most, s_rows, r_rows, rank_r)
    new_latent, dagg, part, grads = node(
        agg_own, agg_nb, cnt_own, cnt_nb, latent, cotangent, w_edge_out, w_node_self, w_node_msg,
        *in_hbm(node_bias[None]), w_node_out, *in_hbm(gain[None]), w_recv)
    dsend, gsend, new_latent = backward(ts, tr, tc, most, rank_t, s_rows, r_rows, dagg.reshape(12, 128, 128),
                            lat_all, new_latent)
    latent_grad, weight_grads = finish(*final(dsend, gsend, grads, part, w_send))
    return new_latent, latent_grad, weight_grads


def solution(mesh):
    in_specs = (
        P(("blk", "grp"), None),
        P(None, ("blk", "grp")),
        P("blk", "grp", None),
        P("blk", "grp", None),
        P("blk", "grp", None, None, None),
        P("blk", "grp"),
        P(),
        P(),
        P(),
        P(),
        P(),
        P(),
        P(),
        P(),
        P(),
        P(),
        P(("blk", "grp"), None),
    )
    out_specs = (P(("blk", "grp"), None), P(("blk", "grp"), None), P())
    return jax.shard_map(body, mesh=mesh, in_specs=in_specs, out_specs=out_specs, check_vma=False)
```

```python
import functools

import jax
import jax.numpy as jnp
from jax import lax
from jax.experimental import pallas as pl
from jax.experimental.pallas import tpu as pltpu
from jax.sharding import PartitionSpec as P

F32, BF16 = jnp.float32, jnp.bfloat16
DN0 = (((0,), (0,)), ((), ()))
DN1 = (((1,), (1,)), ((), ()))
MESH = pl.DeviceIdType.MESH
SMEM = pl.BlockSpec(memory_space=pltpu.SMEM)
VM = pl.BlockSpec(memory_space=pltpu.VMEM)
HBM = pl.BlockSpec(memory_space=pltpu.HBM)
NX, NY, NZ, ZLO, ZHI = 4, 8, 12, 3, 4
SLABS = NX * NY * ZLO
LIMIT = 16 << 20


class Place:
    def __init__(self):
        self.blk = lax.axis_index("blk")
        self.grp = lax.axis_index("grp")
        self.x = self.blk % NX
        self.y = (self.blk // NX) % NY
        self.zl = self.blk // (NX * NY)
        self.core = self.grp % 2
        self.zh = self.grp // 2
        self.z = self.zh * ZLO + self.zl

    def at(self, x=None, y=None, z=None, core=None):
        x = self.x if x is None else x
        y = self.y if y is None else y
        z = self.z if z is None else z
        core = self.core if core is None else core
        return ((z % ZLO) * (NX * NY) + y * NX + x, (z // ZLO) * 2 + core)

    def slab(self, step):
        return ((self.blk + step + SLABS) % SLABS, self.grp)

    def member(self, step):
        return (self.blk, ((self.zh + step + ZHI) % ZHI) * 2 + self.core)

    def partner(self):
        return (self.blk, self.zh * 2 + 1 - self.core)


def meet(peers):
    barrier = pltpu.get_barrier_semaphore()
    for peer in peers:
        pl.semaphore_signal(barrier, inc=1, device_id=peer, device_id_type=MESH)
    pl.semaphore_wait(barrier, len(peers))


class Copies:
    def __init__(self, send_sem, recv_sem):
        self.send_sem, self.recv_sem, self.started = send_sem, recv_sem, []

    def start(self, src, dst, device):
        number = len(self.started)
        copy = pltpu.make_async_remote_copy(
            src_ref=src, dst_ref=dst, send_sem=self.send_sem.at[number],
            recv_sem=self.recv_sem.at[number], device_id=device, device_id_type=MESH)
        copy.start()
        self.started.append(copy)
        return copy

    def sent(self):
        for copy in self.started:
            copy.wait_send()


def fetch(pairs, sem):
    copies = [pltpu.make_async_copy(src, dst, sem.at[i]) for i, (src, dst) in enumerate(pairs)]
    for copy in copies:
        copy.start()
    return copies


def in_hbm(*arrays):
    return [pltpu.with_memory_space_constraint(a, pltpu.HBM) for a in arrays]


def sd(shape, dtype):
    return jax.ShapeDtypeStruct(shape, dtype)


def dot(a, b):
    return jnp.dot(a, b, preferred_element_type=F32)


def dot_t(a, b):
    return lax.dot_general(a, b, DN1, preferred_element_type=F32)


def contract(a, b):
    return lax.dot_general(a, b, DN0, preferred_element_type=F32)


def placed_of(pos, pw):
    return lax.dot_general(pos, pw, DN0, precision=lax.Precision.HIGHEST,
                           preferred_element_type=F32)


def rank_tiles(mask, rank_r, rank_t, top):
    tiles = mask.shape[0]
    row = lax.broadcasted_iota(jnp.int32, (128, 128), 0)
    col = lax.broadcasted_iota(jnp.int32, (128, 128), 1)
    upper = jnp.where(row < col, 1.0, 0.0).astype(BF16)

    def ranks(values):
        return jnp.where(values > 0.0, dot(values.astype(BF16), upper), -1.0)

    def tile(t, _):
        values = mask[t].astype(F32)
        by_row = ranks(values)
        rank_r[t] = by_row
        top[pl.ds(t, 1), :] = jnp.max(by_row, axis=0, keepdims=True)
        by_col = ranks(values.T)
        rank_t[t] = by_col
        top[pl.ds(t + tiles, 1), :] = jnp.max(by_col, axis=0, keepdims=True)
        return 0

    lax.fori_loop(0, tiles, tile, 0)


def slot_counts(top):
    most = jnp.max(top[...], axis=1, keepdims=True) + 1.0
    return jnp.broadcast_to(most, top.shape).astype(jnp.int32)


def picks(ranks, slot):
    one, none = jnp.ones((), BF16), jnp.zeros((), BF16)
    if isinstance(slot, int):
        slot = jnp.full((), slot, BF16)
    else:
        slot = slot.astype(F32).astype(BF16)
    return jnp.where(ranks == slot, one, none)


def slot_batches(first, group):
    return [range(k, min(k + group, first)) for k in range(0, first, group)]


def forward_kernel(first, more, group, ts, tr, tc, most, s_rows, r_rows, rank_r, agg_own, agg_nb,
                   cnt_own, cnt_nb, agg, cnt):
    agg[...] = jnp.zeros_like(agg)
    cnt[...] = jnp.zeros_like(cnt)
    ones = jnp.ones((128, 128), BF16)
    none = jnp.zeros((), BF16)

    def tile(t, _):
        rb = tr[t]
        s = s_rows[ts[t]]
        rk = rank_r[t].astype(BF16)
        floor = -(r_rows[rb].astype(F32))
        floor_b = floor.astype(BF16)

        def add(slots, a, c):
            x = dot(jnp.concatenate([picks(rk, slot) for slot in slots], 0), s)
            for q in range(len(slots)):
                part = x[128 * q:128 * q + 128]
                a = a + jnp.maximum(part, floor)
                c = c + jnp.where(part.astype(BF16) > floor_b, jnp.ones((), BF16), none)
            return a, c

        a = jnp.zeros((128, 128), F32)
        c = jnp.zeros((128, 128), BF16)
        for slots in slot_batches(first, group):
            a, c = add(slots, a, c)
        n = (jnp.maximum(most[t, 0] - first, 0) + more - 1) // more

        def rest(i, carry):
            return add([first + i * more + q for q in range(more)], *carry)

        a, c = lax.fori_loop(0, n, rest, (a, c))
        degree = dot(jnp.where(rk >= none, jnp.ones((), BF16), none), ones)
        spare = (first + n * more).astype(F32) - degree
        agg[rb] += a - degree * floor - spare * jnp.maximum(floor, 0.0)
        cnt[rb] += c.astype(F32) - spare * jnp.where(floor < 0.0, 1.0, 0.0)
        return 0

    lax.fori_loop(0, tc[0], tile, 0)
    for b in range(4):
        sl = pl.ds(b * 128, 128)
        agg_own[sl] = agg[4 + b]
        cnt_own[sl] = cnt[4 + b]
        agg_nb[0, sl] = agg[b].astype(BF16)
        agg_nb[1, sl] = agg[8 + b].astype(BF16)
        cnt_nb[0, sl] = cnt[b].astype(BF16)
        cnt_nb[1, sl] = cnt[8 + b].astype(BF16)


def forward(ts, tr, tc, most, s_rows, r_rows, rank_r, first=18, more=4, group=3):
    own = 512
    return pl.pallas_call(
        functools.partial(forward_kernel, first, more, group),
        out_shape=[sd((own, 128), F32), sd((2, own, 128), BF16), sd((own, 128), F32),
                   sd((2, own, 128), BF16)],
        in_specs=[SMEM] * 4 + [VM] * 3,
        out_specs=[VM] * 4,
        scratch_shapes=[pltpu.VMEM((12, 128, 128), F32), pltpu.VMEM((12, 128, 128), F32)],
        compiler_params=pltpu.CompilerParams(vmem_limit_bytes=LIMIT),
        name="forward",
    )(ts, tr, tc, most, s_rows, r_rows, rank_r)


def backward_kernel(first, more, group, ts, tr, tc, most, rank_t, s_rows, r_rows, dagg, lat_all,
                    new_in, dsend, gsend, new_out, acc):
    new_out[...] = new_in[...]
    acc[...] = jnp.zeros_like(acc)
    tiles = rank_t.shape[0]

    def tile(t, _):
        sb = ts[t]
        rb = tr[t]
        rk = rank_t[t].astype(BF16)
        floor = -(s_rows[sb].astype(F32))
        rhs = jnp.concatenate([r_rows[rb], dagg[rb]], axis=1)

        def add(slots, a):
            x = dot(jnp.concatenate([picks(rk, slot) for slot in slots], 0), rhs)
            for q in range(len(slots)):
                part = x[128 * q:128 * q + 128]
                a = a + jnp.where(part[:, :128] > floor, part[:, 128:], 0.0)
            return a

        a = jnp.zeros((128, 128), F32)
        for slots in slot_batches(first, group):
            a = add(slots, a)
        n = (jnp.maximum(most[t + tiles, 0] - first, 0) + more - 1) // more

        def rest(i, a):
            return add([first + i * more + q for q in range(more)], a)

        acc[sb] += lax.fori_loop(0, n, rest, a)
        return 0

    lax.fori_loop(0, tc[0], tile, 0)
    g = jnp.zeros((128, 128), F32)
    for b in range(8):
        d = acc[pl.ds(4 * b, 4)].reshape(512, 128).astype(BF16)
        dsend[b] = d
        g = g + contract(lat_all[b], d)
    gsend[...] = g


def backward(ts, tr, tc, most, rank_t, s_rows, r_rows, dagg, lat_all, new_lat, first=18, more=4, group=6):
    return pl.pallas_call(
        functools.partial(backward_kernel, first, more, group),
        out_shape=[sd((8, 512, 128), BF16), sd((128, 128), F32), sd((512, 128), BF16)],
        in_specs=[SMEM] * 4 + [VM] * 6,
        out_specs=[VM] * 3,
        scratch_shapes=[pltpu.VMEM((32, 128, 128), F32)],
        compiler_params=pltpu.CompilerParams(vmem_limit_bytes=LIMIT),
        name="backward",
    )(ts, tr, tc, most, rank_t, s_rows, r_rows, dagg, lat_all, new_lat)


GATHER_COPIES = 24


def gather_kernel(lat, pos, w_send_in, w_recv_in, pw_in, bias_in, mask_in, ts_in, tr_in, tc_in,
                  lat_all, s_rows, r_rows, rank_r, rank_t, most, ts, tr, tc, mask, top, pos_all,
                  lat_nb, pos_nb, w_send, w_recv, pw, bias, load_sem, send_sem, recv_sem):
    me = Place()
    own = lat.shape[0]
    g = me.grp
    loads = fetch([(lat, lat_all.at[g]), (pos, pos_all.at[g]), (w_send_in, w_send),
                   (w_recv_in, w_recv), (pw_in, pw), (bias_in, bias), (mask_in, mask), (ts_in, ts),
                   (tr_in, tr), (tc_in, tc)], load_sem)
    up, dn, sib = me.member(1), me.member(-1), me.partner()
    nxt, prv = me.slab(1), me.slab(-1)
    meet([up, dn, sib, nxt, prv])
    cs = Copies(send_sem, recv_sem)
    halves = (pl.ds(0, own // 2), pl.ds(own // 2, own // 2))

    def half(index, h):
        return lat_all.at[index, halves[h]]

    up_pos = cs.start(pos, pos_all.at[g], up)
    dn_pos = cs.start(pos, pos_all.at[g], dn)
    up_a = cs.start(lat.at[halves[0]], half(g, 0), up)
    dn_b = cs.start(lat.at[halves[1]], half(g, 1), dn)
    up_b = cs.start(lat.at[halves[1]], half(g, 1), up)
    dn_a = cs.start(lat.at[halves[0]], half(g, 0), dn)
    beside = [
        cs.start(lat, lat_nb.at[0], nxt),
        cs.start(lat, lat_nb.at[1], prv),
        cs.start(pos, pos_nb.at[0], nxt),
        cs.start(pos, pos_nb.at[1], prv),
    ]
    partner = [
        cs.start(lat, lat_all.at[g], sib),
        cs.start(pos, pos_all.at[g], sib),
    ]
    iu, idn, far = up[1], dn[1], me.member(2)[1]

    def pass_on(ref):
        return cs.start(ref, ref, sib)

    def send_rows(index):
        s_rows[index] = (dot(lat_all[index], w_send[...])
                         + placed_of(pos_all[index], pw[...])).astype(BF16)

    def recv_rows(slab, rows, places):
        r_rows[slab] = (dot(rows, w_recv[...]) - placed_of(places, pw[...])
                        + bias[...]).astype(BF16)

    def other(index):
        return (index // 2) * 2 + 1 - me.core

    for load in loads:
        load.wait()
    recv_rows(1, lat_all[g], pos_all[g])
    send_rows(g)
    rank_tiles(mask, rank_r, rank_t, top)
    most[...] = slot_counts(top)

    up_pos.wait_recv()
    far_pos = cs.start(pos_all.at[idn], pos_all.at[idn], up)
    near = [pass_on(pos_all.at[idn])]
    dn_pos.wait_recv()
    near.append(pass_on(pos_all.at[iu]))
    up_a.wait_recv()
    far_a = cs.start(half(idn, 0), half(idn, 0), up)
    near.append(pass_on(half(idn, 0)))
    dn_b.wait_recv()
    far_b = cs.start(half(iu, 1), half(iu, 1), dn)
    near.append(pass_on(half(iu, 1)))
    for copy in beside + partner:
        copy.wait_recv()
    recv_rows(0, lat_nb[0], pos_nb[0])
    recv_rows(2, lat_nb[1], pos_nb[1])
    send_rows(sib[1])
    up_b.wait_recv()
    near.append(pass_on(half(idn, 1)))
    send_rows(idn)
    dn_a.wait_recv()
    near.append(pass_on(half(iu, 0)))
    send_rows(iu)
    far_pos.wait_recv()
    last = [pass_on(pos_all.at[far])]
    for copy in near:
        copy.wait_recv()
    send_rows(other(idn))
    send_rows(other(iu))
    far_a.wait_recv()
    last.append(pass_on(half(far, 0)))
    far_b.wait_recv()
    last.append(pass_on(half(far, 1)))
    send_rows(far)
    for copy in last:
        copy.wait_recv()
    send_rows(other(far))
    cs.sent()


def gather(lat, pos, w_send, w_recv, pw, bias, mask, ts, tr, tc):
    own = lat.shape[0]
    n = GATHER_COPIES
    tiles = mask.shape[0]
    ranks = sd((tiles, 128, 128), F32)
    return pl.pallas_call(
        gather_kernel,
        out_shape=[sd((8, own, 128), BF16), sd((8, own, 128), BF16), sd((3, own, 128), BF16),
                   ranks, ranks, sd((2 * tiles, 128), jnp.int32), sd((tiles,), jnp.int32),
                   sd((tiles,), jnp.int32), sd((1,), jnp.int32)],
        in_specs=[HBM] * 10,
        out_specs=[VM] * 9,
        scratch_shapes=[pltpu.VMEM((tiles, 128, 128), jnp.int32), pltpu.VMEM((2 * tiles, 128), F32),
                        pltpu.VMEM((8, 3, own), F32), pltpu.VMEM((2, own, 128), BF16),
                        pltpu.VMEM((2, 3, own), F32), pltpu.VMEM((128, 128), BF16),
                        pltpu.VMEM((128, 128), BF16), pltpu.VMEM((3, 128), F32),
                        pltpu.VMEM((1, 128), F32), pltpu.SemaphoreType.DMA((10,)),
                        pltpu.SemaphoreType.DMA((n,)), pltpu.SemaphoreType.DMA((n,))],
        compiler_params=pltpu.CompilerParams(collective_id=0, has_side_effects=True,
                                             vmem_limit_bytes=LIMIT),
        name="gather",
    )(*in_hbm(lat, pos, w_send, w_recv, pw, bias, mask, ts, tr), tc)


PIECES = 1
NODE_COPIES = 4 * PIECES + 2


def node_kernel(agg_own, agg_nb, cnt_own, cnt_nb, lat, cot, w_edge_out, w_node_self, w_node_msg,
                node_bias_in, w_node_out, gain_in, w_recv, new_lat, dagg, part, grads, agg_in, cnt_in,
                d_agg, direct, agg_b, message_b, hidden_b, d_update_b, d_pre_b, d_message_b,
                node_bias, gain, load_sem, send_sem, recv_sem):
    loads = fetch([(node_bias_in, node_bias), (gain_in, gain)], load_sem)
    me = Place()
    nxt, prv = me.slab(1), me.slab(-1)
    meet([nxt, prv])
    cs = Copies(send_sem, recv_sem)
    size = lat.shape[0] // PIECES
    pieces = [pl.ds(p * size, size) for p in range(PIECES)]
    arrive = []
    for p in pieces:
        arrive.append((cs.start(agg_nb.at[0, p], agg_in.at[0, p], prv),
                       cs.start(agg_nb.at[1, p], agg_in.at[1, p], nxt)))
    counts, leave = [], []
    for load in loads:
        load.wait()
    for i, p in enumerate(pieces):
        latent = lat[p]
        self_pre = dot(latent, w_node_self[...]) + node_bias[...]
        c = cot[p].astype(F32)
        d_normed = c * gain[...]
        d_centre = d_normed - jnp.mean(d_normed, axis=-1, keepdims=True)
        for copy in arrive[i]:
            copy.wait_recv()
        if i == PIECES - 1:
            counts = [cs.start(cnt_nb.at[0], cnt_in.at[0], prv),
                      cs.start(cnt_nb.at[1], cnt_in.at[1], nxt)]
        aggregate = agg_own[p] + agg_in[0, p].astype(F32) + agg_in[1, p].astype(F32)
        aggregate_b = aggregate.astype(BF16)
        message = dot(aggregate_b, w_edge_out[...]).astype(BF16)
        hidden_pre = self_pre + dot(message, w_node_msg[...])
        logistic = jax.nn.sigmoid(hidden_pre)
        hidden = (hidden_pre * logistic).astype(BF16)
        update = dot(hidden, w_node_out[...])
        average = jnp.mean(update, axis=-1, keepdims=True)
        centred = update - average
        variance = jnp.mean(centred * centred, axis=-1, keepdims=True)
        inv_std = lax.rsqrt(variance + 1e-05)
        normed = centred * inv_std
        d_update = (inv_std * (d_centre - normed * jnp.mean(d_normed * normed, axis=-1, keepdims=True))
                    ).astype(BF16)
        d_hidden = dot_t(d_update, w_node_out[...])
        d_hidden_pre = (d_hidden * logistic * (1.0 + hidden_pre * (1.0 - logistic))).astype(BF16)
        d_message = dot_t(d_hidden_pre, w_node_msg[...]).astype(BF16)
        d_aggregate = dot_t(d_message, w_edge_out[...])
        dagg[1, p] = d_aggregate.astype(BF16)
        leave.append(cs.start(dagg.at[1, p], dagg.at[0, p], nxt))
        leave.append(cs.start(dagg.at[1, p], dagg.at[2, p], prv))
        new_lat[p] = (latent.astype(F32) + normed * gain[...]).astype(BF16)
        d_agg[p] = d_aggregate
        agg_b[p] = aggregate_b
        message_b[p] = message
        hidden_b[p] = hidden
        d_update_b[p] = d_update
        d_pre_b[p] = d_hidden_pre
        d_message_b[p] = d_message
        direct[p] = c
    latent = lat[...]
    d_hidden_pre = d_pre_b[...]
    grads[1] = contract(agg_b[...], d_message_b[...])
    grads[2] = contract(latent, d_hidden_pre)
    grads[3] = contract(message_b[...], d_hidden_pre)
    grads[4] = contract(hidden_b[...], d_update_b[...])
    base = direct[...] + dot_t(d_hidden_pre, w_node_self[...])
    for copy in counts:
        copy.wait_recv()
    count = cnt_own[...] + cnt_in[0].astype(F32) + cnt_in[1].astype(F32)
    d_recv = (count * d_agg[...]).astype(BF16)
    grads[0] = contract(latent, d_recv)
    part[...] = base + dot_t(d_recv, w_recv[...])
    for copy in leave:
        copy.wait_recv()
    cs.sent()


def node(agg_own, agg_nb, cnt_own, cnt_nb, lat, cot, *weights):
    own = lat.shape[0]
    n = NODE_COPIES
    rows = pltpu.VMEM((own, 128), BF16)
    return pl.pallas_call(
        node_kernel,
        out_shape=[sd((own, 128), BF16), sd((3, own, 128), BF16), sd((own, 128), F32),
                   sd((5, 128, 128), F32)],
        in_specs=[VM] * 9 + [HBM, VM, HBM, VM],
        out_specs=[VM] * 4,
        scratch_shapes=[pltpu.VMEM((2, own, 128), BF16), pltpu.VMEM((2, own, 128), BF16),
                        pltpu.VMEM((own, 128), F32), pltpu.VMEM((own, 128), F32),
                        rows, rows, rows, rows, rows, rows, pltpu.VMEM((1, 128), F32),
                        pltpu.VMEM((1, 128), F32), pltpu.SemaphoreType.DMA((2,)),
                        pltpu.SemaphoreType.DMA((n,)), pltpu.SemaphoreType.DMA((n,))],
        compiler_params=pltpu.CompilerParams(collective_id=1, has_side_effects=True,
                                             vmem_limit_bytes=LIMIT),
        name="node",
    )(agg_own, agg_nb, cnt_own, cnt_nb, lat, cot, *weights)


FINAL_COPIES = 49


def final_kernel(dsend, gsend, grads, part, w_send, latent_grad, weight_grads, v, in_xc, vy, in_y,
                 vz, in_z, out_y, out, rs_core, cs_sum, in_ra, in_rb, in_da, in_db, in_fa, in_fb,
                 fwd_a, fwd_b, ready_y, ready_z, send_sem, recv_sem):
    me = Place()
    own = part.shape[0]
    up, dn, sib = me.member(1), me.member(-1), me.partner()
    core, zh = me.core, me.zh
    v[pl.ds(0, 128)] = gsend[...].astype(BF16)
    for i in range(5):
        v[pl.ds(128 * (i + 1), 128)] = grads[i].astype(BF16)
    vy[...] = jnp.zeros_like(vy)

    def chunk(c, x):
        return pl.ds(pl.multiple_of((c * NX + x) * 96, 16), 96)

    def y_peer(d):
        return me.at(y=(me.y + d + NY) % NY)

    def z_peer(d):
        return me.at(z=(me.z + d + NZ) % NZ)

    plane = [(dx, dc) for dx in range(NX) for dc in range(2) if dx or dc]
    spots = [((core + dc) % 2, (me.x + dx) % NX) for dx, dc in plane]
    peers = [me.at(x=x, core=c) for c, x in spots]
    meet(peers + [y_peer(d) for d in (1, 2, -1, -2)] + [z_peer(d) for d in (1, 2, 3, -1, -2, -3)])
    for d in (2, -2):
        pl.semaphore_signal(ready_y, inc=1, device_id=y_peer(d), device_id_type=MESH)
    for d in (3, -3):
        pl.semaphore_signal(ready_z, inc=1, device_id=z_peer(d), device_id_type=MESH)
    cs = Copies(send_sem, recv_sem)
    ha, hb = pl.ds(0, own // 2), pl.ds(own // 2, own // 2)

    ar_xc = [cs.start(v.at[chunk(*spots[j])], in_xc.at[j], peers[j]) for j in range(len(peers))]
    order = [2, 1, 3, 0]
    rs = [cs.start(dsend.at[((zh + o) % ZHI) * 2 + 1 - core], rs_core.at[(zh + o) % ZHI], sib)
          for o in order]

    def chip_sum(i):
        rs[i].wait_recv()
        k = (zh + order[i]) % ZHI
        cs_sum[k] = (dsend[k * 2 + core].astype(F32) + rs_core[k].astype(F32)).astype(BF16)
        return k

    far = chip_sum(0)
    ra = cs.start(cs_sum.at[far, ha], in_ra, up)
    rb = cs.start(cs_sum.at[far, hb], in_rb, dn)
    ku = chip_sum(1)
    db = cs.start(cs_sum.at[ku, hb], in_db, up)
    kd = chip_sum(2)
    da = cs.start(cs_sum.at[kd, ha], in_da, dn)

    for copy in ar_xc:
        copy.wait_recv()
    total = v[chunk(core, me.x)].astype(F32)
    for j in range(len(peers)):
        total = total + in_xc[j].astype(F32)
    for q in range(NY):
        vy[q, pl.ds(0, 12)] = total[12 * q:12 * q + 12].astype(BF16)
    pl.semaphore_wait(ready_y, 2)
    ar_y = [cs.start(vy.at[(me.y + d) % NY], in_y.at[d - 1], y_peer(d)) for d in range(1, NY)]
    chip_sum(3)

    for copy in ar_y:
        copy.wait_recv()
    total = vy[me.y].astype(F32)
    for d in range(NY - 1):
        total = total + in_y[d].astype(F32)
    vz[...] = total.astype(BF16)
    in_z[me.z] = total.astype(BF16)
    pl.semaphore_wait(ready_z, 2)
    ar_z = [cs.start(vz, in_z.at[me.z], z_peer(d)) for d in range(1, NZ)]

    for copy in ar_z:
        copy.wait_recv()
    total = in_z[0].astype(F32)
    for d in range(1, NZ):
        total = total + in_z[d].astype(F32)
    out_y[me.y] = total.astype(BF16)
    ag_y = [cs.start(out_y.at[me.y], out_y.at[me.y], y_peer(d)) for d in range(1, NY)]

    ra.wait_recv()
    fwd_a[...] = (in_ra[...].astype(F32) + cs_sum[ku, ha].astype(F32)).astype(BF16)
    fa = cs.start(fwd_a, in_fa, up)
    rb.wait_recv()
    fwd_b[...] = (in_rb[...].astype(F32) + cs_sum[kd, hb].astype(F32)).astype(BF16)
    fb = cs.start(fwd_b, in_fb, dn)

    for copy in ag_y:
        copy.wait_recv()
    mine = chunk(core, me.x)
    out[mine] = jnp.concatenate([out_y[q].astype(F32)[:12] for q in range(NY)], 0).astype(BF16)
    ag_xc = [cs.start(out.at[mine], out.at[mine], peer) for peer in peers]
    da.wait_recv()
    db.wait_recv()
    fa.wait_recv()
    d_a = cs_sum[zh, ha].astype(F32) + in_da[...].astype(F32) + in_fa[...].astype(F32)
    latent_grad[ha] = part[ha] + dot_t(d_a.astype(BF16), w_send[...])
    fb.wait_recv()
    d_b = cs_sum[zh, hb].astype(F32) + in_db[...].astype(F32) + in_fb[...].astype(F32)
    latent_grad[hb] = part[hb] + dot_t(d_b.astype(BF16), w_send[...])

    for copy in ag_xc:
        copy.wait_recv()
    for i in range(6):
        weight_grads[i] = out[pl.ds(128 * i, 128)].astype(F32)
    cs.sent()


def final(dsend, gsend, grads, part, w_send):
    own = part.shape[0]
    n = FINAL_COPIES
    b = lambda *shape: pltpu.VMEM(shape, BF16)
    h = own // 2
    return pl.pallas_call(
        final_kernel,
        out_shape=[sd((own, 128), F32), sd((6, 128, 128), F32)],
        in_specs=[VM] * 5,
        out_specs=[VM] * 2,
        scratch_shapes=[
            b(768, 128), b(2 * NX - 1, 96, 128), b(NY, 16, 128), b(NY - 1, 16, 128), b(16, 128),
            b(NZ, 16, 128), b(NY, 16, 128), b(768, 128), b(ZHI, own, 128), b(ZHI, own, 128),
            b(h, 128), b(h, 128), b(h, 128), b(h, 128), b(h, 128), b(h, 128), b(h, 128), b(h, 128),
            pltpu.SemaphoreType.REGULAR, pltpu.SemaphoreType.REGULAR,
            pltpu.SemaphoreType.DMA((n,)), pltpu.SemaphoreType.DMA((n,))],
        compiler_params=pltpu.CompilerParams(collective_id=2, has_side_effects=True,
                                             vmem_limit_bytes=LIMIT),
        name="final",
    )(dsend, gsend, grads, part, w_send)


def finish_kernel(a, b, a_out, b_out, sem):
    for copy in fetch([(a, a_out), (b, b_out)], sem):
        copy.wait()


def finish(a, b):
    return pl.pallas_call(
        finish_kernel,
        out_shape=[sd(a.shape, a.dtype), sd(b.shape, b.dtype)],
        in_specs=[VM] * 2,
        out_specs=[HBM] * 2,
        scratch_shapes=[pltpu.SemaphoreType.DMA((2,))],
        compiler_params=pltpu.CompilerParams(vmem_limit_bytes=LIMIT),
        name="finish",
    )(a, b)


def body(latent, positions, tile_send, tile_recv, tile_mask, tile_count, w_send, w_recv, pos_weight,
         edge_bias, w_edge_out, w_node_self, w_node_msg, node_bias, w_node_out, gain, cotangent):
    ts, tr, tc = tile_send[0, 0], tile_recv[0, 0], tile_count[0]
    lat_all, s_rows, r_rows, rank_r, rank_t, most, ts, tr, tc = gather(
        latent, positions, w_send, w_recv, pos_weight, edge_bias[None], tile_mask[0, 0], ts, tr, tc)
    s_rows = s_rows.reshape(32, 128, 128)
    r_rows = r_rows.reshape(12, 128, 128)
    agg_own, agg_nb, cnt_own, cnt_nb = forward(ts, tr, tc, most, s_rows, r_rows, rank_r)
    new_latent, dagg, part, grads = node(
        agg_own, agg_nb, cnt_own, cnt_nb, latent, cotangent, w_edge_out, w_node_self, w_node_msg,
        *in_hbm(node_bias[None]), w_node_out, *in_hbm(gain[None]), w_recv)
    dsend, gsend, new_latent = backward(ts, tr, tc, most, rank_t, s_rows, r_rows, dagg.reshape(12, 128, 128),
                            lat_all, new_latent)
    latent_grad, weight_grads = finish(*final(dsend, gsend, grads, part, w_send))
    return new_latent, latent_grad, weight_grads


def solution(mesh):
    in_specs = (
        P(("blk", "grp"), None),
        P(None, ("blk", "grp")),
        P("blk", "grp", None),
        P("blk", "grp", None),
        P("blk", "grp", None, None, None),
        P("blk", "grp"),
        P(),
        P(),
        P(),
        P(),
        P(),
        P(),
        P(),
        P(),
        P(),
        P(),
        P(("blk", "grp"), None),
    )
    out_specs = (P(("blk", "grp"), None), P(("blk", "grp"), None), P())
    return jax.shard_map(body, mesh=mesh, in_specs=in_specs, out_specs=out_specs, check_vma=False)
```

```python
import functools

import jax
import jax.numpy as jnp
from jax import lax
from jax.experimental import pallas as pl
from jax.experimental.pallas import tpu as pltpu
from jax.sharding import PartitionSpec as P

F32, BF16 = jnp.float32, jnp.bfloat16
DN0 = (((0,), (0,)), ((), ()))
DN1 = (((1,), (1,)), ((), ()))
MESH = pl.DeviceIdType.MESH
SMEM = pl.BlockSpec(memory_space=pltpu.SMEM)
VM = pl.BlockSpec(memory_space=pltpu.VMEM)
HBM = pl.BlockSpec(memory_space=pltpu.HBM)
NX, NY, NZ, ZLO, ZHI = 4, 8, 12, 3, 4
SLABS = NX * NY * ZLO
LIMIT = 16 << 20


class Place:
    def __init__(self):
        self.blk = lax.axis_index("blk")
        self.grp = lax.axis_index("grp")
        self.x = self.blk % NX
        self.y = (self.blk // NX) % NY
        self.zl = self.blk // (NX * NY)
        self.core = self.grp % 2
        self.zh = self.grp // 2
        self.z = self.zh * ZLO + self.zl

    def at(self, x=None, y=None, z=None, core=None):
        x = self.x if x is None else x
        y = self.y if y is None else y
        z = self.z if z is None else z
        core = self.core if core is None else core
        return ((z % ZLO) * (NX * NY) + y * NX + x, (z // ZLO) * 2 + core)

    def slab(self, step):
        return ((self.blk + step + SLABS) % SLABS, self.grp)

    def member(self, step):
        return (self.blk, ((self.zh + step + ZHI) % ZHI) * 2 + self.core)

    def partner(self):
        return (self.blk, self.zh * 2 + 1 - self.core)


def meet(peers):
    barrier = pltpu.get_barrier_semaphore()
    for peer in peers:
        pl.semaphore_signal(barrier, inc=1, device_id=peer, device_id_type=MESH)
    pl.semaphore_wait(barrier, len(peers))


class Copies:
    def __init__(self, send_sem, recv_sem):
        self.send_sem, self.recv_sem, self.started = send_sem, recv_sem, []

    def start(self, src, dst, device):
        number = len(self.started)
        copy = pltpu.make_async_remote_copy(
            src_ref=src, dst_ref=dst, send_sem=self.send_sem.at[number],
            recv_sem=self.recv_sem.at[number], device_id=device, device_id_type=MESH)
        copy.start()
        self.started.append(copy)
        return copy

    def sent(self):
        for copy in self.started:
            copy.wait_send()


def fetch(pairs, sem):
    copies = [pltpu.make_async_copy(src, dst, sem.at[i]) for i, (src, dst) in enumerate(pairs)]
    for copy in copies:
        copy.start()
    return copies


def in_hbm(*arrays):
    return [pltpu.with_memory_space_constraint(a, pltpu.HBM) for a in arrays]


def sd(shape, dtype):
    return jax.ShapeDtypeStruct(shape, dtype)


def dot(a, b):
    return jnp.dot(a, b, preferred_element_type=F32)


def dot_t(a, b):
    return lax.dot_general(a, b, DN1, preferred_element_type=F32)


def contract(a, b):
    return lax.dot_general(a, b, DN0, preferred_element_type=F32)


def placed_of(pos, pw):
    return lax.dot_general(pos, pw, DN0, precision=lax.Precision.HIGHEST,
                           preferred_element_type=F32)


def rank_tiles(mask, rank_r, rank_t, top):
    tiles = mask.shape[0]
    row = lax.broadcasted_iota(jnp.int32, (128, 128), 0)
    col = lax.broadcasted_iota(jnp.int32, (128, 128), 1)
    upper = jnp.where(row < col, 1.0, 0.0).astype(BF16)

    def ranks(values):
        return jnp.where(values > 0.0, dot(values.astype(BF16), upper), -1.0)

    def tile(t, _):
        values = mask[t].astype(F32)
        by_row = ranks(values)
        rank_r[t] = by_row
        top[pl.ds(t, 1), :] = jnp.max(by_row, axis=0, keepdims=True)
        by_col = ranks(values.T)
        rank_t[t] = by_col
        top[pl.ds(t + tiles, 1), :] = jnp.max(by_col, axis=0, keepdims=True)
        return 0

    lax.fori_loop(0, tiles, tile, 0)


def slot_counts(top):
    most = jnp.max(top[...], axis=1, keepdims=True) + 1.0
    return jnp.broadcast_to(most, top.shape).astype(jnp.int32)


def picks(ranks, slot):
    one, none = jnp.ones((), BF16), jnp.zeros((), BF16)
    if isinstance(slot, int):
        slot = jnp.full((), slot, BF16)
    else:
        slot = slot.astype(F32).astype(BF16)
    return jnp.where(ranks == slot, one, none)


def slot_batches(first, group):
    return [range(k, min(k + group, first)) for k in range(0, first, group)]


def forward_kernel(first, more, group, ts, tr, tc, most, s_rows, r_rows, rank_r, agg_own, agg_nb,
                   cnt, agg):
    agg[...] = jnp.zeros_like(agg)
    cnt[...] = jnp.zeros_like(cnt)
    ones = jnp.ones((128, 128), BF16)
    none = jnp.zeros((), BF16)

    def tile(t, _):
        rb = tr[t]
        s = s_rows[ts[t]]
        rk = rank_r[t].astype(BF16)
        floor = -(r_rows[rb].astype(F32))
        floor_b = floor.astype(BF16)

        def add(slots, a, c):
            x = dot(jnp.concatenate([picks(rk, slot) for slot in slots], 0), s)
            for q in range(len(slots)):
                part = x[128 * q:128 * q + 128]
                a = a + jnp.maximum(part, floor)
                c = c + jnp.where(part.astype(BF16) > floor_b, jnp.ones((), BF16), none)
            return a, c

        a = jnp.zeros((128, 128), F32)
        c = jnp.zeros((128, 128), BF16)
        for slots in slot_batches(first, group):
            a, c = add(slots, a, c)
        n = (jnp.maximum(most[t, 0] - first, 0) + more - 1) // more

        def rest(i, carry):
            return add([first + i * more + q for q in range(more)], *carry)

        a, c = lax.fori_loop(0, n, rest, (a, c))
        degree = dot(jnp.where(rk >= none, jnp.ones((), BF16), none), ones)
        spare = (first + n * more).astype(F32) - degree
        agg[rb] += a - degree * floor - spare * jnp.maximum(floor, 0.0)
        cnt[rb] += c.astype(F32) - spare * jnp.where(floor < 0.0, 1.0, 0.0)
        return 0

    lax.fori_loop(0, tc[0], tile, 0)
    for b in range(4):
        sl = pl.ds(b * 128, 128)
        agg_own[sl] = agg[4 + b]
        agg_nb[0, sl] = agg[b].astype(BF16)
        agg_nb[1, sl] = agg[8 + b].astype(BF16)


def forward(ts, tr, tc, most, s_rows, r_rows, rank_r, first=18, more=4, group=3):
    own = 512
    return pl.pallas_call(
        functools.partial(forward_kernel, first, more, group),
        out_shape=[sd((own, 128), F32), sd((2, own, 128), BF16), sd((12, 128, 128), F32)],
        in_specs=[SMEM] * 4 + [VM] * 3,
        out_specs=[VM] * 3,
        scratch_shapes=[pltpu.VMEM((12, 128, 128), F32)],
        compiler_params=pltpu.CompilerParams(vmem_limit_bytes=LIMIT),
        name="forward",
    )(ts, tr, tc, most, s_rows, r_rows, rank_r)


def backward_kernel(first, more, group, ts, tr, tc, most, rank_t, s_rows, r_rows, dagg, lat_all,
                    new_in, cnt, lat, lat_nb, dsend, gsend, new_out, grecv, dr_nb, dr_own, acc):
    new_out[...] = new_in[...]
    acc[...] = jnp.zeros_like(acc)
    tiles = rank_t.shape[0]

    def tile(t, _):
        sb = ts[t]
        rb = tr[t]
        rk = rank_t[t].astype(BF16)
        floor = -(s_rows[sb].astype(F32))
        rhs = jnp.concatenate([r_rows[rb], dagg[rb]], axis=1)

        def add(slots, a):
            x = dot(jnp.concatenate([picks(rk, slot) for slot in slots], 0), rhs)
            for q in range(len(slots)):
                part = x[128 * q:128 * q + 128]
                a = a + jnp.where(part[:, :128] > floor, part[:, 128:], 0.0)
            return a

        a = jnp.zeros((128, 128), F32)
        for slots in slot_batches(first, group):
            a = add(slots, a)
        n = (jnp.maximum(most[t + tiles, 0] - first, 0) + more - 1) // more

        def rest(i, a):
            return add([first + i * more + q for q in range(more)], a)

        acc[sb] += lax.fori_loop(0, n, rest, a)
        return 0

    lax.fori_loop(0, tc[0], tile, 0)
    g = jnp.zeros((128, 128), F32)
    for b in range(8):
        d = acc[pl.ds(4 * b, 4)].reshape(512, 128).astype(BF16)
        dsend[b] = d
        g = g + contract(lat_all[b], d)
    gsend[...] = g
    g = jnp.zeros((128, 128), F32)
    for slab in range(3):
        block = pl.ds(4 * slab, 4)
        d = (cnt[block] * dagg[block].astype(F32)).reshape(512, 128)
        if slab == 1:
            dr_own[...] = d
            g = g + contract(lat[...], d.astype(BF16))
        else:
            dr_nb[slab // 2] = d.astype(BF16)
            g = g + contract(lat_nb[slab // 2], d.astype(BF16))
    grecv[...] = g


def backward(ts, tr, tc, most, rank_t, s_rows, r_rows, dagg, lat_all, new_lat, cnt, lat, lat_nb,
             first=18, more=4, group=6):
    return pl.pallas_call(
        functools.partial(backward_kernel, first, more, group),
        out_shape=[sd((8, 512, 128), BF16), sd((128, 128), F32), sd((512, 128), BF16),
                   sd((128, 128), F32), sd((2, 512, 128), BF16), sd((512, 128), F32)],
        in_specs=[SMEM] * 4 + [VM] * 9,
        out_specs=[VM] * 6,
        scratch_shapes=[pltpu.VMEM((32, 128, 128), F32)],
        compiler_params=pltpu.CompilerParams(vmem_limit_bytes=LIMIT),
        name="backward",
    )(ts, tr, tc, most, rank_t, s_rows, r_rows, dagg, lat_all, new_lat, cnt, lat, lat_nb)


GATHER_COPIES = 24


def gather_kernel(lat, pos, w_send_in, w_recv_in, pw_in, bias_in, mask_in, ts_in, tr_in, tc_in,
                  lat_all, s_rows, r_rows, rank_r, rank_t, most, ts, tr, tc, lat_nb, mask, top,
                  pos_all, pos_nb, w_send, w_recv, pw, bias, load_sem, send_sem, recv_sem):
    me = Place()
    own = lat.shape[0]
    g = me.grp
    loads = fetch([(lat, lat_all.at[g]), (pos, pos_all.at[g]), (w_send_in, w_send),
                   (w_recv_in, w_recv), (pw_in, pw), (bias_in, bias), (mask_in, mask), (ts_in, ts),
                   (tr_in, tr), (tc_in, tc)], load_sem)
    up, dn, sib = me.member(1), me.member(-1), me.partner()
    nxt, prv = me.slab(1), me.slab(-1)
    meet([up, dn, sib, nxt, prv])
    cs = Copies(send_sem, recv_sem)
    halves = (pl.ds(0, own // 2), pl.ds(own // 2, own // 2))

    def half(index, h):
        return lat_all.at[index, halves[h]]

    up_pos = cs.start(pos, pos_all.at[g], up)
    dn_pos = cs.start(pos, pos_all.at[g], dn)
    up_a = cs.start(lat.at[halves[0]], half(g, 0), up)
    dn_b = cs.start(lat.at[halves[1]], half(g, 1), dn)
    up_b = cs.start(lat.at[halves[1]], half(g, 1), up)
    dn_a = cs.start(lat.at[halves[0]], half(g, 0), dn)
    beside = [
        cs.start(lat, lat_nb.at[0], nxt),
        cs.start(lat, lat_nb.at[1], prv),
        cs.start(pos, pos_nb.at[0], nxt),
        cs.start(pos, pos_nb.at[1], prv),
    ]
    partner = [
        cs.start(lat, lat_all.at[g], sib),
        cs.start(pos, pos_all.at[g], sib),
    ]
    iu, idn, far = up[1], dn[1], me.member(2)[1]

    def pass_on(ref):
        return cs.start(ref, ref, sib)

    def send_rows(index):
        s_rows[index] = (dot(lat_all[index], w_send[...])
                         + placed_of(pos_all[index], pw[...])).astype(BF16)

    def recv_rows(slab, rows, places):
        r_rows[slab] = (dot(rows, w_recv[...]) - placed_of(places, pw[...])
                        + bias[...]).astype(BF16)

    def other(index):
        return (index // 2) * 2 + 1 - me.core

    for load in loads:
        load.wait()
    recv_rows(1, lat_all[g], pos_all[g])
    send_rows(g)
    rank_tiles(mask, rank_r, rank_t, top)
    most[...] = slot_counts(top)

    up_pos.wait_recv()
    far_pos = cs.start(pos_all.at[idn], pos_all.at[idn], up)
    near = [pass_on(pos_all.at[idn])]
    dn_pos.wait_recv()
    near.append(pass_on(pos_all.at[iu]))
    up_a.wait_recv()
    far_a = cs.start(half(idn, 0), half(idn, 0), up)
    near.append(pass_on(half(idn, 0)))
    dn_b.wait_recv()
    far_b = cs.start(half(iu, 1), half(iu, 1), dn)
    near.append(pass_on(half(iu, 1)))
    for copy in beside + partner:
        copy.wait_recv()
    recv_rows(0, lat_nb[0], pos_nb[0])
    recv_rows(2, lat_nb[1], pos_nb[1])
    send_rows(sib[1])
    up_b.wait_recv()
    near.append(pass_on(half(idn, 1)))
    send_rows(idn)
    dn_a.wait_recv()
    near.append(pass_on(half(iu, 0)))
    send_rows(iu)
    far_pos.wait_recv()
    last = [pass_on(pos_all.at[far])]
    for copy in near:
        copy.wait_recv()
    send_rows(other(idn))
    send_rows(other(iu))
    far_a.wait_recv()
    last.append(pass_on(half(far, 0)))
    far_b.wait_recv()
    last.append(pass_on(half(far, 1)))
    send_rows(far)
    for copy in last:
        copy.wait_recv()
    send_rows(other(far))
    cs.sent()


def gather(lat, pos, w_send, w_recv, pw, bias, mask, ts, tr, tc):
    own = lat.shape[0]
    n = GATHER_COPIES
    tiles = mask.shape[0]
    ranks = sd((tiles, 128, 128), F32)
    return pl.pallas_call(
        gather_kernel,
        out_shape=[sd((8, own, 128), BF16), sd((8, own, 128), BF16), sd((3, own, 128), BF16),
                   ranks, ranks, sd((2 * tiles, 128), jnp.int32), sd((tiles,), jnp.int32),
                   sd((tiles,), jnp.int32), sd((1,), jnp.int32), sd((2, own, 128), BF16)],
        in_specs=[HBM] * 10,
        out_specs=[VM] * 10,
        scratch_shapes=[pltpu.VMEM((tiles, 128, 128), jnp.int32), pltpu.VMEM((2 * tiles, 128), F32),
                        pltpu.VMEM((8, 3, own), F32),
                        pltpu.VMEM((2, 3, own), F32), pltpu.VMEM((128, 128), BF16),
                        pltpu.VMEM((128, 128), BF16), pltpu.VMEM((3, 128), F32),
                        pltpu.VMEM((1, 128), F32), pltpu.SemaphoreType.DMA((10,)),
                        pltpu.SemaphoreType.DMA((n,)), pltpu.SemaphoreType.DMA((n,))],
        compiler_params=pltpu.CompilerParams(collective_id=0, has_side_effects=True,
                                             vmem_limit_bytes=LIMIT),
        name="gather",
    )(*in_hbm(lat, pos, w_send, w_recv, pw, bias, mask, ts, tr), tc)


PIECES = 1
NODE_COPIES = 4 * PIECES


def node_kernel(agg_own, agg_nb, lat, cot, w_edge_out, w_node_self, w_node_msg,
                node_bias_in, w_node_out, gain_in, new_lat, dagg, part, grads, agg_in,
                direct, agg_b, message_b, hidden_b, d_update_b, d_pre_b, d_message_b,
                node_bias, gain, load_sem, send_sem, recv_sem):
    loads = fetch([(node_bias_in, node_bias), (gain_in, gain)], load_sem)
    me = Place()
    nxt, prv = me.slab(1), me.slab(-1)
    meet([nxt, prv])
    cs = Copies(send_sem, recv_sem)
    size = lat.shape[0] // PIECES
    pieces = [pl.ds(p * size, size) for p in range(PIECES)]
    arrive = []
    for p in pieces:
        arrive.append((cs.start(agg_nb.at[0, p], agg_in.at[0, p], prv),
                       cs.start(agg_nb.at[1, p], agg_in.at[1, p], nxt)))
    leave = []
    for load in loads:
        load.wait()
    for i, p in enumerate(pieces):
        latent = lat[p]
        self_pre = dot(latent, w_node_self[...]) + node_bias[...]
        c = cot[p].astype(F32)
        d_normed = c * gain[...]
        d_centre = d_normed - jnp.mean(d_normed, axis=-1, keepdims=True)
        for copy in arrive[i]:
            copy.wait_recv()
        aggregate = agg_own[p] + agg_in[0, p].astype(F32) + agg_in[1, p].astype(F32)
        aggregate_b = aggregate.astype(BF16)
        message = dot(aggregate_b, w_edge_out[...]).astype(BF16)
        hidden_pre = self_pre + dot(message, w_node_msg[...])
        logistic = jax.nn.sigmoid(hidden_pre)
        hidden = (hidden_pre * logistic).astype(BF16)
        update = dot(hidden, w_node_out[...])
        average = jnp.mean(update, axis=-1, keepdims=True)
        centred = update - average
        variance = jnp.mean(centred * centred, axis=-1, keepdims=True)
        inv_std = lax.rsqrt(variance + 1e-05)
        normed = centred * inv_std
        d_update = (inv_std * (d_centre - normed * jnp.mean(d_normed * normed, axis=-1, keepdims=True))
                    ).astype(BF16)
        d_hidden = dot_t(d_update, w_node_out[...])
        d_hidden_pre = (d_hidden * logistic * (1.0 + hidden_pre * (1.0 - logistic))).astype(BF16)
        d_message = dot_t(d_hidden_pre, w_node_msg[...]).astype(BF16)
        d_aggregate = dot_t(d_message, w_edge_out[...])
        dagg[1, p] = d_aggregate.astype(BF16)
        leave.append(cs.start(dagg.at[1, p], dagg.at[0, p], nxt))
        leave.append(cs.start(dagg.at[1, p], dagg.at[2, p], prv))
        new_lat[p] = (latent.astype(F32) + normed * gain[...]).astype(BF16)
        agg_b[p] = aggregate_b
        message_b[p] = message
        hidden_b[p] = hidden
        d_update_b[p] = d_update
        d_pre_b[p] = d_hidden_pre
        d_message_b[p] = d_message
        direct[p] = c
    latent = lat[...]
    d_hidden_pre = d_pre_b[...]
    grads[0] = contract(agg_b[...], d_message_b[...])
    grads[1] = contract(latent, d_hidden_pre)
    grads[2] = contract(message_b[...], d_hidden_pre)
    grads[3] = contract(hidden_b[...], d_update_b[...])
    part[...] = direct[...] + dot_t(d_hidden_pre, w_node_self[...])
    for copy in leave:
        copy.wait_recv()
    cs.sent()


def node(agg_own, agg_nb, lat, cot, *weights):
    own = lat.shape[0]
    n = NODE_COPIES
    rows = pltpu.VMEM((own, 128), BF16)
    return pl.pallas_call(
        node_kernel,
        out_shape=[sd((own, 128), BF16), sd((3, own, 128), BF16), sd((own, 128), F32),
                   sd((4, 128, 128), F32)],
        in_specs=[VM] * 7 + [HBM, VM, HBM],
        out_specs=[VM] * 4,
        scratch_shapes=[pltpu.VMEM((2, own, 128), BF16), pltpu.VMEM((own, 128), F32),
                        rows, rows, rows, rows, rows, rows, pltpu.VMEM((1, 128), F32),
                        pltpu.VMEM((1, 128), F32), pltpu.SemaphoreType.DMA((2,)),
                        pltpu.SemaphoreType.DMA((n,)), pltpu.SemaphoreType.DMA((n,))],
        compiler_params=pltpu.CompilerParams(collective_id=1, has_side_effects=True,
                                             vmem_limit_bytes=LIMIT),
        name="node",
    )(agg_own, agg_nb, lat, cot, *weights)


FINAL_COPIES = 51


def final_kernel(dsend, gsend, grecv, grads, part, w_send, w_recv, dr_nb, dr_own, latent_grad, weight_grads, v, in_xc, vy, in_y,
                 vz, in_z, out_y, out, in_dr, rs_core, cs_sum, in_ra, in_rb, in_da, in_db, in_fa, in_fb,
                 fwd_a, fwd_b, ready_y, ready_z, send_sem, recv_sem):
    me = Place()
    own = part.shape[0]
    up, dn, sib = me.member(1), me.member(-1), me.partner()
    core, zh = me.core, me.zh
    v[pl.ds(0, 128)] = gsend[...].astype(BF16)
    v[pl.ds(128, 128)] = grecv[...].astype(BF16)
    for i in range(4):
        v[pl.ds(128 * (i + 2), 128)] = grads[i].astype(BF16)
    vy[...] = jnp.zeros_like(vy)

    def chunk(c, x):
        return pl.ds(pl.multiple_of((c * NX + x) * 96, 16), 96)

    def y_peer(d):
        return me.at(y=(me.y + d + NY) % NY)

    def z_peer(d):
        return me.at(z=(me.z + d + NZ) % NZ)

    plane = [(dx, dc) for dx in range(NX) for dc in range(2) if dx or dc]
    spots = [((core + dc) % 2, (me.x + dx) % NX) for dx, dc in plane]
    peers = [me.at(x=x, core=c) for c, x in spots]
    nxt, prv = me.slab(1), me.slab(-1)
    meet(peers + [nxt, prv] + [y_peer(d) for d in (1, 2, -1, -2)] + [z_peer(d) for d in (1, 2, 3, -1, -2, -3)])
    for d in (2, -2):
        pl.semaphore_signal(ready_y, inc=1, device_id=y_peer(d), device_id_type=MESH)
    for d in (3, -3):
        pl.semaphore_signal(ready_z, inc=1, device_id=z_peer(d), device_id_type=MESH)
    cs = Copies(send_sem, recv_sem)
    ha, hb = pl.ds(0, own // 2), pl.ds(own // 2, own // 2)

    ar_xc = [cs.start(v.at[chunk(*spots[j])], in_xc.at[j], peers[j]) for j in range(len(peers))]
    order = [2, 1, 3, 0]
    rs = [cs.start(dsend.at[((zh + o) % ZHI) * 2 + 1 - core], rs_core.at[(zh + o) % ZHI], sib)
          for o in order]

    def chip_sum(i):
        rs[i].wait_recv()
        k = (zh + order[i]) % ZHI
        cs_sum[k] = (dsend[k * 2 + core].astype(F32) + rs_core[k].astype(F32)).astype(BF16)
        return k

    far = chip_sum(0)
    ra = cs.start(cs_sum.at[far, ha], in_ra, up)
    rb = cs.start(cs_sum.at[far, hb], in_rb, dn)
    ku = chip_sum(1)
    db = cs.start(cs_sum.at[ku, hb], in_db, up)
    kd = chip_sum(2)
    da = cs.start(cs_sum.at[kd, ha], in_da, dn)

    for copy in ar_xc:
        copy.wait_recv()
    total = v[chunk(core, me.x)].astype(F32)
    for j in range(len(peers)):
        total = total + in_xc[j].astype(F32)
    for q in range(NY):
        vy[q, pl.ds(0, 12)] = total[12 * q:12 * q + 12].astype(BF16)
    pl.semaphore_wait(ready_y, 2)
    ar_y = [cs.start(vy.at[(me.y + d) % NY], in_y.at[d - 1], y_peer(d)) for d in range(1, NY)]
    beside = [cs.start(dr_nb.at[0], in_dr.at[0], prv), cs.start(dr_nb.at[1], in_dr.at[1], nxt)]
    chip_sum(3)

    for copy in ar_y:
        copy.wait_recv()
    total = vy[me.y].astype(F32)
    for d in range(NY - 1):
        total = total + in_y[d].astype(F32)
    vz[...] = total.astype(BF16)
    in_z[me.z] = total.astype(BF16)
    pl.semaphore_wait(ready_z, 2)
    ar_z = [cs.start(vz, in_z.at[me.z], z_peer(d)) for d in range(1, NZ)]

    for copy in ar_z:
        copy.wait_recv()
    total = in_z[0].astype(F32)
    for d in range(1, NZ):
        total = total + in_z[d].astype(F32)
    out_y[me.y] = total.astype(BF16)
    ag_y = [cs.start(out_y.at[me.y], out_y.at[me.y], y_peer(d)) for d in range(1, NY)]

    ra.wait_recv()
    fwd_a[...] = (in_ra[...].astype(F32) + cs_sum[ku, ha].astype(F32)).astype(BF16)
    fa = cs.start(fwd_a, in_fa, up)
    rb.wait_recv()
    fwd_b[...] = (in_rb[...].astype(F32) + cs_sum[kd, hb].astype(F32)).astype(BF16)
    fb = cs.start(fwd_b, in_fb, dn)

    for copy in ag_y:
        copy.wait_recv()
    mine = chunk(core, me.x)
    out[mine] = jnp.concatenate([out_y[q].astype(F32)[:12] for q in range(NY)], 0).astype(BF16)
    ag_xc = [cs.start(out.at[mine], out.at[mine], peer) for peer in peers]
    for copy in beside:
        copy.wait_recv()
    d_recv = (dr_own[...] + in_dr[0].astype(F32) + in_dr[1].astype(F32)).astype(BF16)
    latent_grad[...] = part[...] + dot_t(d_recv, w_recv[...])
    da.wait_recv()
    db.wait_recv()
    fa.wait_recv()
    d_a = cs_sum[zh, ha].astype(F32) + in_da[...].astype(F32) + in_fa[...].astype(F32)
    latent_grad[ha] = latent_grad[ha] + dot_t(d_a.astype(BF16), w_send[...])
    fb.wait_recv()
    d_b = cs_sum[zh, hb].astype(F32) + in_db[...].astype(F32) + in_fb[...].astype(F32)
    latent_grad[hb] = latent_grad[hb] + dot_t(d_b.astype(BF16), w_send[...])

    for copy in ag_xc:
        copy.wait_recv()
    for i in range(6):
        weight_grads[i] = out[pl.ds(128 * i, 128)].astype(F32)
    cs.sent()


def final(dsend, gsend, grecv, grads, part, w_send, w_recv, dr_nb, dr_own):
    own = part.shape[0]
    n = FINAL_COPIES
    b = lambda *shape: pltpu.VMEM(shape, BF16)
    h = own // 2
    return pl.pallas_call(
        final_kernel,
        out_shape=[sd((own, 128), F32), sd((6, 128, 128), F32)],
        in_specs=[VM] * 9,
        out_specs=[VM] * 2,
        scratch_shapes=[
            b(768, 128), b(2 * NX - 1, 96, 128), b(NY, 16, 128), b(NY - 1, 16, 128), b(16, 128),
            b(NZ, 16, 128), b(NY, 16, 128), b(768, 128), b(2, own, 128), b(ZHI, own, 128), b(ZHI, own, 128),
            b(h, 128), b(h, 128), b(h, 128), b(h, 128), b(h, 128), b(h, 128), b(h, 128), b(h, 128),
            pltpu.SemaphoreType.REGULAR, pltpu.SemaphoreType.REGULAR,
            pltpu.SemaphoreType.DMA((n,)), pltpu.SemaphoreType.DMA((n,))],
        compiler_params=pltpu.CompilerParams(collective_id=2, has_side_effects=True,
                                             vmem_limit_bytes=LIMIT),
        name="final",
    )(dsend, gsend, grecv, grads, part, w_send, w_recv, dr_nb, dr_own)


def finish_kernel(a, b, a_out, b_out, sem):
    for copy in fetch([(a, a_out), (b, b_out)], sem):
        copy.wait()


def finish(a, b):
    return pl.pallas_call(
        finish_kernel,
        out_shape=[sd(a.shape, a.dtype), sd(b.shape, b.dtype)],
        in_specs=[VM] * 2,
        out_specs=[HBM] * 2,
        scratch_shapes=[pltpu.SemaphoreType.DMA((2,))],
        compiler_params=pltpu.CompilerParams(vmem_limit_bytes=LIMIT),
        name="finish",
    )(a, b)


def body(latent, positions, tile_send, tile_recv, tile_mask, tile_count, w_send, w_recv, pos_weight,
         edge_bias, w_edge_out, w_node_self, w_node_msg, node_bias, w_node_out, gain, cotangent):
    ts, tr, tc = tile_send[0, 0], tile_recv[0, 0], tile_count[0]
    lat_all, s_rows, r_rows, rank_r, rank_t, most, ts, tr, tc, lat_nb = gather(
        latent, positions, w_send, w_recv, pos_weight, edge_bias[None], tile_mask[0, 0], ts, tr, tc)
    s_rows = s_rows.reshape(32, 128, 128)
    r_rows = r_rows.reshape(12, 128, 128)
    agg_own, agg_nb, cnt = forward(ts, tr, tc, most, s_rows, r_rows, rank_r)
    new_latent, dagg, part, grads = node(
        agg_own, agg_nb, latent, cotangent, w_edge_out, w_node_self, w_node_msg,
        *in_hbm(node_bias[None]), w_node_out, *in_hbm(gain[None]))
    dsend, gsend, new_latent, grecv, dr_nb, dr_own = backward(
        ts, tr, tc, most, rank_t, s_rows, r_rows, dagg.reshape(12, 128, 128), lat_all, new_latent,
        cnt, latent, lat_nb)
    latent_grad, weight_grads = finish(*final(dsend, gsend, grecv, grads, part, w_send, w_recv,
                                              dr_nb, dr_own))
    return new_latent, latent_grad, weight_grads


def solution(mesh):
    in_specs = (
        P(("blk", "grp"), None),
        P(None, ("blk", "grp")),
        P("blk", "grp", None),
        P("blk", "grp", None),
        P("blk", "grp", None, None, None),
        P("blk", "grp"),
        P(),
        P(),
        P(),
        P(),
        P(),
        P(),
        P(),
        P(),
        P(),
        P(),
        P(("blk", "grp"), None),
    )
    out_specs = (P(("blk", "grp"), None), P(("blk", "grp"), None), P())
    return jax.shard_map(body, mesh=mesh, in_specs=in_specs, out_specs=out_specs, check_vma=False)
```

```python
import functools

import jax
import jax.numpy as jnp
from jax import lax
from jax.experimental import pallas as pl
from jax.experimental.pallas import tpu as pltpu
from jax.sharding import PartitionSpec as P

F32, BF16 = jnp.float32, jnp.bfloat16
DN0 = (((0,), (0,)), ((), ()))
DN1 = (((1,), (1,)), ((), ()))
MESH = pl.DeviceIdType.MESH
SMEM = pl.BlockSpec(memory_space=pltpu.SMEM)
VM = pl.BlockSpec(memory_space=pltpu.VMEM)
HBM = pl.BlockSpec(memory_space=pltpu.HBM)
NX, NY, NZ, ZLO, ZHI = 4, 8, 12, 3, 4
SLABS = NX * NY * ZLO
LIMIT = 16 << 20


class Place:
    def __init__(self):
        self.blk = lax.axis_index("blk")
        self.grp = lax.axis_index("grp")
        self.x = self.blk % NX
        self.y = (self.blk // NX) % NY
        self.zl = self.blk // (NX * NY)
        self.core = self.grp % 2
        self.zh = self.grp // 2
        self.z = self.zh * ZLO + self.zl

    def at(self, x=None, y=None, z=None, core=None):
        x = self.x if x is None else x
        y = self.y if y is None else y
        z = self.z if z is None else z
        core = self.core if core is None else core
        return ((z % ZLO) * (NX * NY) + y * NX + x, (z // ZLO) * 2 + core)

    def slab(self, step):
        return ((self.blk + step + SLABS) % SLABS, self.grp)

    def member(self, step):
        return (self.blk, ((self.zh + step + ZHI) % ZHI) * 2 + self.core)

    def partner(self):
        return (self.blk, self.zh * 2 + 1 - self.core)


def meet(peers):
    barrier = pltpu.get_barrier_semaphore()
    for peer in peers:
        pl.semaphore_signal(barrier, inc=1, device_id=peer, device_id_type=MESH)
    pl.semaphore_wait(barrier, len(peers))


class Copies:
    def __init__(self, send_sem, recv_sem):
        self.send_sem, self.recv_sem, self.started = send_sem, recv_sem, []

    def start(self, src, dst, device):
        number = len(self.started)
        copy = pltpu.make_async_remote_copy(
            src_ref=src, dst_ref=dst, send_sem=self.send_sem.at[number],
            recv_sem=self.recv_sem.at[number], device_id=device, device_id_type=MESH)
        copy.start()
        self.started.append(copy)
        return copy

    def sent(self):
        for copy in self.started:
            copy.wait_send()


def fetch(pairs, sem):
    copies = [pltpu.make_async_copy(src, dst, sem.at[i]) for i, (src, dst) in enumerate(pairs)]
    for copy in copies:
        copy.start()
    return copies


def in_hbm(*arrays):
    return [pltpu.with_memory_space_constraint(a, pltpu.HBM) for a in arrays]


def sd(shape, dtype):
    return jax.ShapeDtypeStruct(shape, dtype)


def dot(a, b):
    return jnp.dot(a, b, preferred_element_type=F32)


def dot_t(a, b):
    return lax.dot_general(a, b, DN1, preferred_element_type=F32)


def contract(a, b):
    return lax.dot_general(a, b, DN0, preferred_element_type=F32)


def placed_of(pos, pw):
    return lax.dot_general(pos, pw, DN0, precision=lax.Precision.HIGHEST,
                           preferred_element_type=F32)


def rank_tiles(mask, rank_r, rank_t, top):
    tiles = mask.shape[0]
    row = lax.broadcasted_iota(jnp.int32, (128, 128), 0)
    col = lax.broadcasted_iota(jnp.int32, (128, 128), 1)
    upper = jnp.where(row < col, 1.0, 0.0).astype(BF16)

    def ranks(values):
        return jnp.where(values > 0.0, dot(values.astype(BF16), upper), -1.0)

    def tile(t, _):
        values = mask[t].astype(F32)
        by_row = ranks(values)
        rank_r[t] = by_row
        top[pl.ds(t, 1), :] = jnp.max(by_row, axis=0, keepdims=True)
        by_col = ranks(values.T)
        rank_t[t] = by_col
        top[pl.ds(t + tiles, 1), :] = jnp.max(by_col, axis=0, keepdims=True)
        return 0

    lax.fori_loop(0, tiles, tile, 0)


def slot_counts(top):
    most = jnp.max(top[...], axis=1, keepdims=True) + 1.0
    return jnp.broadcast_to(most, top.shape).astype(jnp.int32)


def picks(ranks, slot):
    one, none = jnp.ones((), BF16), jnp.zeros((), BF16)
    if isinstance(slot, int):
        slot = jnp.full((), slot, BF16)
    else:
        slot = slot.astype(F32).astype(BF16)
    return jnp.where(ranks == slot, one, none)


def slot_batches(first, group):
    return [range(k, min(k + group, first)) for k in range(0, first, group)]


def forward_kernel(first, more, group, ts, tr, tc, most, s_rows, r_rows, rank_r, agg_own, agg_nb,
                   cnt, agg):
    agg[...] = jnp.zeros_like(agg)
    cnt[...] = jnp.zeros_like(cnt)
    ones = jnp.ones((128, 128), BF16)
    none = jnp.zeros((), BF16)

    def tile(t, _):
        rb = tr[t]
        s = s_rows[ts[t]]
        rk = rank_r[t].astype(BF16)
        floor = -(r_rows[rb].astype(F32))
        floor_b = floor.astype(BF16)

        def add(slots, a, c):
            x = dot(jnp.concatenate([picks(rk, slot) for slot in slots], 0), s)
            for q in range(len(slots)):
                part = x[128 * q:128 * q + 128]
                a = a + jnp.maximum(part, floor)
                c = c + jnp.where(part.astype(BF16) > floor_b, jnp.ones((), BF16), none)
            return a, c

        a = jnp.zeros((128, 128), F32)
        c = jnp.zeros((128, 128), BF16)
        for slots in slot_batches(first, group):
            a, c = add(slots, a, c)
        n = (jnp.maximum(most[t, 0] - first, 0) + more - 1) // more

        def rest(i, carry):
            return add([first + i * more + q for q in range(more)], *carry)

        a, c = lax.fori_loop(0, n, rest, (a, c))
        degree = dot(jnp.where(rk >= none, jnp.ones((), BF16), none), ones)
        spare = (first + n * more).astype(F32) - degree
        agg[rb] += a - degree * floor - spare * jnp.maximum(floor, 0.0)
        cnt[rb] += c.astype(F32) - spare * jnp.where(floor < 0.0, 1.0, 0.0)
        return 0

    lax.fori_loop(0, tc[0], tile, 0)
    for b in range(4):
        sl = pl.ds(b * 128, 128)
        agg_own[sl] = agg[4 + b]
        agg_nb[0, sl] = agg[b].astype(BF16)
        agg_nb[1, sl] = agg[8 + b].astype(BF16)


def forward(ts, tr, tc, most, s_rows, r_rows, rank_r, first=18, more=4, group=3):
    own = 512
    return pl.pallas_call(
        functools.partial(forward_kernel, first, more, group),
        out_shape=[sd((own, 128), F32), sd((2, own, 128), BF16), sd((12, 128, 128), F32)],
        in_specs=[SMEM] * 4 + [VM] * 3,
        out_specs=[VM] * 3,
        scratch_shapes=[pltpu.VMEM((12, 128, 128), F32)],
        compiler_params=pltpu.CompilerParams(vmem_limit_bytes=LIMIT),
        name="forward",
    )(ts, tr, tc, most, s_rows, r_rows, rank_r)


def backward_kernel(first, more, group, ts, tr, tc, most, rank_t, s_rows, r_rows, dagg, lat_all,
                    new_in, cnt, lat, lat_nb, dsend, gsend, new_out, grecv, dr_nb, dr_own, acc):
    new_out[...] = new_in[...]
    acc[...] = jnp.zeros_like(acc)
    tiles = rank_t.shape[0]

    def tile(t, _):
        sb = ts[t]
        rb = tr[t]
        rk = rank_t[t].astype(BF16)
        floor = -(s_rows[sb].astype(F32))
        rhs = jnp.concatenate([r_rows[rb], dagg[rb]], axis=1)

        def add(slots, a):
            x = dot(jnp.concatenate([picks(rk, slot) for slot in slots], 0), rhs)
            for q in range(len(slots)):
                part = x[128 * q:128 * q + 128]
                a = a + jnp.where(part[:, :128] > floor, part[:, 128:], 0.0)
            return a

        a = jnp.zeros((128, 128), F32)
        for slots in slot_batches(first, group):
            a = add(slots, a)
        n = (jnp.maximum(most[t + tiles, 0] - first, 0) + more - 1) // more

        def rest(i, a):
            return add([first + i * more + q for q in range(more)], a)

        acc[sb] += lax.fori_loop(0, n, rest, a)
        return 0

    lax.fori_loop(0, tc[0], tile, 0)
    g = jnp.zeros((128, 128), F32)
    for b in range(8):
        d = acc[pl.ds(4 * b, 4)].reshape(512, 128).astype(BF16)
        dsend[b] = d
        g = g + contract(lat_all[b], d)
    gsend[...] = g
    g = jnp.zeros((128, 128), F32)
    for slab in range(3):
        block = pl.ds(4 * slab, 4)
        d = (cnt[block] * dagg[block].astype(F32)).reshape(512, 128)
        if slab == 1:
            dr_own[...] = d
            g = g + contract(lat[...], d.astype(BF16))
        else:
            dr_nb[slab // 2] = d.astype(BF16)
            g = g + contract(lat_nb[slab // 2], d.astype(BF16))
    grecv[...] = g


def backward(ts, tr, tc, most, rank_t, s_rows, r_rows, dagg, lat_all, new_lat, cnt, lat, lat_nb,
             first=18, more=4, group=6):
    return pl.pallas_call(
        functools.partial(backward_kernel, first, more, group),
        out_shape=[sd((8, 512, 128), BF16), sd((128, 128), F32), sd((512, 128), BF16),
                   sd((128, 128), F32), sd((2, 512, 128), BF16), sd((512, 128), F32)],
        in_specs=[SMEM] * 4 + [VM] * 9,
        out_specs=[VM] * 6,
        scratch_shapes=[pltpu.VMEM((32, 128, 128), F32)],
        compiler_params=pltpu.CompilerParams(vmem_limit_bytes=LIMIT),
        name="backward",
    )(ts, tr, tc, most, rank_t, s_rows, r_rows, dagg, lat_all, new_lat, cnt, lat, lat_nb)


GATHER_COPIES = 24


def gather_kernel(lat, pos, w_send_in, w_recv_in, pw_in, bias_in, mask_in, ts_in, tr_in, tc_in,
                  lat_all, s_rows, r_rows, rank_r, rank_t, most, ts, tr, tc, lat_nb, mask, top,
                  pos_all, pos_nb, w_send, w_recv, pw, bias, placed, load_sem, send_sem, recv_sem):
    me = Place()
    own = lat.shape[0]
    g = me.grp
    loads = fetch([(lat, lat_all.at[g]), (pos, pos_all.at[g]), (w_send_in, w_send),
                   (w_recv_in, w_recv), (pw_in, pw), (bias_in, bias), (mask_in, mask), (ts_in, ts),
                   (tr_in, tr), (tc_in, tc)], load_sem)
    up, dn, sib = me.member(1), me.member(-1), me.partner()
    nxt, prv = me.slab(1), me.slab(-1)
    meet([up, dn, sib, nxt, prv])
    cs = Copies(send_sem, recv_sem)
    halves = (pl.ds(0, own // 2), pl.ds(own // 2, own // 2))

    def half(index, h):
        return lat_all.at[index, halves[h]]

    up_pos = cs.start(pos, pos_all.at[g], up)
    dn_pos = cs.start(pos, pos_all.at[g], dn)
    up_a = cs.start(lat.at[halves[0]], half(g, 0), up)
    dn_b = cs.start(lat.at[halves[1]], half(g, 1), dn)
    up_b = cs.start(lat.at[halves[1]], half(g, 1), up)
    dn_a = cs.start(lat.at[halves[0]], half(g, 0), dn)
    beside = [
        cs.start(lat, lat_nb.at[0], nxt),
        cs.start(lat, lat_nb.at[1], prv),
        cs.start(pos, pos_nb.at[0], nxt),
        cs.start(pos, pos_nb.at[1], prv),
    ]
    partner = [
        cs.start(lat, lat_all.at[g], sib),
        cs.start(pos, pos_all.at[g], sib),
    ]
    iu, idn, far = up[1], dn[1], me.member(2)[1]

    def pass_on(ref):
        return cs.start(ref, ref, sib)

    def place(index):
        placed[index] = placed_of(pos_all[index], pw[...])

    def send_rows(index):
        s_rows[index] = (dot(lat_all[index], w_send[...]) + placed[index]).astype(BF16)

    def recv_rows(slab, rows, places):
        r_rows[slab] = (dot(rows, w_recv[...]) - placed_of(places, pw[...])
                        + bias[...]).astype(BF16)

    def other(index):
        return (index // 2) * 2 + 1 - me.core

    for load in loads:
        load.wait()
    recv_rows(1, lat_all[g], pos_all[g])
    place(g)
    send_rows(g)
    rank_tiles(mask, rank_r, rank_t, top)
    most[...] = slot_counts(top)

    up_pos.wait_recv()
    far_pos = cs.start(pos_all.at[idn], pos_all.at[idn], up)
    near = [pass_on(pos_all.at[idn])]
    dn_pos.wait_recv()
    near.append(pass_on(pos_all.at[iu]))
    up_a.wait_recv()
    far_a = cs.start(half(idn, 0), half(idn, 0), up)
    near.append(pass_on(half(idn, 0)))
    dn_b.wait_recv()
    far_b = cs.start(half(iu, 1), half(iu, 1), dn)
    near.append(pass_on(half(iu, 1)))
    place(idn)
    place(iu)
    for copy in beside + partner:
        copy.wait_recv()
    recv_rows(0, lat_nb[0], pos_nb[0])
    recv_rows(2, lat_nb[1], pos_nb[1])
    place(sib[1])
    send_rows(sib[1])
    up_b.wait_recv()
    near.append(pass_on(half(idn, 1)))
    send_rows(idn)
    dn_a.wait_recv()
    near.append(pass_on(half(iu, 0)))
    send_rows(iu)
    far_pos.wait_recv()
    last = [pass_on(pos_all.at[far])]
    place(far)
    for copy in near:
        copy.wait_recv()
    for index in (other(idn), other(iu)):
        place(index)
        send_rows(index)
    last[0].wait_recv()
    place(other(far))
    far_a.wait_recv()
    last.append(pass_on(half(far, 0)))
    far_b.wait_recv()
    last.append(pass_on(half(far, 1)))
    send_rows(far)
    for copy in last[1:]:
        copy.wait_recv()
    send_rows(other(far))
    cs.sent()


def gather(lat, pos, w_send, w_recv, pw, bias, mask, ts, tr, tc):
    own = lat.shape[0]
    n = GATHER_COPIES
    tiles = mask.shape[0]
    ranks = sd((tiles, 128, 128), F32)
    return pl.pallas_call(
        gather_kernel,
        out_shape=[sd((8, own, 128), BF16), sd((8, own, 128), BF16), sd((3, own, 128), BF16),
                   ranks, ranks, sd((2 * tiles, 128), jnp.int32), sd((tiles,), jnp.int32),
                   sd((tiles,), jnp.int32), sd((1,), jnp.int32), sd((2, own, 128), BF16)],
        in_specs=[HBM] * 10,
        out_specs=[VM] * 10,
        scratch_shapes=[pltpu.VMEM((tiles, 128, 128), jnp.int32), pltpu.VMEM((2 * tiles, 128), F32),
                        pltpu.VMEM((8, 3, own), F32),
                        pltpu.VMEM((2, 3, own), F32), pltpu.VMEM((128, 128), BF16),
                        pltpu.VMEM((128, 128), BF16), pltpu.VMEM((3, 128), F32),
                        pltpu.VMEM((1, 128), F32), pltpu.VMEM((8, own, 128), F32),
                        pltpu.SemaphoreType.DMA((10,)),
                        pltpu.SemaphoreType.DMA((n,)), pltpu.SemaphoreType.DMA((n,))],
        compiler_params=pltpu.CompilerParams(collective_id=0, has_side_effects=True,
                                             vmem_limit_bytes=LIMIT),
        name="gather",
    )(*in_hbm(lat, pos, w_send, w_recv, pw, bias, mask, ts, tr), tc)


PIECES = 1
NODE_COPIES = 4 * PIECES


def node_kernel(agg_own, agg_nb, lat, cot, w_edge_out, w_node_self, w_node_msg,
                node_bias_in, w_node_out, gain_in, new_lat, dagg, part, grads, agg_in,
                direct, agg_b, message_b, hidden_b, d_update_b, d_pre_b, d_message_b,
                node_bias, gain, load_sem, send_sem, recv_sem):
    loads = fetch([(node_bias_in, node_bias), (gain_in, gain)], load_sem)
    me = Place()
    nxt, prv = me.slab(1), me.slab(-1)
    meet([nxt, prv])
    cs = Copies(send_sem, recv_sem)
    size = lat.shape[0] // PIECES
    pieces = [pl.ds(p * size, size) for p in range(PIECES)]
    arrive = []
    for p in pieces:
        arrive.append((cs.start(agg_nb.at[0, p], agg_in.at[0, p], prv),
                       cs.start(agg_nb.at[1, p], agg_in.at[1, p], nxt)))
    leave = []
    for load in loads:
        load.wait()
    for i, p in enumerate(pieces):
        latent = lat[p]
        self_pre = dot(latent, w_node_self[...]) + node_bias[...]
        c = cot[p].astype(F32)
        d_normed = c * gain[...]
        d_centre = d_normed - jnp.mean(d_normed, axis=-1, keepdims=True)
        for copy in arrive[i]:
            copy.wait_recv()
        aggregate = agg_own[p] + agg_in[0, p].astype(F32) + agg_in[1, p].astype(F32)
        aggregate_b = aggregate.astype(BF16)
        message = dot(aggregate_b, w_edge_out[...]).astype(BF16)
        hidden_pre = self_pre + dot(message, w_node_msg[...])
        logistic = jax.nn.sigmoid(hidden_pre)
        hidden = (hidden_pre * logistic).astype(BF16)
        update = dot(hidden, w_node_out[...])
        average = jnp.mean(update, axis=-1, keepdims=True)
        centred = update - average
        variance = jnp.mean(centred * centred, axis=-1, keepdims=True)
        inv_std = lax.rsqrt(variance + 1e-05)
        normed = centred * inv_std
        d_update = (inv_std * (d_centre - normed * jnp.mean(d_normed * normed, axis=-1, keepdims=True))
                    ).astype(BF16)
        d_hidden = dot_t(d_update, w_node_out[...])
        d_hidden_pre = (d_hidden * logistic * (1.0 + hidden_pre * (1.0 - logistic))).astype(BF16)
        d_message = dot_t(d_hidden_pre, w_node_msg[...]).astype(BF16)
        d_aggregate = dot_t(d_message, w_edge_out[...])
        dagg[1, p] = d_aggregate.astype(BF16)
        leave.append(cs.start(dagg.at[1, p], dagg.at[0, p], nxt))
        leave.append(cs.start(dagg.at[1, p], dagg.at[2, p], prv))
        new_lat[p] = (latent.astype(F32) + normed * gain[...]).astype(BF16)
        agg_b[p] = aggregate_b
        message_b[p] = message
        hidden_b[p] = hidden
        d_update_b[p] = d_update
        d_pre_b[p] = d_hidden_pre
        d_message_b[p] = d_message
        direct[p] = c
    latent = lat[...]
    d_hidden_pre = d_pre_b[...]
    grads[0] = contract(agg_b[...], d_message_b[...])
    grads[1] = contract(latent, d_hidden_pre)
    grads[2] = contract(message_b[...], d_hidden_pre)
    grads[3] = contract(hidden_b[...], d_update_b[...])
    part[...] = direct[...] + dot_t(d_hidden_pre, w_node_self[...])
    for copy in leave:
        copy.wait_recv()
    cs.sent()


def node(agg_own, agg_nb, lat, cot, *weights):
    own = lat.shape[0]
    n = NODE_COPIES
    rows = pltpu.VMEM((own, 128), BF16)
    return pl.pallas_call(
        node_kernel,
        out_shape=[sd((own, 128), BF16), sd((3, own, 128), BF16), sd((own, 128), F32),
                   sd((4, 128, 128), F32)],
        in_specs=[VM] * 7 + [HBM, VM, HBM],
        out_specs=[VM] * 4,
        scratch_shapes=[pltpu.VMEM((2, own, 128), BF16), pltpu.VMEM((own, 128), F32),
                        rows, rows, rows, rows, rows, rows, pltpu.VMEM((1, 128), F32),
                        pltpu.VMEM((1, 128), F32), pltpu.SemaphoreType.DMA((2,)),
                        pltpu.SemaphoreType.DMA((n,)), pltpu.SemaphoreType.DMA((n,))],
        compiler_params=pltpu.CompilerParams(collective_id=1, has_side_effects=True,
                                             vmem_limit_bytes=LIMIT),
        name="node",
    )(agg_own, agg_nb, lat, cot, *weights)


FINAL_COPIES = 51


def final_kernel(dsend, gsend, grecv, grads, part, w_send, w_recv, dr_nb, dr_own, latent_grad, weight_grads, v, in_xc, vy, in_y,
                 vz, in_z, out_y, out, in_dr, rs_core, cs_sum, in_ra, in_rb, in_da, in_db, in_fa, in_fb,
                 fwd_a, fwd_b, ready_y, ready_z, send_sem, recv_sem):
    me = Place()
    own = part.shape[0]
    up, dn, sib = me.member(1), me.member(-1), me.partner()
    core, zh = me.core, me.zh
    v[pl.ds(0, 128)] = gsend[...].astype(BF16)
    v[pl.ds(128, 128)] = grecv[...].astype(BF16)
    for i in range(4):
        v[pl.ds(128 * (i + 2), 128)] = grads[i].astype(BF16)
    vy[...] = jnp.zeros_like(vy)

    def chunk(c, x):
        return pl.ds(pl.multiple_of((c * NX + x) * 96, 16), 96)

    def y_peer(d):
        return me.at(y=(me.y + d + NY) % NY)

    def z_peer(d):
        return me.at(z=(me.z + d + NZ) % NZ)

    plane = [(dx, dc) for dx in range(NX) for dc in range(2) if dx or dc]
    spots = [((core + dc) % 2, (me.x + dx) % NX) for dx, dc in plane]
    peers = [me.at(x=x, core=c) for c, x in spots]
    nxt, prv = me.slab(1), me.slab(-1)
    meet(peers + [nxt, prv] + [y_peer(d) for d in (1, 2, -1, -2)] + [z_peer(d) for d in (1, 2, 3, -1, -2, -3)])
    for d in (2, -2):
        pl.semaphore_signal(ready_y, inc=1, device_id=y_peer(d), device_id_type=MESH)
    for d in (3, -3):
        pl.semaphore_signal(ready_z, inc=1, device_id=z_peer(d), device_id_type=MESH)
    cs = Copies(send_sem, recv_sem)
    ha, hb = pl.ds(0, own // 2), pl.ds(own // 2, own // 2)

    ar_xc = [cs.start(v.at[chunk(*spots[j])], in_xc.at[j], peers[j]) for j in range(len(peers))]
    order = [2, 1, 3, 0]
    rs = [cs.start(dsend.at[((zh + o) % ZHI) * 2 + 1 - core], rs_core.at[(zh + o) % ZHI], sib)
          for o in order]

    def chip_sum(i):
        rs[i].wait_recv()
        k = (zh + order[i]) % ZHI
        cs_sum[k] = (dsend[k * 2 + core].astype(F32) + rs_core[k].astype(F32)).astype(BF16)
        return k

    far = chip_sum(0)
    ra = cs.start(cs_sum.at[far, ha], in_ra, up)
    rb = cs.start(cs_sum.at[far, hb], in_rb, dn)
    ku = chip_sum(1)
    db = cs.start(cs_sum.at[ku, hb], in_db, up)
    kd = chip_sum(2)
    da = cs.start(cs_sum.at[kd, ha], in_da, dn)

    for copy in ar_xc:
        copy.wait_recv()
    total = v[chunk(core, me.x)].astype(F32)
    for j in range(len(peers)):
        total = total + in_xc[j].astype(F32)
    for q in range(NY):
        vy[q, pl.ds(0, 12)] = total[12 * q:12 * q + 12].astype(BF16)
    pl.semaphore_wait(ready_y, 2)
    ar_y = [cs.start(vy.at[(me.y + d) % NY], in_y.at[d - 1], y_peer(d)) for d in range(1, NY)]
    chip_sum(3)

    for copy in ar_y:
        copy.wait_recv()
    total = vy[me.y].astype(F32)
    for d in range(NY - 1):
        total = total + in_y[d].astype(F32)
    vz[...] = total.astype(BF16)
    in_z[me.z] = total.astype(BF16)
    pl.semaphore_wait(ready_z, 2)
    ar_z = [cs.start(vz, in_z.at[me.z], z_peer(d)) for d in range(1, NZ)]
    beside = [cs.start(dr_nb.at[0], in_dr.at[0], prv), cs.start(dr_nb.at[1], in_dr.at[1], nxt)]

    for copy in ar_z:
        copy.wait_recv()
    total = in_z[0].astype(F32)
    for d in range(1, NZ):
        total = total + in_z[d].astype(F32)
    out_y[me.y] = total.astype(BF16)
    ag_y = [cs.start(out_y.at[me.y], out_y.at[me.y], y_peer(d)) for d in range(1, NY)]

    ra.wait_recv()
    fwd_a[...] = (in_ra[...].astype(F32) + cs_sum[ku, ha].astype(F32)).astype(BF16)
    fa = cs.start(fwd_a, in_fa, up)
    rb.wait_recv()
    fwd_b[...] = (in_rb[...].astype(F32) + cs_sum[kd, hb].astype(F32)).astype(BF16)
    fb = cs.start(fwd_b, in_fb, dn)

    for copy in ag_y:
        copy.wait_recv()
    mine = chunk(core, me.x)
    out[mine] = jnp.concatenate([out_y[q].astype(F32)[:12] for q in range(NY)], 0).astype(BF16)
    ag_xc = [cs.start(out.at[mine], out.at[mine], peer) for peer in peers]
    for copy in beside:
        copy.wait_recv()
    d_recv = (dr_own[...] + in_dr[0].astype(F32) + in_dr[1].astype(F32)).astype(BF16)
    latent_grad[...] = part[...] + dot_t(d_recv, w_recv[...])
    da.wait_recv()
    db.wait_recv()
    fa.wait_recv()
    d_a = cs_sum[zh, ha].astype(F32) + in_da[...].astype(F32) + in_fa[...].astype(F32)
    latent_grad[ha] = latent_grad[ha] + dot_t(d_a.astype(BF16), w_send[...])
    fb.wait_recv()
    d_b = cs_sum[zh, hb].astype(F32) + in_db[...].astype(F32) + in_fb[...].astype(F32)
    latent_grad[hb] = latent_grad[hb] + dot_t(d_b.astype(BF16), w_send[...])

    for copy in ag_xc:
        copy.wait_recv()
    for i in range(6):
        weight_grads[i] = out[pl.ds(128 * i, 128)].astype(F32)
    cs.sent()


def final(dsend, gsend, grecv, grads, part, w_send, w_recv, dr_nb, dr_own):
    own = part.shape[0]
    n = FINAL_COPIES
    b = lambda *shape: pltpu.VMEM(shape, BF16)
    h = own // 2
    return pl.pallas_call(
        final_kernel,
        out_shape=[sd((own, 128), F32), sd((6, 128, 128), F32)],
        in_specs=[VM] * 9,
        out_specs=[VM] * 2,
        scratch_shapes=[
            b(768, 128), b(2 * NX - 1, 96, 128), b(NY, 16, 128), b(NY - 1, 16, 128), b(16, 128),
            b(NZ, 16, 128), b(NY, 16, 128), b(768, 128), b(2, own, 128), b(ZHI, own, 128), b(ZHI, own, 128),
            b(h, 128), b(h, 128), b(h, 128), b(h, 128), b(h, 128), b(h, 128), b(h, 128), b(h, 128),
            pltpu.SemaphoreType.REGULAR, pltpu.SemaphoreType.REGULAR,
            pltpu.SemaphoreType.DMA((n,)), pltpu.SemaphoreType.DMA((n,))],
        compiler_params=pltpu.CompilerParams(collective_id=2, has_side_effects=True,
                                             vmem_limit_bytes=LIMIT),
        name="final",
    )(dsend, gsend, grecv, grads, part, w_send, w_recv, dr_nb, dr_own)


def finish_kernel(a, b, a_out, b_out, sem):
    for copy in fetch([(a, a_out), (b, b_out)], sem):
        copy.wait()


def finish(a, b):
    return pl.pallas_call(
        finish_kernel,
        out_shape=[sd(a.shape, a.dtype), sd(b.shape, b.dtype)],
        in_specs=[VM] * 2,
        out_specs=[HBM] * 2,
        scratch_shapes=[pltpu.SemaphoreType.DMA((2,))],
        compiler_params=pltpu.CompilerParams(vmem_limit_bytes=LIMIT),
        name="finish",
    )(a, b)


def body(latent, positions, tile_send, tile_recv, tile_mask, tile_count, w_send, w_recv, pos_weight,
         edge_bias, w_edge_out, w_node_self, w_node_msg, node_bias, w_node_out, gain, cotangent):
    ts, tr, tc = tile_send[0, 0], tile_recv[0, 0], tile_count[0]
    lat_all, s_rows, r_rows, rank_r, rank_t, most, ts, tr, tc, lat_nb = gather(
        latent, positions, w_send, w_recv, pos_weight, edge_bias[None], tile_mask[0, 0], ts, tr, tc)
    s_rows = s_rows.reshape(32, 128, 128)
    r_rows = r_rows.reshape(12, 128, 128)
    agg_own, agg_nb, cnt = forward(ts, tr, tc, most, s_rows, r_rows, rank_r)
    new_latent, dagg, part, grads = node(
        agg_own, agg_nb, latent, cotangent, w_edge_out, w_node_self, w_node_msg,
        *in_hbm(node_bias[None]), w_node_out, *in_hbm(gain[None]))
    dsend, gsend, new_latent, grecv, dr_nb, dr_own = backward(
        ts, tr, tc, most, rank_t, s_rows, r_rows, dagg.reshape(12, 128, 128), lat_all, new_latent,
        cnt, latent, lat_nb)
    latent_grad, weight_grads = finish(*final(dsend, gsend, grecv, grads, part, w_send, w_recv,
                                              dr_nb, dr_own))
    return new_latent, latent_grad, weight_grads


def solution(mesh):
    in_specs = (
        P(("blk", "grp"), None),
        P(None, ("blk", "grp")),
        P("blk", "grp", None),
        P("blk", "grp", None),
        P("blk", "grp", None, None, None),
        P("blk", "grp"),
        P(),
        P(),
        P(),
        P(),
        P(),
        P(),
        P(),
        P(),
        P(),
        P(),
        P(("blk", "grp"), None),
    )
    out_specs = (P(("blk", "grp"), None), P(("blk", "grp"), None), P())
    return jax.shard_map(body, mesh=mesh, in_specs=in_specs, out_specs=out_specs, check_vma=False)
```
